32 devices in a mesh: groups: 2 (over y), gx: 4 (over z), gy: 2 (over x), gz: 2 (over core).
Axes of the slice: x: 2, y: 2, z: 4, core: 2. Of those that a mesh axis runs over, the one named last changes fastest.
Arguments:
- log_perm: float32 [32, 32, 1024], P(('groups', 'gx'), 'gy', 'gz'), parts along dimension 0, may hold values from -4 to 4
- source: float32 [32, 32, 1024], P(('groups', 'gx'), 'gy', 'gz'), parts along dimension 0, may hold values from -24 to 24
- low_bound: float32 [1], replicated, may hold values from 0.05 to 0.4
- high_bound: float32 [1], replicated, may hold values from 1.8 to 2.4
Outputs:
- fine_pressure: float32 [32, 32, 1024], P(('groups', 'gx'), 'gy', 'gz'), parts along dimension 0
- difference: float32 [32, 32, 1024], P(('groups', 'gx'), 'gy', 'gz'), parts along dimension 0
The draws below stay inside these ranges and needn't reach their ends.
There are 2 independent parts, one for each index of `groups`. The reference program is written for one: setup_inputs(seed, part) draws one part's arguments, and reference() takes and returns one part's arrays. A program takes and returns all parts, laid end to end along the dimension named above; an argument that names none is the same for every part. Nothing has to cross between parts.
All inputs are finite; a program needn't handle non-finite values.
Results may differ from the reference program's by a relative error of at most 0.00002.
Values sent between devices are 32-bit elements; how exact they have to be, the bound alone decides.
A program may use at most 64 MiB of HBM per device.

```python
import jax
import jax.numpy as jnp

DEGREE = 3
NX = 16
NY = 32
NZ = 1024


def steps_of(own_key, dims, split, low, largest):
    factor_of, own = 1.0, jax.random.fold_in(own_key, 6)
    for position, shards_of in split:
        heights = jnp.exp(jax.random.uniform(jax.random.fold_in(own, position), (shards_of,), jnp.float32, low / len(split), largest / len(split)))
        factor_of = factor_of * jnp.repeat(heights, dims[position] // shards_of).reshape([-1 if axis == position else 1 for axis in range(len(dims))])
    return factor_of


def bell_draw(rng, extent, scale, most, split=(), kind=jnp.bfloat16):
    drawn = jax.random.normal(rng, extent, jnp.float32) * scale
    if len(split) > 0:
        drawn = steps_of(rng, extent, split, -0.22, 0.18) * drawn
    return jnp.clip(drawn, min=-most, max=most).astype(kind)


def setup_inputs(seed: int = 0, part: int = 0) -> dict:
    key_list = jax.random.split(jax.random.key(seed), 5)
    own_keys = jax.random.split(jax.random.fold_in(key_list[4], part), 5)
    return {
        "log_perm": bell_draw(own_keys[0], (NX, NY, NZ), 1.0, 4.0, ((0, 4), (1, 2), (2, 2)), jnp.float32),
        "source": bell_draw(own_keys[1], (NX, NY, NZ), 4.0, 24.0, ((0, 4), (1, 2), (2, 2)), jnp.float32),
        "low_bound": jnp.clip(jax.random.uniform(key_list[2], (1,), jnp.float32, 0.05, 0.4), 0.05, 0.4),
        "high_bound": jnp.clip(jax.random.uniform(key_list[3], (1,), jnp.float32, 1.8, 2.4), 1.8, 2.4),
    }


storage_rate = 0.1


def harmonic(first_perm, second_perm, face_scale):
    return face_scale * 2.0 * first_perm * second_perm / (first_perm + second_perm)


def coefficients(padded, face_scale, storage):
    centre = padded[1:-1, 1:-1, 1:-1]
    east_face = harmonic(centre, padded[2:, 1:-1, 1:-1], face_scale)
    west_face = harmonic(centre, padded[:-2, 1:-1, 1:-1], face_scale)
    north_face = harmonic(centre, padded[1:-1, 2:, 1:-1], face_scale)
    south_face = harmonic(centre, padded[1:-1, :-2, 1:-1], face_scale)
    upper_face = harmonic(centre, padded[1:-1, 1:-1, 2:], face_scale)
    lower_face = harmonic(centre, padded[1:-1, 1:-1, :-2], face_scale)
    diagonal = storage + east_face + west_face + north_face + south_face + upper_face + lower_face
    return (east_face, west_face, north_face, south_face, upper_face, lower_face, diagonal)


def operate(padded, face_terms):
    east_face, west_face, north_face, south_face, upper_face, lower_face, diagonal = face_terms
    centre = padded[1:-1, 1:-1, 1:-1]
    beside = east_face * padded[2:, 1:-1, 1:-1] + west_face * padded[:-2, 1:-1, 1:-1]
    beside = beside + north_face * padded[1:-1, 2:, 1:-1] + south_face * padded[1:-1, :-2, 1:-1]
    beside = beside + upper_face * padded[1:-1, 1:-1, 2:] + lower_face * padded[1:-1, 1:-1, :-2]
    return diagonal * centre - beside


def solve_level(log_field, source_field, lower_edge, upper_edge, face_scale, storage):
    face_terms = coefficients(jnp.pad(jnp.exp(log_field), 1), face_scale, storage)
    diagonal = face_terms[6]
    centre_value = (upper_edge + lower_edge) * 0.5
    half_width = (upper_edge - lower_edge) * 0.5
    ratio_sigma = centre_value / half_width
    rho_now = 1.0 / ratio_sigma
    direction = source_field / (centre_value * diagonal)
    solution = direction
    residual = source_field
    for iteration in range(DEGREE):
        residual = residual - operate(jnp.pad(direction, 1), face_terms)
        rho_next = 1.0 / (2.0 * ratio_sigma - rho_now)
        direction = rho_next * rho_now * direction + (2.0 * rho_next / half_width) * residual / diagonal
        solution = solution + direction
        rho_now = rho_next
    return solution


def reference(log_perm, source, low_bound, high_bound):
    lower_edge = low_bound[0]
    upper_edge = high_bound[0]
    fine = solve_level(log_perm, source, lower_edge, upper_edge, 1.0, storage_rate)
    blocks = (NX // 2, 2, NY // 2, 2, NZ // 2, 2)
    coarse_log = log_perm.reshape(blocks).mean(axis=(1, 3, 5))
    coarse_source = source.reshape(blocks).sum(axis=(1, 3, 5))
    coarse = solve_level(coarse_log, coarse_source, lower_edge, upper_edge, 2.0, 8.0 * storage_rate)
    spread = jnp.broadcast_to(coarse[:, None, :, None, :, None], blocks).reshape(NX, NY, NZ)
    return fine, fine - spread
```

```python
import functools

import jax
import jax.numpy as jnp
from jax import lax
from jax.experimental import pallas as pl
from jax.experimental.pallas import tpu as pltpu
from jax.sharding import PartitionSpec as P

DEGREE = 3
STORAGE = 0.1
LANES = 128
ROWS = 8
MESH = pl.DeviceIdType.MESH
AXES = ("gx", "gy", "gz")


def roll(a, shift, axis):
    return pltpu.roll(a, shift % a.shape[axis], axis)


def iota(shape, axis):
    return lax.broadcasted_iota(jnp.int32, shape, axis)


def even(shape, axis):
    return iota(shape, axis) % 2 == 0


def pair_sum(a, axis):
    return a + jnp.where(even(a.shape, axis), roll(a, -1, axis), roll(a, 1, axis))


def pooled(a, b):
    return pair_sum(pair_sum(a + b, 0), 1)


def packed(a):
    rows, lanes = a.shape[0] // 2, a.shape[1] // 2
    a = jnp.where(even((a.shape[0], lanes), 1), a[:, :lanes], a[:, lanes:])
    return jnp.where(even((rows, lanes), 0), a[:rows], a[rows:])


def unpacked(a):
    for axis in (0, 1):
        is_even = even(a.shape, axis)
        first = jnp.where(is_even, a, roll(a, 1, axis))
        second = jnp.where(is_even, roll(a, -1, axis), a)
        a = jnp.concatenate([first, second], axis=axis)
    return a


def kernel(sizes, low_hbm, high_hbm, log_hbm, src_hbm, sol, last,
           low_ref, high_ref, log_ref, src_ref, dirs, face_c, face_y, halo_x, halo_c, halo_y, halo_z,
           inv_k, t_x, t_y, t_z, b_x, b_y, b_z, held, inv_d, res,
           io_sem, send_sem, recv_sem):
    nx, ny, nz = log_ref.shape
    nc = nx // 2
    nl = nx + nc
    me = {axis: lax.axis_index(axis) for axis in AXES}
    has = {axis: (me[axis] > 0, me[axis] < sizes[axis] - 1) for axis in AXES}

    barrier = pltpu.get_barrier_semaphore()
    count = 0
    for axis in AXES:
        if sizes[axis] == 2:
            pl.semaphore_signal(barrier, inc=1, device_id={axis: 1 - me[axis]},
                                device_id_type=MESH)
            count = count + 1
        elif sizes[axis] > 2:
            for side, step in ((0, -1), (1, 1)):
                @pl.when(has[axis][side])
                def _():
                    pl.semaphore_signal(barrier, inc=1, device_id={axis: me[axis] + step},
                                        device_id_type=MESH)
                count = count + has[axis][side].astype(jnp.int32)

    log_in = pltpu.make_async_copy(log_hbm, log_ref, io_sem.at[0])
    src_in = pltpu.make_async_copy(src_hbm, src_ref, io_sem.at[1])
    low_in = pltpu.make_async_copy(low_hbm, low_ref, io_sem.at[2])
    high_in = pltpu.make_async_copy(high_hbm, high_ref, io_sem.at[3])
    for copy in (log_in, src_in, low_in, high_in):
        copy.start()

    for axis, halos in (("gx", (halo_x, halo_c)), ("gy", (halo_y,)), ("gz", (halo_z,))):
        if sizes[axis] > 2:
            for side in (0, 1):
                @pl.when(jnp.logical_not(has[axis][side]))
                def _():
                    for halo in halos:
                        for turn in range(DEGREE + 1):
                            halo[turn, side] = jnp.zeros_like(halo[turn, side])

    def sides(axis):
        if sizes[axis] == 1:
            return []
        if sizes[axis] == 2:
            return [(0, 1 - me[axis], None)]
        return [(s, s, has[axis][s].astype(jnp.float32)) for s in (0, 1)]

    def tile(side, length, size):
        first = side * (length - size)
        return pl.ds(first if isinstance(first, int) else pl.multiple_of(first, size), size)

    def faces(turn, kind):
        if kind == 0:
            source = log_hbm if turn == 0 else dirs.at[turn]
            return "gx", (lambda s: source.at[s * (nx - 1)]), (lambda s: halo_x.at[turn, s])
        if kind == 1:
            return "gx", (lambda s: face_c.at[turn, s]), (lambda s: halo_c.at[turn, s])
        if kind == 2:
            return "gy", (lambda s: face_y.at[turn, s]), (lambda s: halo_y.at[turn, s])
        return ("gz", (lambda s: dirs.at[turn, :, :, tile(s, nz, LANES)]),
                (lambda s: halo_z.at[turn, s]))

    def each(turn, kind, outgoing, act):
        axis, source_of, target_of = faces(turn, kind)
        n, here = sizes[axis], me[axis]
        if n == 1:
            return
        if n == 2:
            act(pltpu.make_async_remote_copy(
                src_ref=source_of(1 - here), dst_ref=target_of(here),
                send_sem=send_sem.at[turn, kind, 0], recv_sem=recv_sem.at[turn, kind, 0],
                device_id={axis: 1 - here}, device_id_type=MESH))
            return
        for side, step in ((0, -1), (1, 1)):
            there = 1 - side if outgoing else side

            @pl.when(has[axis][side])
            def _():
                act(pltpu.make_async_remote_copy(
                    src_ref=source_of(side), dst_ref=target_of(there),
                    send_sem=send_sem.at[turn, kind, side],
                    recv_sem=recv_sem.at[turn, kind, there],
                    device_id={axis: here + step}, device_id_type=MESH))

    def start(turn, kind):
        each(turn, kind, True, lambda copy: copy.start())

    def arrive(turn, kind):
        each(turn, kind, False, lambda copy: copy.wait_recv())

    def drain(turn, kind):
        each(turn, kind, True, lambda copy: copy.wait_send())

    def field(turn):
        return dirs.at[turn] if turn <= DEGREE else last

    def level(i):
        return (1, 1.0, STORAGE) if i < nx else (2, 2.0, 8.0 * STORAGE)

    def send_coarse(turn):
        face_c[turn, 0] = packed(dirs[turn, nx])
        face_c[turn, 1] = packed(dirs[turn, nl - 1])
        start(turn, 1)

    def send_rows(turn):
        for i in range(nl):
            face_y[turn, 0, i:i + 1, :] = dirs[turn, i, 0:1, :]
            face_y[turn, 1, i:i + 1, :] = dirs[turn, i, ny - 1:ny, :]
        start(turn, 2)

    log_in.wait()
    for i in range(nx):
        dirs[0, i] = log_ref[i]
    for j in range(nc):
        dirs[0, nx + j] = pooled(log_ref[2 * j], log_ref[2 * j + 1]) * 0.125
    pl.semaphore_wait(barrier, count)
    start(0, 0)
    send_coarse(0)
    send_rows(0)
    start(0, 3)

    row = iota((ny, nz), 0)
    lane = iota((ny, nz), 1)
    for i in range(nl):
        inv_k[i] = jnp.exp(-dirs[0, i])
    for i in range(nl):
        k, scale, storage = level(i)
        own = inv_k[i]
        along_y = jnp.where(row < ny - k, 2.0 * scale / (own + roll(own, -k, 0)), 0.0)
        along_z = jnp.where(lane < nz - k, 2.0 * scale / (own + roll(own, -k, 1)), 0.0)
        t_y[i] = along_y
        t_z[i] = along_z
        inv_d[i] = (along_y + roll(along_y, k, 0)) + (along_z + roll(along_z, k, 1))
        held[i] = jnp.full((ny, nz), storage)
    for i in range(nl):
        if i not in (nx - 1, nl - 1):
            along_x = 2.0 * level(i)[1] / (inv_k[i] + inv_k[i + 1])
            t_x[i] = along_x
            inv_d[i] += along_x
            inv_d[i + 1] += along_x

    for copy in (src_in, low_in, high_in):
        copy.wait()
    for i in range(nx):
        res[i] = src_ref[i]
    for j in range(nc):
        res[nx + j] = pooled(src_ref[2 * j], src_ref[2 * j + 1])

    low = jnp.full((1, nz), low_ref[0])
    high = jnp.full((1, nz), high_ref[0])
    theta = (high + low) * 0.5
    delta = (high - low) * 0.5
    sigma = theta / delta
    rho = 1.0 / sigma
    inv_theta = 1.0 / theta

    row_b = iota((ROWS, nz), 0)
    lane_b = iota((ny, LANES), 1)

    def beside(index, side, size, k):
        first = side * (size - k)
        return (index >= first) & (index < first + k)

    def side_x(turn, side, lev):
        return halo_x[turn, side] if lev == 0 else unpacked(halo_c[turn, side])

    def side_y(turn, side, i):
        return halo_y[turn, side, i:i + 1, :]

    def side_z(turn, side, i):
        k = level(i)[0]
        return pltpu.roll(halo_z[turn, side, i], k + side * (LANES - 2 * k), 1)

    def edge(lev, side):
        if isinstance(side, int):
            return (0, nx - 1)[side] if lev == 0 else (nx, nl - 1)[side]
        return side * (nx - 1) if lev == 0 else nx + side * (nc - 1)

    def across(at, scale, own, beyond, factor):
        t = 2.0 * scale / (own + jnp.exp(-beyond))
        if at is not None:
            t = jnp.where(at, t, 0.0)
        return t if factor is None else t * factor

    arrive(0, 3)
    for slot, side, factor in sides("gz"):
        where = tile(side, nz, LANES)
        for i in range(nl):
            k, scale, _ = level(i)
            t = across(beside(lane_b, side, LANES, k), scale, inv_k[i, :, where],
                       side_z(0, side, i), factor)
            b_z[slot, i] = t
            held[i, :, where] += t
    arrive(0, 2)
    for slot, side, factor in sides("gy"):
        where = tile(side, ny, ROWS)
        for i in range(nl):
            k, scale, _ = level(i)
            t = across(beside(row_b, side, ROWS, k), scale, inv_k[i, where, :],
                       side_y(0, side, i), factor)
            b_y[slot, i] = t
            held[i, where, :] += t

    def begin(i):
        inverse = 1.0 / (inv_d[i] + held[i])
        inv_d[i] = inverse
        dirs[1, i] = res[i] * inverse * inv_theta

    for i in range(1, nx - 1):
        begin(i)
    for lev in (0, 1):
        arrive(0, lev)
        for slot, side, factor in sides("gx"):
            i = edge(lev, side)
            t = across(None, (1.0, 2.0)[lev], inv_k[i], side_x(0, side, lev), factor)
            b_x[lev, slot] = t
            held[i] += t
        if lev == 0:
            for i in dict.fromkeys((0, nx - 1)):
                begin(i)
            start(1, 0)
    for i in range(nx, nl):
        begin(i)
    send_coarse(1)
    send_rows(1)
    start(1, 3)

    for turn in range(1, DEGREE + 1):
        rho_next = 1.0 / (2.0 * sigma - rho)
        keep = rho_next * rho
        gain = 2.0 * rho_next / delta
        rho = rho_next
        later = field(turn + 1)
        for kind in (0, 1, 2, 3):
            drain(turn - 1, kind)
        flow_x = None
        for i in range(nl):
            k = level(i)[0]
            d = dirs[turn, i]
            sol[i] = d if turn == 1 else sol[i] + d
            flow_y = t_y[i] * (d - roll(d, -k, 0))
            flow_z = t_z[i] * (d - roll(d, -k, 1))
            r = res[i] - held[i] * d
            r = r - (flow_y - roll(flow_y, k, 0)) - (flow_z - roll(flow_z, k, 1))
            if i not in (0, nx):
                r = r + flow_x
            if i not in (nx - 1, nl - 1):
                flow_x = t_x[i] * (d - dirs[turn, i + 1])
                r = r - flow_x
            res[i] = r
            later[i] = keep * d + gain * (r * inv_d[i])

        def add(at, t, wide):
            if turn < DEGREE:
                res[at] += t
            later[at] += wide * (t * inv_d[at])

        arrive(turn, 3)
        for slot, side, _ in sides("gz"):
            for i in range(nl):
                add((i, slice(None), tile(side, nz, LANES)),
                    b_z[slot, i] * side_z(turn, side, i), gain[:, :LANES])
        arrive(turn, 2)
        for slot, side, _ in sides("gy"):
            for i in range(nl):
                add((i, tile(side, ny, ROWS), slice(None)),
                    b_y[slot, i] * side_y(turn, side, i), gain)
        for lev in (0, 1):
            arrive(turn, lev)
            for slot, side, _ in sides("gx"):
                add((edge(lev, side),), b_x[lev, slot] * side_x(turn, side, lev), gain)
            if lev == 0 and turn < DEGREE:
                start(turn + 1, 0)
        if turn < DEGREE:
            send_coarse(turn + 1)
            send_rows(turn + 1)
            start(turn + 1, 3)

    for kind in (0, 1, 2, 3):
        drain(DEGREE, kind)


def shards(sizes, log_perm, source, low_bound, high_bound):
    nx, ny, nz = log_perm.shape
    nc = nx // 2
    nl = nx + nc
    pack = -(-nl // ROWS) * ROWS
    turns = DEGREE + 1
    f32 = lambda *shape: pltpu.VMEM(shape, jnp.float32)
    block = f32(nx, ny, nz)
    both = f32(nl, ny, nz)
    shape = jax.ShapeDtypeStruct((nl, ny, nz), jnp.float32)
    hbm = pl.BlockSpec(memory_space=pltpu.HBM)
    log_perm = pltpu.with_memory_space_constraint(log_perm, pltpu.HBM)
    source = pltpu.with_memory_space_constraint(source, pltpu.HBM)
    vmem = pl.BlockSpec(memory_space=pltpu.VMEM)
    sol, last = pl.pallas_call(
        functools.partial(kernel, sizes),
        out_shape=(shape, shape),
        in_specs=[hbm] * 4,
        out_specs=(vmem, vmem),
        scratch_shapes=[
            pltpu.SMEM((1,), jnp.float32),
            pltpu.SMEM((1,), jnp.float32),
            block, block,
            f32(turns, nl, ny, nz),
            f32(turns, 2, ny // 2, nz // 2),
            f32(turns, 2, pack, nz),
            f32(turns, 2, ny, nz),
            f32(turns, 2, ny // 2, nz // 2),
            f32(turns, 2, pack, nz),
            f32(turns, 2, nl, ny, LANES),
            both, both, both, both,
            f32(2, 2, ny, nz),
            f32(2, nl, ROWS, nz),
            f32(2, nl, ny, LANES),
            both, both, both,
            pltpu.SemaphoreType.DMA((4,)),
            pltpu.SemaphoreType.DMA((turns, 4, 2)),
            pltpu.SemaphoreType.DMA((turns, 4, 2)),
        ],
        compiler_params=pltpu.CompilerParams(
            collective_id=0, has_side_effects=True, vmem_limit_bytes=16 * 2**20),
    )(low_bound, high_bound, log_perm, source)
    total = sol + last
    fine = total[:nx]
    return fine, fine - jnp.repeat(total[nx:], 2, axis=0)


def solution(mesh):
    sizes = {axis: mesh.shape[axis] for axis in AXES}
    spec = P(("groups", "gx"), "gy", "gz")
    return jax.shard_map(
        functools.partial(shards, sizes),
        mesh=mesh,
        in_specs=(spec, spec, P(), P()),
        out_specs=(spec, spec),
        check_vma=False,
    )
```

```python
import functools

import jax
import jax.numpy as jnp
from jax import lax
from jax.experimental import pallas as pl
from jax.experimental.pallas import tpu as pltpu
from jax.sharding import PartitionSpec as P

DEGREE = 3
REACH = DEGREE + 1
STORAGE = 0.1
LANES = 128
ROWS = 8
MESH = pl.DeviceIdType.MESH
AXES = ("gx", "gy", "gz")


def roll(a, shift, axis):
    return pltpu.roll(a, shift % a.shape[axis], axis)


def iota(shape, axis):
    return lax.broadcasted_iota(jnp.int32, shape, axis)


def even(shape, axis):
    return iota(shape, axis) % 2 == 0


def pair_sum(a, axis):
    return a + jnp.where(even(a.shape, axis), roll(a, -1, axis), roll(a, 1, axis))


def pooled(a, b):
    return pair_sum(pair_sum(a + b, 0), 1)


def inverse(a):
    r = pl.reciprocal(a, approx=True)
    return r * (2.0 - a * r)


def pick(condition, a, b):
    if isinstance(condition, bool):
        return a if condition else b
    return jnp.where(condition, a, b)


def both(a, b):
    if a is True:
        return b
    return a if b is True else jnp.logical_and(a, b)


def when(condition, act):
    if condition is True:
        act()
    else:
        pl.when(condition)(act)


def sides(size):
    return min(size - 1, 2)


def kernel(sizes, low_hbm, high_hbm, log_hbm, src_hbm, part, last, coarse,
           low_ref, high_ref, logs, srcs, packs, own_pack, own_rows, got_rows,
           inv_k, t_x, t_y, t_z, inv_d, res, dirs1, dirs2, dirs3,
           c_inv_k, c_t_x, c_t_y, c_t_z, c_inv_d, c_res, c_dirs1, c_dirs2, c_dirs3,
           io_sem, send_sem, recv_sem):
    nx, ny, nz = log_hbm.shape
    half = nz // 2
    wide_y, wide_z = logs.shape[1:]
    me = {axis: lax.axis_index(axis) for axis in AXES}
    count_x = sizes["gx"]
    x = me["gx"]

    def slots_x(step):
        return [({"gx": x + step}, x + step < count_x, x >= step, 0),
                ({"gx": x - step}, x >= step, x + step < count_x, 1)]

    def ring(axis, length, tile):
        n, here = sizes[axis], me[axis]
        if n == 1:
            return []
        if n == 2:
            start = pl.multiple_of((1 - here) * (length - tile), tile)
            return [dict(to={axis: 1 - here}, send=True, get=True, start=start, place=length,
                         send_high=here == 0, get_high=here == 1, index=0)]
        return [dict(to={axis: here - 1}, send=here > 0, get=here < n - 1, start=0, place=length,
                     send_high=False, get_high=False, index=0),
                dict(to={axis: here + 1}, send=here < n - 1, get=here > 0, start=length - tile,
                     place=length + tile, send_high=True, get_high=True, index=1)]

    ring_y = ring("gy", ny, ROWS)
    ring_z = ring("gz", nz, LANES)

    def packed_start(z):
        if isinstance(z["start"], int):
            return z["start"] * (half - LANES) // (nz - LANES)
        return pl.multiple_of((1 - me["gz"]) * (half - LANES), LANES)

    used = []

    class Message:
        def __init__(self, to, send, get, source, target):
            index = len(used)
            used.append(index)
            self.send, self.get = send, get
            self.copy = lambda: pltpu.make_async_remote_copy(
                src_ref=source, dst_ref=target, send_sem=send_sem.at[index],
                recv_sem=recv_sem.at[index], device_id=to, device_id_type=MESH)

    def start(messages):
        for m in messages:
            when(m.send, lambda: m.copy().start())

    def arrive(messages):
        for m in messages:
            when(m.get, lambda: m.copy().wait_recv())

    def drain(messages):
        for m in messages:
            when(m.send, lambda: m.copy().wait_send())

    partners = [(to, send) for step in (1, 2) for to, send, _, _ in slots_x(step)]
    partners += [(r["to"], r["send"]) for r in ring_y + ring_z]
    partners += [({**a["to"], **b["to"]}, both(a["send"], b["send"])) for a in ring_y for b in ring_z]
    partners += [({**to, **a["to"]}, both(send, a["send"]))
                 for step in (1, 2) for to, send, _, _ in slots_x(step) for a in ring_y]
    barrier = pltpu.get_barrier_semaphore()
    count = 0
    for to, send in partners:
        when(send, lambda: pl.semaphore_signal(barrier, inc=1, device_id=to, device_id_type=MESH))
        count = count + (1 if send is True else send.astype(jnp.int32))

    own = pl.ds(REACH, nx)
    own_s = pl.ds(DEGREE, nx)
    log_in = pltpu.make_async_copy(log_hbm, logs.at[own, 0:ny, 0:nz], io_sem.at[0])
    src_in = pltpu.make_async_copy(src_hbm, srcs.at[own_s, 0:ny, 0:nz], io_sem.at[1])
    low_in = pltpu.make_async_copy(low_hbm, low_ref, io_sem.at[2])
    high_in = pltpu.make_async_copy(high_hbm, high_ref, io_sem.at[3])
    for copy in (log_in, src_in, low_in, high_in):
        copy.start()

    def plane(hbm, ref, layers):
        edge = [Message(b["to"], b["send"], b["get"],
                        hbm.at[:, :, pl.ds(b["start"], LANES)],
                        ref.at[layers, 0:ny, pl.ds(b["place"], LANES)]) for b in ring_z]
        edge += [Message(a["to"], a["send"], a["get"],
                         hbm.at[:, pl.ds(a["start"], ROWS), :],
                         ref.at[layers, pl.ds(a["place"], ROWS), 0:nz]) for a in ring_y]
        edge += [Message({**a["to"], **b["to"]}, both(a["send"], b["send"]), both(a["get"], b["get"]),
                         hbm.at[:, pl.ds(a["start"], ROWS), pl.ds(b["start"], LANES)],
                         ref.at[layers, pl.ds(a["place"], ROWS), pl.ds(b["place"], LANES)])
                 for a in ring_y for b in ring_z]
        return edge

    def span(side, first, last_, base):
        if side == 0:
            return pl.ds(nx - last_, last_ - first + 1), pl.ds(base - last_, last_ - first + 1)
        return pl.ds(first - 1, last_ - first + 1), pl.ds(base + nx + first - 1, last_ - first + 1)

    def along(hbm, ref, base, first, last_):
        out = []
        for to, send, get, side in slots_x(1):
            mine, theirs = span(side, first, last_, base)
            out.append(Message(to, send, get, hbm.at[mine], ref.at[theirs, 0:ny, 0:nz]))
        return out

    def relay(ref, base, first, last_):
        out = []
        for _, _, get, side in slots_x(1):
            _, there = span(side, first, last_, base)
            for b in ring_z:
                out.append(Message(b["to"], both(b["send"], get), both(b["get"], get),
                                   ref.at[there, :, pl.ds(b["start"], LANES)],
                                   ref.at[there, :, pl.ds(b["place"], LANES)]))
        return out

    plane_log = plane(log_hbm, logs, own)
    plane_src = plane(src_hbm, srcs, own_s)
    x_log = {1: along(log_hbm, logs, REACH, 1, 2), 3: along(log_hbm, logs, REACH, 3, 3),
             4: along(log_hbm, logs, REACH, 4, 4)}
    x_src = {i: along(src_hbm, srcs, DEGREE, i, i) for i in (1, 2, 3)}
    z_log = {1: relay(logs, REACH, 1, 2), 3: relay(logs, REACH, 3, 3)}
    z_src = {i: relay(srcs, DEGREE, i, i) for i in (1, 2)}
    rows = [Message({**to, **a["to"]}, both(send, a["send"]), both(get, a["get"]),
                    own_rows.at[side, a["index"]], got_rows.at[side, a["index"]])
            for to, send, get, side in slots_x(1) for a in ring_y]

    def pack_messages(step):
        kinds = pl.ds(0, 3 - step)
        whole = [Message(to, send, get, own_pack, packs.at[side, step - 1, :, 0:ny, 0:half])
                 for to, send, get, side in slots_x(step)]
        edge = [Message({**to, **a["to"]}, both(send, a["send"]), both(get, a["get"]),
                        own_pack.at[kinds, pl.ds(a["start"], ROWS), :],
                        packs.at[side, step - 1, kinds, pl.ds(a["place"], ROWS), 0:half])
                for to, send, get, side in slots_x(step) for a in ring_y]
        return whole + edge

    def pack_relay(step):
        kinds = pl.ds(0, 3 - step)
        return [Message(b["to"], both(b["send"], get), both(b["get"], get),
                        packs.at[side, step - 1, kinds, :, pl.ds(packed_start(b), LANES)],
                        packs.at[side, step - 1, kinds, :, pl.ds(half + b["place"] - nz, LANES)])
                for _, _, get, side in slots_x(step) for b in ring_z]

    packs_in = {step: pack_messages(step) for step in (1, 2)}
    z_packs = {step: pack_relay(step) for step in (1, 2)}

    def clear(ref, *at):
        ref[at] = jnp.zeros_like(ref[at])

    for layer in (0, REACH + nx + REACH - 1):
        clear(logs, layer, slice(ny, wide_y), slice(None))
        clear(logs, layer, slice(0, ny), slice(nz, wide_z))
    for layer in (0, DEGREE + nx + DEGREE - 1):
        clear(srcs, layer, slice(ny, wide_y), slice(None))
        clear(srcs, layer, slice(0, ny), slice(nz, wide_z))
    for side in (0, 1):
        clear(packs, side, 1, 1, slice(ny, wide_y), slice(None))
        clear(packs, side, 1, 1, slice(0, ny), slice(half, packs.shape[4]))
    for step in (1, 2):
        for _, _, get, side in slots_x(step):
            @pl.when(jnp.logical_not(get))
            def _():
                clear(packs, side, step - 1)
                if step == 1:
                    clear(got_rows, side)
                    for i in range(1, REACH + 1):
                        layer = (-i, nx - 1 + i)[side]
                        clear(logs, REACH + layer)
                        if i < REACH:
                            clear(srcs, DEGREE + layer)
    for a in ring_y:
        if a["get"] is not True:
            @pl.when(jnp.logical_not(a["get"]))
            def _():
                at = slice(a["place"], a["place"] + ROWS)
                for layer in range(nx + 2 * REACH):
                    clear(logs, layer, at)
                for layer in range(nx + 2 * DEGREE):
                    clear(srcs, layer, at)
                for side in (0, 1):
                    for step in (1, 2):
                        clear(packs, side, step - 1, slice(None), at)
                    clear(got_rows, side, a["index"])

    pl.semaphore_wait(barrier, count)
    start(x_log[1])
    start(plane_log)
    start(x_src[1])
    start(plane_src)

    def pair_block(ref, base, at):
        a = pooled(ref[(base,) + at], ref[(base + 1,) + at])
        b = pooled(ref[(base + 2,) + at], ref[(base + 3,) + at])
        return jnp.where(even(a.shape, 0), a, b)

    core = (slice(0, ny), slice(0, nz))
    rims = []
    if wide_y > ny:
        rims.append((slice(ny, wide_y), slice(0, wide_z)))
    if wide_z > nz:
        rims.append((slice(0, ny), slice(nz, wide_z)))

    def pack_own(kind, a):
        own_pack[kind] = jnp.where(even((ny, half), 1), a[:, :half], a[:, half:])

    spot = iota((ROWS, nz), 0)

    log_in.wait()
    block = pair_block(logs, REACH, core) * 0.125
    pack_own(0, block)
    c_inv_k[(0,) + core] = jnp.exp(-block)

    def pack_rows(side, a, kind, ref, base):
        def edge(i):
            layer = (nx - i, i - 1)[side]
            return ref[base + layer, pl.ds(a["start"], ROWS), 0:nz]
        high = a["send_high"]
        if kind == 0:
            one, two, three = edge(1), edge(2), edge(3)
            two = pick(high, roll(two, 5, 0), roll(two, 3, 0))
            three = pick(high, roll(three, 3, 0), roll(three, 5, 0))
            first = pick(high, spot - 5, 2 - spot) >= 0
            second = (spot == 3) | (spot == 4)
            own_rows[side, a["index"], 0] = jnp.where(first, one, jnp.where(second, two, three))
        else:
            one, two = edge(1), edge(2)
            two = pick(high, roll(two, 6, 0), roll(two, 2, 0))
            first = pick(high, spot - 6, 1 - spot) >= 0
            own_rows[side, a["index"], 1] = jnp.where(first, one, two)

    for side in (0, 1):
        for a in ring_y:
            pack_rows(side, a, 0, logs, REACH)
    src_in.wait()
    for side in (0, 1):
        for a in ring_y:
            pack_rows(side, a, 1, srcs, DEGREE)
    start(rows)
    block = pair_block(srcs, DEGREE, core)
    pack_own(1, block)
    c_res[(0,) + core] = block
    start(packs_in[1])
    start(x_log[3])
    start(packs_in[2])
    start(x_src[2])
    start(x_log[4])
    start(x_src[3])

    row = iota((wide_y, wide_z), 0)
    lane = iota((wide_y, wide_z), 1)

    def cuts(axis, ring_, length, total, tile):
        n, here = sizes[axis], me[axis]
        if n == 1:
            return [total - 1]
        if n == 2:
            return [jnp.where(here == 0, total - 1, length - 1)]
        return [length + tile - 1, jnp.where(here < n - 1, -1, length - 1),
                jnp.where(here > 0, -1, total - 1)]

    cuts_y = cuts("gy", ring_y, ny, wide_y, ROWS)
    cuts_z = cuts("gz", ring_z, nz, wide_z, LANES)

    def cut(t, index, at):
        for c in at:
            t = jnp.where(index == c, 0.0, t)
        return t

    row_pair, lane_pair = row | 1, lane | 1
    even_row = even((wide_y, wide_z), 0)

    def fine_k(i):
        inv_k[REACH + i] = jnp.exp(-logs[REACH + i])

    def fine_yz(i):
        mine = inv_k[REACH + i]
        t_y[DEGREE + i] = cut(2.0 * inverse(mine + roll(mine, -1, 0)), row, cuts_y)
        t_z[DEGREE + i] = cut(2.0 * inverse(mine + roll(mine, -1, 1)), lane, cuts_z)

    flag = {(step, side): get.astype(jnp.float32)
            for step in (1, 2) for _, _, get, side in slots_x(step)}

    def fine_x(i):
        t = 2.0 * inverse(inv_k[REACH + i] + inv_k[REACH + i + 1])
        if i == -1:
            t = t * flag[1, 0]
        if i == nx - 1:
            t = t * flag[1, 1]
        t_x[REACH + i] = t

    def fine_d(i):
        y, z = t_y[DEGREE + i], t_z[DEGREE + i]
        total = (y + roll(y, 1, 0)) + (z + roll(z, 1, 1)) + (t_x[REACH + i] + t_x[REACH + i - 1])
        inv_d[DEGREE + i] = inverse(total + STORAGE)

    def coarse_yz(i):
        mine = c_inv_k[i]
        c_t_y[i] = cut(4.0 * inverse(mine + roll(mine, -2, 0)), row_pair, cuts_y)
        c_t_z[i] = cut(4.0 * inverse(mine + roll(mine, -2, 1)), lane_pair, cuts_z)

    def swap(a):
        return jnp.where(even_row, roll(a, -1, 0), roll(a, 1, 0))

    def coarse_x(i):
        if i < 0:
            mine = c_inv_k[0]
            c_t_x[0] = 4.0 * inverse(mine + swap(mine))
            return
        t = 4.0 * inverse(c_inv_k[i] + c_inv_k[i + 1])
        if i in (0, 2):
            step = i // 2 + 1
            t = t * jnp.where(even_row, flag[step, 0], flag[step, 1])
        c_t_x[i + 1] = t

    def coarse_d(i):
        y, z = c_t_y[i], c_t_z[i]
        total = (y + roll(y, 2, 0)) + (z + roll(z, 2, 1)) + (c_t_x[i] + c_t_x[i + 1])
        c_inv_d[i] = inverse(total + 8.0 * STORAGE)

    low_in.wait()
    high_in.wait()
    low = jnp.full((1, wide_z), low_ref[0])
    high = jnp.full((1, wide_z), high_ref[0])
    theta = (high + low) * 0.5
    delta = (high - low) * 0.5
    sigma = theta / delta
    rho = 1.0 / sigma
    inv_theta = 1.0 / theta
    keep, gain = [None], [None]
    for _ in range(DEGREE):
        rho_next = 1.0 / (2.0 * sigma - rho)
        keep.append(rho_next * rho)
        gain.append(2.0 * rho_next / delta)
        rho = rho_next

    def fine_first(i):
        dirs1[DEGREE + i] = srcs[DEGREE + i] * inv_d[DEGREE + i] * inv_theta

    def coarse_first(i):
        c_dirs1[i] = c_res[i] * c_inv_d[i] * inv_theta

    fields = [None, dirs1, dirs2, dirs3]
    c_fields = [None, c_dirs1, c_dirs2, c_dirs3]

    def fine_turn(turn, i):
        ref, base = fields[turn], DEGREE + 1 - turn
        d = ref[base + i]
        y = t_y[DEGREE + i] * (d - roll(d, -1, 0))
        z = t_z[DEGREE + i] * (d - roll(d, -1, 1))
        r = (srcs if turn == 1 else res)[DEGREE + i] - STORAGE * d
        r = r - (y - roll(y, 1, 0)) - (z - roll(z, 1, 1))
        r = r - t_x[REACH + i] * (d - ref[base + i + 1])
        r = r - t_x[REACH + i - 1] * (d - ref[base + i - 1])
        later = keep[turn] * d + gain[turn] * (r * inv_d[DEGREE + i])
        if turn < DEGREE:
            res[DEGREE + i] = r
            fields[turn + 1][base - 1 + i] = later
        else:
            part[i] = (dirs1[DEGREE + i] + dirs2[DEGREE - 1 + i] + d)[:ny, :nz]
            last[i] = later[:ny, :nz]

    def coarse_turn(turn, i):
        ref = c_fields[turn]
        d = ref[i]
        y = c_t_y[i] * (d - roll(d, -2, 0))
        z = c_t_z[i] * (d - roll(d, -2, 1))
        r = c_res[i] - 8.0 * STORAGE * d
        r = r - (y - roll(y, 2, 0)) - (z - roll(z, 2, 1))
        r = r - c_t_x[i + 1] * (d - ref[i + 1])
        r = r - c_t_x[i] * (d - (swap(d) if i == 0 else ref[i - 1]))
        later = keep[turn] * d + gain[turn] * (r * c_inv_d[i])
        if turn < DEGREE:
            c_res[i] = r
            c_fields[turn + 1][i] = later
        else:
            total = (c_dirs1[i] + c_dirs2[i] + d + later)[:ny, :nz]
            top = even((ny, nz), 0)
            coarse[0] = jnp.where(top, total, roll(total, 1, 0))
            coarse[1] = jnp.where(top, roll(total, -1, 0), total)

    def unpack_rows(side, kind):
        ref, base = (logs, REACH) if kind == 0 else (srcs, DEGREE)
        for a in ring_y:
            got = got_rows[side, a["index"], kind]
            up = a["get_high"]
            at = slice(a["place"], a["place"] + ROWS)
            shifts = [(3, 5), (5, 3)] if kind == 0 else [(2, 6)]
            ref[base + (-1, nx)[side], at, 0:nz] = got
            for i, (if_high, if_low) in enumerate(shifts):
                layer = (-2 - i, nx + 1 + i)[side]
                ref[base + layer, at, 0:nz] = pick(up, roll(got, if_high, 0), roll(got, if_low, 0))

    def spread(step, kind, near):
        left, right = packs[0, step - 1, kind], packs[1, step - 1, kind]
        top = even(left.shape, 0)
        if near:
            a = jnp.where(top, roll(left, -1, 0), roll(right, 1, 0))
        else:
            a = jnp.where(top, left, right)
        main = a[:, :half]
        even_lane = even(main.shape, 1)
        pieces = [jnp.where(even_lane, main, roll(main, 1, 1)),
                  jnp.where(even_lane, roll(main, -1, 1), main)]
        for b in ring_z:
            at = half + b["place"] - nz
            tile = a[:, at:at + LANES]
            even_lane = even(tile.shape, 1)
            pieces.append(pick(b["get_high"], jnp.where(even_lane, roll(tile, -1, 1), tile),
                               jnp.where(even_lane, tile, roll(tile, 1, 1))))
        return jnp.concatenate(pieces, axis=1)

    def halo(i):
        return (-i, nx - 1 + i)

    mine = range(nx)
    inner = range(1, nx - 1)
    ends = (0, nx - 1)

    arrive(plane_log)
    for i in mine:
        fine_k(i)
    for i in mine:
        fine_yz(i)
    for i in inner:
        fine_x(i - 1)
    fine_x(nx - 2)
    for at in rims:
        c_inv_k[(0,) + at] = jnp.exp(-0.125 * pair_block(logs, REACH, at))
    coarse_yz(0)
    coarse_x(-1)
    for i in inner:
        fine_d(i)
    arrive(plane_src)
    for at in rims:
        c_res[(0,) + at] = pair_block(srcs, DEGREE, at)
    for i in inner:
        fine_first(i)

    arrive(x_log[1])
    arrive(rows)
    for side in (0, 1):
        unpack_rows(side, 0)
        unpack_rows(side, 1)
    start(z_log[1])
    arrive(x_src[1])
    start(z_src[1])
    arrive(packs_in[1])
    start(z_packs[1])
    arrive(z_log[1])
    for i in halo(1) + halo(2):
        fine_k(i)
    for i in halo(1):
        fine_yz(i)
    for i in (-2, -1, nx - 1, nx):
        fine_x(i)
    for i in ends + halo(1):
        fine_d(i)
    for i in ends:
        fine_first(i)
    for i in inner:
        fine_turn(1, i)
    arrive(z_src[1])
    for i in halo(1):
        fine_first(i)
    for i in ends:
        fine_turn(1, i)
    for i in inner:
        fine_turn(2, i)

    arrive(z_packs[1])
    c_inv_k[1] = jnp.exp(-spread(1, 0, True))
    c_inv_k[2] = jnp.exp(-spread(1, 0, False))
    c_res[1] = spread(1, 1, True)
    c_res[2] = spread(1, 1, False)
    coarse_yz(1)
    coarse_x(0)
    coarse_x(1)
    coarse_yz(2)
    for i in (0, 1):
        coarse_d(i)
        coarse_first(i)
    coarse_turn(1, 0)

    arrive(x_log[3])
    start(z_log[3])
    arrive(packs_in[2])
    start(z_packs[2])
    arrive(x_src[2])
    start(z_src[2])
    arrive(z_log[3])
    for i in halo(3):
        fine_k(i)
    for i in halo(2):
        fine_yz(i)
    for i in (-3, nx + 1):
        fine_x(i)
    for i in halo(2):
        fine_d(i)

    arrive(z_packs[2])
    c_inv_k[3] = jnp.exp(-spread(2, 0, True))
    c_inv_k[4] = jnp.exp(-spread(2, 0, False))
    c_res[3] = spread(2, 1, True)
    coarse_yz(3)
    coarse_x(2)
    coarse_x(3)
    for i in (2, 3):
        coarse_d(i)
        coarse_first(i)
    coarse_turn(1, 1)
    coarse_turn(1, 2)
    coarse_turn(2, 0)
    coarse_turn(2, 1)
    coarse_turn(3, 0)

    arrive(z_src[2])
    for i in halo(2):
        fine_first(i)
    for i in halo(1):
        fine_turn(1, i)
    for i in ends:
        fine_turn(2, i)
    for i in inner:
        fine_turn(3, i)
    for i in halo(3):
        fine_yz(i)

    arrive(x_log[4])
    for i in halo(4):
        fine_k(i)
    for i in (-4, nx + 2):
        fine_x(i)
    for i in halo(3):
        fine_d(i)
    arrive(x_src[3])
    for i in halo(3):
        fine_first(i)
    for i in halo(2):
        fine_turn(1, i)
    for i in halo(1):
        fine_turn(2, i)
    for i in ends:
        fine_turn(3, i)

    for group in ([plane_log, plane_src, rows] + list(x_log.values()) + list(x_src.values())
                  + list(z_log.values()) + list(z_src.values())
                  + list(packs_in.values()) + list(z_packs.values())):
        drain(group)


def shards(sizes, log_perm, source, low_bound, high_bound):
    nx, ny, nz = log_perm.shape
    wide_y = ny + ROWS * sides(sizes["gy"])
    wide_z = nz + LANES * sides(sizes["gz"])
    half = nz // 2
    f32 = lambda *shape: pltpu.VMEM(shape, jnp.float32)
    fine = lambda reach: f32(nx + 2 * reach, wide_y, wide_z)
    pairs = lambda n: f32(n, wide_y, wide_z)
    log_perm = pltpu.with_memory_space_constraint(log_perm, pltpu.HBM)
    source = pltpu.with_memory_space_constraint(source, pltpu.HBM)
    hbm = pl.BlockSpec(memory_space=pltpu.HBM)
    vmem = pl.BlockSpec(memory_space=pltpu.VMEM)
    whole = jax.ShapeDtypeStruct((nx, ny, nz), jnp.float32)
    messages = 96
    part, last, coarse = pl.pallas_call(
        functools.partial(kernel, sizes),
        out_shape=(whole, whole, jax.ShapeDtypeStruct((nx // 2, ny, nz), jnp.float32)),
        in_specs=[hbm] * 4,
        out_specs=(vmem,) * 3,
        scratch_shapes=[
            pltpu.SMEM((1,), jnp.float32),
            pltpu.SMEM((1,), jnp.float32),
            fine(REACH), fine(DEGREE),
            f32(2, 2, 2, wide_y, half + wide_z - nz),
            f32(2, ny, half),
            f32(2, max(1, sides(sizes["gy"])), 2, ROWS, nz),
            f32(2, max(1, sides(sizes["gy"])), 2, ROWS, nz),
            fine(REACH), fine(REACH), fine(DEGREE), fine(DEGREE), fine(DEGREE), fine(DEGREE),
            fine(DEGREE), fine(DEGREE - 1), fine(DEGREE - 2),
            pairs(5), pairs(5), pairs(4), pairs(4), pairs(4), pairs(4), pairs(4), pairs(3), pairs(2),
            pltpu.SemaphoreType.DMA((4,)),
            pltpu.SemaphoreType.DMA((messages,)),
            pltpu.SemaphoreType.DMA((messages,)),
        ],
        compiler_params=pltpu.CompilerParams(
            collective_id=0, has_side_effects=True, vmem_limit_bytes=24 * 2**20),
    )(low_bound, high_bound, log_perm, source)
    fine_pressure = part + last
    return fine_pressure, fine_pressure - jnp.repeat(coarse, 2, axis=0)


def solution(mesh):
    sizes = {axis: mesh.shape[axis] for axis in AXES}
    spec = P(("groups", "gx"), "gy", "gz")
    return jax.shard_map(
        functools.partial(shards, sizes),
        mesh=mesh,
        in_specs=(spec, spec, P(), P()),
        out_specs=(spec, spec),
        check_vma=False,
    )
```

```python
import functools

import jax
import jax.numpy as jnp
from jax import lax
from jax.experimental import pallas as pl
from jax.experimental.pallas import tpu as pltpu
from jax.sharding import PartitionSpec as P

DEGREE = 3
REACH = DEGREE
STORAGE = 0.1
LANES = 128
ROWS = 8
MESH = pl.DeviceIdType.MESH
AXES = ("gx", "gy", "gz")


def roll(a, shift, axis):
    return pltpu.roll(a, shift % a.shape[axis], axis)


def iota(shape, axis):
    return lax.broadcasted_iota(jnp.int32, shape, axis)


def even(shape, axis):
    return iota(shape, axis) % 2 == 0


def pair_sum(a, axis):
    return a + jnp.where(even(a.shape, axis), roll(a, -1, axis), roll(a, 1, axis))


def pooled(a, b):
    return pair_sum(pair_sum(a + b, 0), 1)


def inverse(a):
    r = pl.reciprocal(a, approx=True)
    return r * (2.0 - a * r)


def pick(condition, a, b):
    if isinstance(condition, bool):
        return a if condition else b
    return jnp.where(condition, a, b)


def both(a, b):
    if a is True:
        return b
    return a if b is True else jnp.logical_and(a, b)


def when(condition, act):
    if condition is True:
        act()
    else:
        pl.when(condition)(act)


def sides(size):
    return min(size - 1, 2)


def kernel(sizes, low_hbm, high_hbm, log_hbm, src_hbm, part, last, coarse,
           low_ref, high_ref, logs, srcs, packs, own_pack, own_rows, got_rows, own_lanes, got_lanes,
           own_far, got_far, own_corner, got_corner,
           inv_k, t_x, t_y, t_z, inv_d, res, dirs1, dirs2, dirs3,
           c_inv_k, c_t_x, c_t_y, c_t_z, c_inv_d, c_res, c_dirs1, c_dirs2, c_dirs3,
           io_sem, send_sem, recv_sem):
    nx, ny, nz = log_hbm.shape
    half = nz // 2
    wide_y, wide_z = logs.shape[1:]
    me = {axis: lax.axis_index(axis) for axis in AXES}
    count_x = sizes["gx"]
    x = me["gx"]

    def slots_x(step):
        return [({"gx": x + step}, x + step < count_x, x >= step, 0),
                ({"gx": x - step}, x >= step, x + step < count_x, 1)]

    def ring(axis, length, tile):
        n, here = sizes[axis], me[axis]
        if n == 1:
            return []
        if n == 2:
            start = pl.multiple_of((1 - here) * (length - tile), tile)
            return [dict(to={axis: 1 - here}, send=True, get=True, start=start, place=length,
                         send_high=here == 0, get_high=here == 1, index=0)]
        return [dict(to={axis: here - 1}, send=here > 0, get=here < n - 1, start=0, place=length,
                     send_high=False, get_high=False, index=0),
                dict(to={axis: here + 1}, send=here < n - 1, get=here > 0, start=length - tile,
                     place=length + tile, send_high=True, get_high=True, index=1)]

    ring_y = ring("gy", ny, ROWS)
    ring_z = ring("gz", nz, LANES)

    def packed_start(b):
        if isinstance(b["start"], int):
            return b["start"] * (half - LANES) // (nz - LANES)
        return pl.multiple_of((1 - me["gz"]) * (half - LANES), LANES)

    used = []

    class Message:
        def __init__(self, to, send, get, source, target):
            index = len(used)
            used.append(index)
            self.send, self.get = send, get
            self.copy = lambda: pltpu.make_async_remote_copy(
                src_ref=source, dst_ref=target, send_sem=send_sem.at[index],
                recv_sem=recv_sem.at[index], device_id=to, device_id_type=MESH)

    def start(messages):
        for m in messages:
            when(m.send, lambda: m.copy().start())

    def arrive(messages):
        for m in messages:
            when(m.get, lambda: m.copy().wait_recv())

    def drain(messages):
        for m in messages:
            when(m.send, lambda: m.copy().wait_send())

    partners = [(to, send) for step in (1, 2) for to, send, _, _ in slots_x(step)]
    partners += [(r["to"], r["send"]) for r in ring_y + ring_z]
    partners += [({**a["to"], **b["to"]}, both(a["send"], b["send"])) for a in ring_y for b in ring_z]
    partners += [({**to, **a["to"]}, both(send, a["send"]))
                 for to, send, _, _ in slots_x(1) for a in ring_y]
    barrier = pltpu.get_barrier_semaphore()
    count = 0
    for to, send in partners:
        when(send, lambda: pl.semaphore_signal(barrier, inc=1, device_id=to, device_id_type=MESH))
        count = count + (1 if send is True else send.astype(jnp.int32))

    own = pl.ds(REACH, nx)
    own_s = pl.ds(DEGREE, nx)
    log_in = pltpu.make_async_copy(log_hbm, logs.at[own, 0:ny, 0:nz], io_sem.at[0])
    src_in = pltpu.make_async_copy(src_hbm, srcs.at[own_s, 0:ny, 0:nz], io_sem.at[1])
    low_in = pltpu.make_async_copy(low_hbm, low_ref, io_sem.at[2])
    high_in = pltpu.make_async_copy(high_hbm, high_ref, io_sem.at[3])
    for copy in (log_in, src_in, low_in, high_in):
        copy.start()

    def plane_z(hbm, ref, layers):
        return [Message(b["to"], b["send"], b["get"],
                        hbm.at[:, :, pl.ds(b["start"], LANES)],
                        ref.at[layers, 0:ny, pl.ds(b["place"], LANES)]) for b in ring_z]

    def plane_y(hbm, ref, layers):
        edge = [Message(a["to"], a["send"], a["get"],
                        hbm.at[:, pl.ds(a["start"], ROWS), :],
                        ref.at[layers, pl.ds(a["place"], ROWS), 0:nz]) for a in ring_y]
        edge += [Message({**a["to"], **b["to"]}, both(a["send"], b["send"]), both(a["get"], b["get"]),
                         hbm.at[:, pl.ds(a["start"], ROWS), pl.ds(b["start"], LANES)],
                         ref.at[layers, pl.ds(a["place"], ROWS), pl.ds(b["place"], LANES)])
                 for a in ring_y for b in ring_z]
        return edge

    def span(side, first, last_, base):
        if side == 0:
            return pl.ds(nx - last_, last_ - first + 1), pl.ds(base - last_, last_ - first + 1)
        return pl.ds(first - 1, last_ - first + 1), pl.ds(base + nx + first - 1, last_ - first + 1)

    def along(hbm, ref, base, first, last_):
        out = []
        for to, send, get, side in slots_x(1):
            mine, theirs = span(side, first, last_, base)
            out.append(Message(to, send, get, hbm.at[mine], ref.at[theirs, 0:ny, 0:nz]))
        return out

    z_log = plane_z(log_hbm, logs, own)
    z_src = plane_z(src_hbm, srcs, own_s)
    y_log = plane_y(log_hbm, logs, own)
    y_src = plane_y(src_hbm, srcs, own_s)
    x_log = {1: along(log_hbm, logs, REACH, 1, 2), 3: along(log_hbm, logs, REACH, 3, 3)}
    x_src = {i: along(src_hbm, srcs, DEGREE, i, i) for i in (1, 2)}
    x_dir = [Message(to, send, get, dirs1.at[DEGREE + (nx - DEGREE, DEGREE - 1)[side], 0:ny, 0:nz],
                     dirs1.at[DEGREE + (-DEGREE, nx - 1 + DEGREE)[side], 0:ny, 0:nz])
             for to, send, get, side in slots_x(1)]
    rows = [Message({**to, **a["to"]}, both(send, a["send"]), both(get, a["get"]),
                    own_rows.at[side, a["index"]], got_rows.at[side, a["index"]])
            for to, send, get, side in slots_x(1) for a in ring_y]
    lanes = [Message(to, both(send, b["get"]), both(get, b["get"]),
                     own_lanes.at[side, b["index"]], got_lanes.at[0, side, b["index"]])
             for to, send, get, side in slots_x(1) for b in ring_z]
    corner = [Message({**to, **a["to"]}, both(send, both(a["send"], b["get"])), both(get, both(a["get"], b["get"])),
                      own_corner.at[side, a["index"], b["index"]], got_corner.at[side, a["index"], b["index"]])
              for to, send, get, side in slots_x(1) for a in ring_y for b in ring_z]
    packs_near = [Message(to, send, get, own_pack.at[:, :, 0:half],
                          packs.at[side, 0, :, 0:ny, 0:half]) for to, send, get, side in slots_x(1)]
    packs_edge = [Message({**to, **a["to"]}, both(send, a["send"]), both(get, a["get"]),
                          own_pack.at[:, pl.ds(a["start"], ROWS), 0:half],
                          packs.at[side, 0, :, pl.ds(a["place"], ROWS), 0:half])
                  for to, send, get, side in slots_x(1) for a in ring_y]
    packs_far = [Message(to, send, get, own_pack.at[0, :, 0:half],
                         packs.at[side, 1, 0, 0:ny, 0:half]) for to, send, get, side in slots_x(2)]
    packs_far += [Message(to, send, get, own_far.at[side], got_far.at[side])
                  for to, send, get, side in slots_x(2)]
    far = [get for _, _, get, _ in slots_x(2)]
    pass_y = [Message(a["to"], both(a["send"], far[side]), both(a["get"], far[side]),
                      packs.at[side, 1, 0, pl.ds(a["start"], ROWS), 0:half],
                      packs.at[side, 1, 0, pl.ds(a["place"], ROWS), 0:half])
              for side in (0, 1) for a in ring_y]
    pass_z = [Message(b["to"], both(b["send"], far[side]), both(b["get"], far[side]),
                      packs.at[side, 1, 0, 0:ny, pl.ds(packed_start(b), LANES)],
                      got_lanes.at[1, side, b["index"]])
              for side in (0, 1) for b in ring_z]

    def pair_block(ref, base, at):
        a = pooled(ref[(base,) + at], ref[(base + 1,) + at])
        b = pooled(ref[(base + 2,) + at], ref[(base + 3,) + at])
        return jnp.where(even(a.shape, 0), a, b)

    tile_lane = iota((ny, LANES), 1)

    def pack_rows(side, a, kind, at):
        ref, base = ((logs, REACH), (srcs, DEGREE))[kind]

        def edge(i):
            layer = (nx - i, i - 1)[side]
            return ref[base + layer, pl.ds(a["start"], ROWS), at]
        high = a["send_high"]
        one, two = edge(1), edge(2)
        spot = iota(one.shape, 0)
        if kind == 0:
            three = edge(3)
            two = pick(high, roll(two, 5, 0), roll(two, 3, 0))
            three = pick(high, roll(three, 3, 0), roll(three, 5, 0))
            first = pick(high, spot - 5, 2 - spot) >= 0
            second = (spot == 3) | (spot == 4)
            return jnp.where(first, one, jnp.where(second, two, three))
        two = pick(high, roll(two, 6, 0), roll(two, 2, 0))
        first = pick(high, spot - 6, 1 - spot) >= 0
        return jnp.where(first, one, two)

    STRIP = 8

    def side_by_side(tiles, high):
        out = None
        for k, a in enumerate(tiles):
            a = pick(high, roll(a, STRIP * (k + 1), 1), roll(a, STRIP * k, 1))
            out = a if out is None else jnp.where(tile_lane[:a.shape[0]] >= STRIP * k, a, out)
        return out

    def strip(a, k, high):
        return pick(high, roll(a, -STRIP * (k + 1), 1), roll(a, -STRIP * k, 1))

    def tile_of(b):
        return (slice(b["place"], b["place"] + LANES),
                slice(half + b["place"] - nz, half + b["place"] - nz + LANES))

    def pack_lanes(side, b):
        at, at_pack = tile_of(b)
        tiles = [logs[REACH + (nx - i, i - 1)[side], 0:ny, at] for i in (1, 2, 3)]
        tiles += [srcs[DEGREE + (nx - i, i - 1)[side], 0:ny, at] for i in (1, 2)]
        tiles += [own_pack[kind, :, at_pack] for kind in (0, 1)]
        own_lanes[side, b["index"]] = side_by_side(tiles, b["get_high"])
        for a in ring_y:
            tiles = [pack_rows(side, a, kind, at) for kind in (0, 1)]
            tiles += [own_pack[kind, pl.ds(a["start"], ROWS), at_pack] for kind in (0, 1)]
            own_corner[side, a["index"], b["index"]] = side_by_side(tiles, b["get_high"])

    def unpack_far(side, b):
        tile = got_lanes[1, side, b["index"]]
        even_lane = even(tile.shape, 1)
        packs[side, 1, 0, 0:ny, tile_of(b)[1]] = pick(
            b["get_high"], jnp.where(even_lane, roll(tile, -1, 1), tile),
            jnp.where(even_lane, tile, roll(tile, 1, 1)))

    def unpack_lanes(side, b):
        got = got_lanes[0, side, b["index"]]
        at, at_pack = tile_of(b)
        high = b["get_high"]
        packs[side, 0, 0, 0:ny, at_pack] = strip(got, 5, high)
        packs[side, 0, 1, 0:ny, at_pack] = strip(got, 6, high)
        for i in (1, 2, 3):
            logs[REACH + (-i, nx - 1 + i)[side], 0:ny, at] = strip(got, i - 1, high)
        for i in (1, 2):
            srcs[DEGREE + (-i, nx - 1 + i)[side], 0:ny, at] = strip(got, i + 2, high)
        for a in ring_y:
            got = got_corner[side, a["index"], b["index"]]
            rows_at = slice(a["place"], a["place"] + ROWS)
            for kind in (0, 1):
                place_rows(side, a, kind, strip(got, kind, high), at)
                packs[side, 0, kind, rows_at, at_pack] = strip(got, kind + 2, high)

    def place_rows(side, a, kind, got, at):
        ref, base = ((logs, REACH), (srcs, DEGREE))[kind]
        rows_at = slice(a["place"], a["place"] + ROWS)
        shifts = ((3, 5), (5, 3)) if kind == 0 else ((2, 6),)
        ref[base + (-1, nx)[side], rows_at, at] = got
        for i, (if_high, if_low) in enumerate(shifts):
            layer = (-2 - i, nx + 1 + i)[side]
            ref[base + layer, rows_at, at] = pick(a["get_high"], roll(got, if_high, 0), roll(got, if_low, 0))

    core = (slice(0, ny), slice(0, nz))
    beside = (slice(0, ny), slice(nz, wide_z))
    rim = (slice(ny, wide_y), slice(0, wide_z))
    scales = (0.125, 1.0)
    whole = (logs, srcs)
    bases = (REACH, DEGREE)

    def own_coarse(kind, at):
        return pair_block(whole[kind], bases[kind], at) * scales[kind]

    def keep_coarse(kind, at, block):
        if kind == 0:
            c_inv_k[(0,) + at] = jnp.exp(-block)
        else:
            c_res[(0,) + at] = block

    def fold_lanes(a):
        return jnp.where(even((a.shape[0], half), 1), a[:, :half], a[:, half:nz])

    log_in.wait()
    block = own_coarse(0, core)
    own_pack[0, :, 0:half] = fold_lanes(block)
    keep_coarse(0, core, block)
    src_in.wait()
    block = own_coarse(1, core)
    flat = fold_lanes(block)
    own_pack[1, :, 0:half] = flat
    keep_coarse(1, core, block)
    upper, lower = flat[:ny // 2], flat[ny // 2:]
    upper_even = even(upper.shape, 0)
    own_far[0] = jnp.where(upper_even, roll(upper, -1, 0), lower)
    own_far[1] = jnp.where(upper_even, upper, roll(lower, 1, 0))
    for side in (0, 1):
        for a in ring_y:
            for kind in (0, 1):
                own_rows[side, a["index"], kind] = pack_rows(side, a, kind, slice(0, nz))

    pl.semaphore_wait(barrier, count)
    start(z_log)
    start(z_src)
    start(x_log[1])
    start(y_log)
    start(y_src)
    start(rows)
    start(packs_far)
    start(packs_edge)
    start(packs_near)
    start(x_src[1])

    def clear(ref, *at):
        ref[at] = jnp.zeros_like(ref[at])

    if ring_y and ring_z:
        for side in (0, 1):
            clear(packs, side, 1, 0, slice(ny, wide_y), slice(half, packs.shape[4]))
    for step in (1, 2):
        for _, _, get, side in slots_x(step):
            @pl.when(jnp.logical_not(get))
            def _():
                clear(packs, side, step - 1)
                clear(got_lanes, step - 1, side)
                if step == 2:
                    clear(got_far, side)
                if step == 1:
                    clear(got_rows, side)
                    clear(got_corner, side)
                    for i in range(1, DEGREE + 1):
                        layer = (-i, nx - 1 + i)[side]
                        clear(logs, REACH + layer)
                        clear(srcs, DEGREE + layer)
                    clear(dirs1, DEGREE + layer)
    for a in ring_y:
        if a["get"] is not True:
            @pl.when(jnp.logical_not(a["get"]))
            def _():
                at = slice(a["place"], a["place"] + ROWS)
                for layer in range(nx + 2 * REACH):
                    clear(logs, layer, at)
                for layer in range(nx + 2 * DEGREE):
                    clear(srcs, layer, at)
                for side in (0, 1):
                    for step in (1, 2):
                        clear(packs, side, step - 1, slice(None), at)
                    clear(got_rows, side, a["index"])
                    clear(got_corner, side, a["index"])

    arrive(z_log)
    arrive(z_src)
    if ring_z:
        for kind in (0, 1):
            block = own_coarse(kind, beside)
            own_pack[kind, :, half:] = block
            keep_coarse(kind, beside, block)
    for side in (0, 1):
        for b in ring_z:
            pack_lanes(side, b)
    start(lanes)
    start(corner)
    start(x_log[3])
    start(x_src[2])

    row = iota((wide_y, wide_z), 0)
    lane = iota((wide_y, wide_z), 1)

    def cuts(axis, ring_, length, total, tile):
        n, here = sizes[axis], me[axis]
        if n == 1:
            return [total - 1]
        if n == 2:
            return [jnp.where(here == 0, total - 1, length - 1)]
        return [length + tile - 1, jnp.where(here < n - 1, -1, length - 1),
                jnp.where(here > 0, -1, total - 1)]

    cuts_y = cuts("gy", ring_y, ny, wide_y, ROWS)
    cuts_z = cuts("gz", ring_z, nz, wide_z, LANES)

    def cut(t, index, at):
        for c in at:
            t = jnp.where(index == c, 0.0, t)
        return t

    row_pair, lane_pair = row | 1, lane | 1
    even_row = even((wide_y, wide_z), 0)

    all_rows = slice(0, wide_y)
    own_part = slice(0, ny)
    rim_part = slice(ny, wide_y)

    def fine_k(i, part_=all_rows):
        inv_k[REACH + i, part_] = jnp.exp(-logs[REACH + i, part_])

    def fine_z(i, part_=all_rows):
        mine = inv_k[REACH + i, part_]
        t_z[DEGREE + i, part_] = cut(2.0 * inverse(mine + roll(mine, -1, 1)), lane[part_], cuts_z)

    def fine_y(i):
        mine = inv_k[REACH + i]
        t_y[DEGREE + i] = cut(2.0 * inverse(mine + roll(mine, -1, 0)), row, cuts_y)

    flag = {(step, side): get.astype(jnp.float32)
            for step in (1, 2) for _, _, get, side in slots_x(step)}

    def fine_x(i, part_=all_rows):
        t = 2.0 * inverse(inv_k[REACH + i, part_] + inv_k[REACH + i + 1, part_])
        if i == -1:
            t = t * flag[1, 0]
        if i == nx - 1:
            t = t * flag[1, 1]
        t_x[REACH + i, part_] = t

    def fine_d(i):
        y, z = t_y[DEGREE + i], t_z[DEGREE + i]
        total = (y + roll(y, 1, 0)) + (z + roll(z, 1, 1)) + (t_x[REACH + i] + t_x[REACH + i - 1])
        inv_d[DEGREE + i] = inverse(total + STORAGE)

    def coarse_yz(i):
        mine = c_inv_k[i]
        c_t_y[i] = cut(4.0 * inverse(mine + roll(mine, -2, 0)), row_pair, cuts_y)
        c_t_z[i] = cut(4.0 * inverse(mine + roll(mine, -2, 1)), lane_pair, cuts_z)

    def swap(a):
        return jnp.where(even_row, roll(a, -1, 0), roll(a, 1, 0))

    def coarse_x(i):
        if i < 0:
            mine = c_inv_k[0]
            c_t_x[0] = 4.0 * inverse(mine + swap(mine))
            return
        t = 4.0 * inverse(c_inv_k[i] + c_inv_k[i + 1])
        if i in (0, 2):
            step = i // 2 + 1
            t = t * jnp.where(even_row, flag[step, 0], flag[step, 1])
        c_t_x[i + 1] = t

    def coarse_d(i):
        y, z = c_t_y[i], c_t_z[i]
        total = (y + roll(y, 2, 0)) + (z + roll(z, 2, 1)) + (c_t_x[i] + c_t_x[i + 1])
        c_inv_d[i] = inverse(total + 8.0 * STORAGE)

    low_in.wait()
    high_in.wait()
    low = jnp.full((1, wide_z), low_ref[0])
    high = jnp.full((1, wide_z), high_ref[0])
    theta = (high + low) * 0.5
    delta = (high - low) * 0.5
    sigma = theta / delta
    rho = 1.0 / sigma
    inv_theta = 1.0 / theta
    keep, gain = [None], [None]
    for _ in range(DEGREE):
        rho_next = 1.0 / (2.0 * sigma - rho)
        keep.append(rho_next * rho)
        gain.append(2.0 * rho_next / delta)
        rho = rho_next

    def fine_first(i, at=(slice(None), slice(None))):
        dirs1[(DEGREE + i,) + at] = (srcs[(DEGREE + i,) + at] * inv_d[(DEGREE + i,) + at]
                                     * inv_theta[:, at[1]])

    def coarse_first(i, at=(slice(None), slice(None))):
        c_dirs1[(i,) + at] = c_res[(i,) + at] * c_inv_d[(i,) + at] * inv_theta[:, at[1]]

    fields = [None, dirs1, dirs2, dirs3]
    c_fields = [None, c_dirs1, c_dirs2, c_dirs3]

    def fine_turn(turn, i, small=False):
        ref, base = fields[turn], DEGREE + 1 - turn
        at = core if small else (all_rows, slice(0, wide_z))
        d = ref[base + i]
        y = t_y[DEGREE + i] * (d - roll(d, -1, 0))
        z = t_z[DEGREE + i] * (d - roll(d, -1, 1))
        flow = ((y - roll(y, 1, 0)) + (z - roll(z, 1, 1)))[at]
        d = d[at]
        r = (srcs if turn == 1 else res)[(DEGREE + i,) + at] - STORAGE * d - flow
        r = r - t_x[(REACH + i,) + at] * (d - ref[(base + i + 1,) + at])
        r = r - t_x[(REACH + i - 1,) + at] * (d - ref[(base + i - 1,) + at])
        later = keep[turn][:, at[1]] * d + gain[turn][:, at[1]] * (r * inv_d[(DEGREE + i,) + at])
        if turn < DEGREE:
            res[(DEGREE + i,) + at] = r
            fields[turn + 1][(base - 1 + i,) + at] = later
        else:
            part[i] = dirs1[(DEGREE + i,) + at] + dirs2[(DEGREE - 1 + i,) + at] + d
            last[i] = later

    def coarse_turn(turn, i, small=False):
        ref = c_fields[turn]
        at = core if small else (all_rows, slice(0, wide_z))
        d = ref[i]
        y = c_t_y[i] * (d - roll(d, -2, 0))
        z = c_t_z[i] * (d - roll(d, -2, 1))
        flow = ((y - roll(y, 2, 0)) + (z - roll(z, 2, 1)))[at]
        inner_side = swap(d)[at] if i == 0 else ref[(i - 1,) + at]
        d = d[at]
        r = c_res[(i,) + at] - 8.0 * STORAGE * d - flow
        r = r - c_t_x[(i + 1,) + at] * (d - ref[(i + 1,) + at])
        r = r - c_t_x[(i,) + at] * (d - inner_side)
        later = keep[turn][:, at[1]] * d + gain[turn][:, at[1]] * (r * c_inv_d[(i,) + at])
        if turn < DEGREE:
            c_res[(i,) + at] = r
            c_fields[turn + 1][(i,) + at] = later
        else:
            total = c_dirs1[(i,) + at] + c_dirs2[(i,) + at] + d + later
            top = even((ny, nz), 0)
            coarse[0] = jnp.where(top, total, roll(total, 1, 0))
            coarse[1] = jnp.where(top, roll(total, -1, 0), total)

    def unpack_rows(side, kind):
        for a in ring_y:
            place_rows(side, a, kind, got_rows[side, a["index"], kind], slice(0, nz))

    def spread(step, kind, near):
        left, right = packs[0, step - 1, kind], packs[1, step - 1, kind]
        top = even(left.shape, 0)
        if near:
            a = jnp.where(top, roll(left, -1, 0), roll(right, 1, 0))
        else:
            a = jnp.where(top, left, right)
        return jnp.concatenate([spread_lanes(a[:, :half]), a[:, half:]], axis=1)

    def spread_lanes(main):
        even_lane = even(main.shape, 1)
        return jnp.concatenate([jnp.where(even_lane, main, roll(main, 1, 1)),
                                jnp.where(even_lane, roll(main, -1, 1), main)], axis=1)

    def spread_far():
        left, right = got_far[0], got_far[1]
        first = even(left.shape, 0)
        upper = jnp.where(first, left, roll(right, 1, 0))
        lower = jnp.where(first, roll(left, -1, 0), right)
        return spread_lanes(jnp.concatenate([upper, lower], axis=0))

    def halo(i):
        return (-i, nx - 1 + i)

    mine = range(nx)
    inner = range(1, nx - 1)
    ends = (0, nx - 1)

    for i in mine:
        fine_k(i, own_part)
    for i in mine:
        fine_z(i, own_part)
    for i in range(nx - 1):
        fine_x(i, own_part)
    arrive(y_log)
    if ring_y:
        for i in mine:
            fine_k(i, rim_part)
        for i in mine:
            fine_z(i, rim_part)
        for i in range(nx - 1):
            fine_x(i, rim_part)
        keep_coarse(0, rim, own_coarse(0, rim))
    for i in inner:
        fine_y(i)
        fine_d(i)
        fine_first(i, core)
    start(x_dir)
    for i in ends:
        fine_y(i)
    arrive(y_src)
    for i in inner:
        if ring_z:
            fine_first(i, beside)
        if ring_y:
            fine_first(i, rim)
    if ring_y:
        keep_coarse(1, rim, own_coarse(1, rim))
    coarse_yz(0)
    coarse_x(-1)

    arrive(x_log[1])
    arrive(rows)
    arrive(packs_far)
    start(pass_y)
    start(pass_z)
    arrive(lanes)
    arrive(corner)
    for side in (0, 1):
        unpack_rows(side, 0)
        unpack_rows(side, 1)
        for b in ring_z:
            unpack_lanes(side, b)
    for i in halo(1) + halo(2):
        fine_k(i)
    for i in halo(1):
        fine_y(i)
        fine_z(i)
    for i in (-2, -1, nx - 1, nx):
        fine_x(i)
    for i in ends + halo(1):
        fine_d(i)
    for i in ends:
        fine_first(i)
    for i in inner:
        fine_turn(1, i)
    arrive(x_src[1])
    for i in halo(1):
        fine_first(i)
    for i in ends:
        fine_turn(1, i)
    for i in inner:
        fine_turn(2, i)

    arrive(packs_near)
    arrive(packs_edge)
    c_inv_k[1] = jnp.exp(-spread(1, 0, True))
    c_inv_k[2] = jnp.exp(-spread(1, 0, False))
    c_res[1] = spread(1, 1, True)
    c_res[2] = spread(1, 1, False)
    coarse_yz(1)
    coarse_x(0)
    coarse_x(1)
    coarse_yz(2)
    for i in (0, 1):
        coarse_d(i)
        coarse_first(i)
    coarse_turn(1, 0)

    arrive(x_log[3])
    for i in halo(3):
        fine_k(i)
    for i in halo(2):
        fine_y(i)
        fine_z(i)
    for i in (-3, nx + 1):
        fine_x(i)
    for i in halo(2):
        fine_d(i)
    arrive(x_src[2])
    for i in halo(2):
        fine_first(i)
    for i in halo(1):
        fine_turn(1, i)
    for i in ends:
        fine_turn(2, i)
    for i in inner:
        fine_turn(3, i, True)

    arrive(pass_z)
    for side in (0, 1):
        for b in ring_z:
            unpack_far(side, b)
    arrive(pass_y)
    c_inv_k[3] = jnp.exp(-spread(2, 0, True))
    c_inv_k[4] = jnp.exp(-spread(2, 0, False))
    c_res[(3,) + core] = spread_far()
    coarse_yz(3)
    coarse_x(2)
    coarse_x(3)
    for i in (2, 3):
        coarse_d(i)
    coarse_first(2)
    coarse_first(3, core)
    coarse_turn(1, 1)
    coarse_turn(1, 2, True)
    coarse_turn(2, 0)
    coarse_turn(2, 1, True)
    coarse_turn(3, 0, True)

    arrive(x_dir)
    for i in halo(2):
        fine_turn(1, i, True)
    for i in halo(1):
        fine_turn(2, i, True)
    for i in ends:
        fine_turn(3, i, True)

    for group in ([z_log, z_src, y_log, y_src, rows, corner, x_dir, packs_near, packs_edge, packs_far, pass_y, pass_z, lanes]
                  + list(x_log.values()) + list(x_src.values())):
        drain(group)


def shards(sizes, log_perm, source, low_bound, high_bound):
    nx, ny, nz = log_perm.shape
    wide_y = ny + ROWS * sides(sizes["gy"])
    wide_z = nz + LANES * sides(sizes["gz"])
    half = nz // 2
    f32 = lambda *shape: pltpu.VMEM(shape, jnp.float32)
    fine = lambda reach: f32(nx + 2 * reach, wide_y, wide_z)
    pairs = lambda n: f32(n, wide_y, wide_z)
    log_perm = pltpu.with_memory_space_constraint(log_perm, pltpu.HBM)
    source = pltpu.with_memory_space_constraint(source, pltpu.HBM)
    hbm = pl.BlockSpec(memory_space=pltpu.HBM)
    vmem = pl.BlockSpec(memory_space=pltpu.VMEM)
    whole = jax.ShapeDtypeStruct((nx, ny, nz), jnp.float32)
    messages = 96
    part, last, coarse = pl.pallas_call(
        functools.partial(kernel, sizes),
        out_shape=(whole, whole, jax.ShapeDtypeStruct((nx // 2, ny, nz), jnp.float32)),
        in_specs=[hbm] * 4,
        out_specs=(vmem,) * 3,
        scratch_shapes=[
            pltpu.SMEM((1,), jnp.float32),
            pltpu.SMEM((1,), jnp.float32),
            fine(REACH), fine(DEGREE),
            f32(2, 2, 2, wide_y, half + wide_z - nz),
            f32(2, ny, half + wide_z - nz),
            f32(2, max(1, sides(sizes["gy"])), 2, ROWS, nz),
            f32(2, max(1, sides(sizes["gy"])), 2, ROWS, nz),
            f32(2, max(1, sides(sizes["gz"])), ny, LANES),
            f32(2, 2, max(1, sides(sizes["gz"])), ny, LANES),
            f32(2, ny // 2, half),
            f32(2, ny // 2, half),
            f32(2, max(1, sides(sizes["gy"])), max(1, sides(sizes["gz"])), ROWS, LANES),
            f32(2, max(1, sides(sizes["gy"])), max(1, sides(sizes["gz"])), ROWS, LANES),
            fine(REACH), fine(REACH), fine(DEGREE), fine(DEGREE), fine(DEGREE), fine(DEGREE),
            fine(DEGREE), fine(DEGREE - 1), fine(DEGREE - 2),
            pairs(5), pairs(5), pairs(4), pairs(4), pairs(4), pairs(4), pairs(4), pairs(3), pairs(2),
            pltpu.SemaphoreType.DMA((4,)),
            pltpu.SemaphoreType.DMA((messages,)),
            pltpu.SemaphoreType.DMA((messages,)),
        ],
        compiler_params=pltpu.CompilerParams(
            collective_id=0, has_side_effects=True, vmem_limit_bytes=24 * 2**20),
    )(low_bound, high_bound, log_perm, source)
    fine_pressure = part + last
    return fine_pressure, fine_pressure - jnp.repeat(coarse, 2, axis=0)


def solution(mesh):
    sizes = {axis: mesh.shape[axis] for axis in AXES}
    spec = P(("groups", "gx"), "gy", "gz")
    return jax.shard_map(
        functools.partial(shards, sizes),
        mesh=mesh,
        in_specs=(spec, spec, P(), P()),
        out_specs=(spec, spec),
        check_vma=False,
    )
```

```python
import functools

import jax
import jax.numpy as jnp
from jax import lax
from jax.experimental import pallas as pl
from jax.experimental.pallas import tpu as pltpu
from jax.sharding import PartitionSpec as P

DEGREE = 3
REACH = DEGREE
STORAGE = 0.1
LANES = 128
ROWS = 8
MESH = pl.DeviceIdType.MESH
AXES = ("gx", "gy", "gz")


def roll(a, shift, axis):
    return pltpu.roll(a, shift % a.shape[axis], axis)


def iota(shape, axis):
    return lax.broadcasted_iota(jnp.int32, shape, axis)


def even(shape, axis):
    return iota(shape, axis) % 2 == 0


def pair_sum(a, axis):
    return a + jnp.where(even(a.shape, axis), roll(a, -1, axis), roll(a, 1, axis))


def pooled(a, b):
    return pair_sum(pair_sum(a + b, 0), 1)


def inverse(a):
    r = pl.reciprocal(a, approx=True)
    return r * (2.0 - a * r)


def pick(condition, a, b):
    if isinstance(condition, bool):
        return a if condition else b
    return jnp.where(condition, a, b)


def both(a, b):
    if a is True:
        return b
    return a if b is True else jnp.logical_and(a, b)


def when(condition, act):
    if condition is True:
        act()
    else:
        pl.when(condition)(act)


def sides(size):
    return min(size - 1, 2)


def kernel(sizes, low_hbm, high_hbm, log_hbm, src_hbm, part, last, coarse,
           low_ref, high_ref, logs, srcs, packs, own_pack, own_rows, got_rows, own_lanes, got_lanes,
           own_far, got_far, own_corner, got_corner,
           inv_k, t_x, t_y, t_z, inv_d, res, dirs1, dirs2, dirs3,
           c_inv_k, c_t_x, c_t_y, c_t_z, c_inv_d, c_res, c_dirs1, c_dirs2, c_dirs3,
           io_sem, send_sem, recv_sem):
    nx, ny, nz = log_hbm.shape
    half = nz // 2
    wide_y, wide_z = logs.shape[1:]
    me = {axis: lax.axis_index(axis) for axis in AXES}
    count_x = sizes["gx"]
    x = me["gx"]

    def slots_x(step):
        return [({"gx": x + step}, x + step < count_x, x >= step, 0),
                ({"gx": x - step}, x >= step, x + step < count_x, 1)]

    def ring(axis, length, tile):
        n, here = sizes[axis], me[axis]
        if n == 1:
            return []
        if n == 2:
            start = pl.multiple_of((1 - here) * (length - tile), tile)
            return [dict(to={axis: 1 - here}, send=True, get=True, start=start, place=length,
                         send_high=here == 0, get_high=here == 1, index=0)]
        return [dict(to={axis: here - 1}, send=here > 0, get=here < n - 1, start=0, place=length,
                     send_high=False, get_high=False, index=0),
                dict(to={axis: here + 1}, send=here < n - 1, get=here > 0, start=length - tile,
                     place=length + tile, send_high=True, get_high=True, index=1)]

    ring_y = ring("gy", ny, ROWS)
    ring_z = ring("gz", nz, LANES)

    def packed_start(b):
        if isinstance(b["start"], int):
            return b["start"] * (half - LANES) // (nz - LANES)
        return pl.multiple_of((1 - me["gz"]) * (half - LANES), LANES)

    used = []

    class Message:
        def __init__(self, to, send, get, source, target):
            index = len(used)
            used.append(index)
            self.send, self.get = send, get
            self.copy = lambda: pltpu.make_async_remote_copy(
                src_ref=source, dst_ref=target, send_sem=send_sem.at[index],
                recv_sem=recv_sem.at[index], device_id=to, device_id_type=MESH)

    def start(messages):
        for m in messages:
            when(m.send, lambda: m.copy().start())

    def arrive(messages):
        for m in messages:
            when(m.get, lambda: m.copy().wait_recv())

    def drain(messages):
        for m in messages:
            when(m.send, lambda: m.copy().wait_send())

    partners = [(to, send) for step in (1, 2) for to, send, _, _ in slots_x(step)]
    partners += [(r["to"], r["send"]) for r in ring_y + ring_z]
    partners += [({**a["to"], **b["to"]}, both(a["send"], b["send"])) for a in ring_y for b in ring_z]
    partners += [({**to, **a["to"]}, both(send, a["send"]))
                 for to, send, _, _ in slots_x(1) for a in ring_y]
    barrier = pltpu.get_barrier_semaphore()
    count = 0
    for to, send in partners:
        when(send, lambda: pl.semaphore_signal(barrier, inc=1, device_id=to, device_id_type=MESH))
        count = count + (1 if send is True else send.astype(jnp.int32))

    own = pl.ds(REACH, nx)
    own_s = pl.ds(DEGREE, nx)
    log_in = pltpu.make_async_copy(log_hbm, logs.at[own, 0:ny, 0:nz], io_sem.at[0])
    src_in = pltpu.make_async_copy(src_hbm, srcs.at[own_s, 0:ny, 0:nz], io_sem.at[1])
    low_in = pltpu.make_async_copy(low_hbm, low_ref, io_sem.at[2])
    high_in = pltpu.make_async_copy(high_hbm, high_ref, io_sem.at[3])
    for copy in (log_in, src_in, low_in, high_in):
        copy.start()

    def plane_z(hbm, ref, layers):
        return [Message(b["to"], b["send"], b["get"],
                        hbm.at[:, :, pl.ds(b["start"], LANES)],
                        ref.at[layers, 0:ny, pl.ds(b["place"], LANES)]) for b in ring_z]

    def plane_y(hbm, ref, base, first, count_):
        return [Message(a["to"], a["send"], a["get"],
                        hbm.at[pl.ds(first, count_), pl.ds(a["start"], ROWS), :],
                        ref.at[pl.ds(base + first, count_), pl.ds(a["place"], ROWS), 0:nz])
                for a in ring_y]

    def plane_yz(hbm, ref, layers):
        return [Message({**a["to"], **b["to"]}, both(a["send"], b["send"]), both(a["get"], b["get"]),
                        hbm.at[:, pl.ds(a["start"], ROWS), pl.ds(b["start"], LANES)],
                        ref.at[layers, pl.ds(a["place"], ROWS), pl.ds(b["place"], LANES)])
                for a in ring_y for b in ring_z]

    def span(side, first, last_, base):
        if side == 0:
            return pl.ds(nx - last_, last_ - first + 1), pl.ds(base - last_, last_ - first + 1)
        return pl.ds(first - 1, last_ - first + 1), pl.ds(base + nx + first - 1, last_ - first + 1)

    def along(hbm, ref, base, first, last_):
        out = []
        for to, send, get, side in slots_x(1):
            mine, theirs = span(side, first, last_, base)
            out.append(Message(to, send, get, hbm.at[mine], ref.at[theirs, 0:ny, 0:nz]))
        return out

    z_log = plane_z(log_hbm, logs, own)
    z_src = plane_z(src_hbm, srcs, own_s)
    y_first = plane_y(log_hbm, logs, REACH, 1, nx - 2)
    y_log = (plane_y(log_hbm, logs, REACH, 0, 1) + plane_y(log_hbm, logs, REACH, nx - 1, 1)
             + plane_yz(log_hbm, logs, own))
    y_src = plane_y(src_hbm, srcs, DEGREE, 0, nx) + plane_yz(src_hbm, srcs, own_s)
    x_log = {1: along(log_hbm, logs, REACH, 1, 2), 3: along(log_hbm, logs, REACH, 3, 3)}
    x_src = {i: along(src_hbm, srcs, DEGREE, i, i) for i in (1, 2)}
    x_dir = [Message(to, send, get, dirs1.at[DEGREE + (nx - DEGREE, DEGREE - 1)[side], 0:ny, 0:nz],
                     dirs1.at[DEGREE + (-DEGREE, nx - 1 + DEGREE)[side], 0:ny, 0:nz])
             for to, send, get, side in slots_x(1)]
    rows = [Message({**to, **a["to"]}, both(send, a["send"]), both(get, a["get"]),
                    own_rows.at[side, a["index"]], got_rows.at[side, a["index"]])
            for to, send, get, side in slots_x(1) for a in ring_y]
    lanes = [Message(to, both(send, b["get"]), both(get, b["get"]),
                     own_lanes.at[side, b["index"]], got_lanes.at[0, side, b["index"]])
             for to, send, get, side in slots_x(1) for b in ring_z]
    corner = [Message({**to, **a["to"]}, both(send, both(a["send"], b["get"])), both(get, both(a["get"], b["get"])),
                      own_corner.at[side, a["index"], b["index"]], got_corner.at[side, a["index"], b["index"]])
              for to, send, get, side in slots_x(1) for a in ring_y for b in ring_z]
    packs_near = [Message(to, send, get, own_pack.at[:, :, 0:half],
                          packs.at[side, 0, :, 0:ny, 0:half]) for to, send, get, side in slots_x(1)]
    packs_edge = [Message({**to, **a["to"]}, both(send, a["send"]), both(get, a["get"]),
                          own_pack.at[:, pl.ds(a["start"], ROWS), 0:half],
                          packs.at[side, 0, :, pl.ds(a["place"], ROWS), 0:half])
                  for to, send, get, side in slots_x(1) for a in ring_y]
    packs_far = [Message(to, send, get, own_pack.at[0, :, 0:half],
                         packs.at[side, 1, 0, 0:ny, 0:half]) for to, send, get, side in slots_x(2)]
    packs_far += [Message(to, send, get, own_far.at[side], got_far.at[side])
                  for to, send, get, side in slots_x(2)]
    far = [get for _, _, get, _ in slots_x(2)]
    pass_y = [Message(a["to"], both(a["send"], far[side]), both(a["get"], far[side]),
                      packs.at[side, 1, 0, pl.ds(a["start"], ROWS), 0:half],
                      packs.at[side, 1, 0, pl.ds(a["place"], ROWS), 0:half])
              for side in (0, 1) for a in ring_y]
    pass_z = [Message(b["to"], both(b["send"], far[side]), both(b["get"], far[side]),
                      packs.at[side, 1, 0, 0:ny, pl.ds(packed_start(b), LANES)],
                      got_lanes.at[1, side, b["index"]])
              for side in (0, 1) for b in ring_z]

    def pair_block(ref, base, at):
        a = pooled(ref[(base,) + at], ref[(base + 1,) + at])
        b = pooled(ref[(base + 2,) + at], ref[(base + 3,) + at])
        return jnp.where(even(a.shape, 0), a, b)

    tile_lane = iota((ny, LANES), 1)

    def pack_rows(side, a, kind, at):
        ref, base = ((logs, REACH), (srcs, DEGREE))[kind]

        def edge(i):
            layer = (nx - i, i - 1)[side]
            return ref[base + layer, pl.ds(a["start"], ROWS), at]
        high = a["send_high"]
        one, two = edge(1), edge(2)
        spot = iota(one.shape, 0)
        if kind == 0:
            three = edge(3)
            two = pick(high, roll(two, 5, 0), roll(two, 3, 0))
            three = pick(high, roll(three, 3, 0), roll(three, 5, 0))
            first = pick(high, spot - 5, 2 - spot) >= 0
            second = (spot == 3) | (spot == 4)
            return jnp.where(first, one, jnp.where(second, two, three))
        two = pick(high, roll(two, 6, 0), roll(two, 2, 0))
        first = pick(high, spot - 6, 1 - spot) >= 0
        return jnp.where(first, one, two)

    STRIP = 8

    def side_by_side(tiles, high):
        out = None
        for k, a in enumerate(tiles):
            a = pick(high, roll(a, STRIP * (k + 1), 1), roll(a, STRIP * k, 1))
            out = a if out is None else jnp.where(tile_lane[:a.shape[0]] >= STRIP * k, a, out)
        return out

    def strip(a, k, high):
        return pick(high, roll(a, -STRIP * (k + 1), 1), roll(a, -STRIP * k, 1))

    def tile_of(b):
        return (slice(b["place"], b["place"] + LANES),
                slice(half + b["place"] - nz, half + b["place"] - nz + LANES))

    def pack_lanes(side, b):
        at, at_pack = tile_of(b)
        tiles = [logs[REACH + (nx - i, i - 1)[side], 0:ny, at] for i in (1, 2, 3)]
        tiles += [srcs[DEGREE + (nx - i, i - 1)[side], 0:ny, at] for i in (1, 2)]
        tiles += [own_pack[kind, :, at_pack] for kind in (0, 1)]
        own_lanes[side, b["index"]] = side_by_side(tiles, b["get_high"])
        for a in ring_y:
            tiles = [pack_rows(side, a, kind, at) for kind in (0, 1)]
            tiles += [own_pack[kind, pl.ds(a["start"], ROWS), at_pack] for kind in (0, 1)]
            own_corner[side, a["index"], b["index"]] = side_by_side(tiles, b["get_high"])

    def unpack_far(side, b):
        tile = got_lanes[1, side, b["index"]]
        even_lane = even(tile.shape, 1)
        packs[side, 1, 0, 0:ny, tile_of(b)[1]] = pick(
            b["get_high"], jnp.where(even_lane, roll(tile, -1, 1), tile),
            jnp.where(even_lane, tile, roll(tile, 1, 1)))

    def unpack_lanes(side, b):
        got = got_lanes[0, side, b["index"]]
        at, at_pack = tile_of(b)
        high = b["get_high"]
        packs[side, 0, 0, 0:ny, at_pack] = strip(got, 5, high)
        packs[side, 0, 1, 0:ny, at_pack] = strip(got, 6, high)
        for i in (1, 2, 3):
            logs[REACH + (-i, nx - 1 + i)[side], 0:ny, at] = strip(got, i - 1, high)
        for i in (1, 2):
            srcs[DEGREE + (-i, nx - 1 + i)[side], 0:ny, at] = strip(got, i + 2, high)
        for a in ring_y:
            got = got_corner[side, a["index"], b["index"]]
            rows_at = slice(a["place"], a["place"] + ROWS)
            for kind in (0, 1):
                place_rows(side, a, kind, strip(got, kind, high), at)
                packs[side, 0, kind, rows_at, at_pack] = strip(got, kind + 2, high)

    def place_rows(side, a, kind, got, at):
        ref, base = ((logs, REACH), (srcs, DEGREE))[kind]
        rows_at = slice(a["place"], a["place"] + ROWS)
        shifts = ((3, 5), (5, 3)) if kind == 0 else ((2, 6),)
        ref[base + (-1, nx)[side], rows_at, at] = got
        for i, (if_high, if_low) in enumerate(shifts):
            layer = (-2 - i, nx + 1 + i)[side]
            ref[base + layer, rows_at, at] = pick(a["get_high"], roll(got, if_high, 0), roll(got, if_low, 0))

    core = (slice(0, ny), slice(0, nz))
    beside = (slice(0, ny), slice(nz, wide_z))
    rim = (slice(ny, wide_y), slice(0, wide_z))
    scales = (0.125, 1.0)
    whole = (logs, srcs)
    bases = (REACH, DEGREE)

    def own_coarse(kind, at):
        return pair_block(whole[kind], bases[kind], at) * scales[kind]

    def keep_coarse(kind, at, block):
        if kind == 0:
            c_inv_k[(0,) + at] = jnp.exp(-block)
        else:
            c_res[(0,) + at] = block

    def fold_lanes(a):
        return jnp.where(even((a.shape[0], half), 1), a[:, :half], a[:, half:nz])

    log_in.wait()
    block = own_coarse(0, core)
    own_pack[0, :, 0:half] = fold_lanes(block)
    keep_coarse(0, core, block)
    src_in.wait()
    block = own_coarse(1, core)
    flat = fold_lanes(block)
    own_pack[1, :, 0:half] = flat
    keep_coarse(1, core, block)
    upper, lower = flat[:ny // 2], flat[ny // 2:]
    upper_even = even(upper.shape, 0)
    own_far[0] = jnp.where(upper_even, roll(upper, -1, 0), lower)
    own_far[1] = jnp.where(upper_even, upper, roll(lower, 1, 0))
    for side in (0, 1):
        for a in ring_y:
            for kind in (0, 1):
                own_rows[side, a["index"], kind] = pack_rows(side, a, kind, slice(0, nz))

    pl.semaphore_wait(barrier, count)
    start(z_log)
    start(z_src)
    start(y_first)
    start(packs_far)
    start(x_log[1])
    start(rows)
    start(y_log)
    start(y_src)

    arrive(z_log)
    arrive(z_src)
    if ring_z:
        for kind in (0, 1):
            block = own_coarse(kind, beside)
            own_pack[kind, :, half:] = block
            keep_coarse(kind, beside, block)
    for side in (0, 1):
        for b in ring_z:
            pack_lanes(side, b)
    start(lanes)
    start(corner)
    start(x_src[1])
    start(packs_edge)
    start(packs_near)
    start(x_log[3])
    start(x_src[2])

    def clear(ref, *at):
        ref[at] = jnp.zeros_like(ref[at])

    if ring_y and ring_z:
        for side in (0, 1):
            clear(packs, side, 1, 0, slice(ny, wide_y), slice(half, packs.shape[4]))
    for step in (1, 2):
        for _, _, get, side in slots_x(step):
            @pl.when(jnp.logical_not(get))
            def _():
                clear(packs, side, step - 1)
                clear(got_lanes, step - 1, side)
                if step == 2:
                    clear(got_far, side)
                if step == 1:
                    clear(got_rows, side)
                    clear(got_corner, side)
                    for i in range(1, DEGREE + 1):
                        layer = (-i, nx - 1 + i)[side]
                        clear(logs, REACH + layer)
                        clear(srcs, DEGREE + layer)
                    clear(dirs1, DEGREE + layer)
    for a in ring_y:
        if a["get"] is not True:
            @pl.when(jnp.logical_not(a["get"]))
            def _():
                at = slice(a["place"], a["place"] + ROWS)
                for layer in range(nx + 2 * REACH):
                    clear(logs, layer, at)
                for layer in range(nx + 2 * DEGREE):
                    clear(srcs, layer, at)
                for side in (0, 1):
                    for step in (1, 2):
                        clear(packs, side, step - 1, slice(None), at)
                    clear(got_rows, side, a["index"])
                    clear(got_corner, side, a["index"])

    row = iota((wide_y, wide_z), 0)
    lane = iota((wide_y, wide_z), 1)

    def cuts(axis, ring_, length, total, tile):
        n, here = sizes[axis], me[axis]
        if n == 1:
            return [total - 1]
        if n == 2:
            return [jnp.where(here == 0, total - 1, length - 1)]
        return [length + tile - 1, jnp.where(here < n - 1, -1, length - 1),
                jnp.where(here > 0, -1, total - 1)]

    cuts_y = cuts("gy", ring_y, ny, wide_y, ROWS)
    cuts_z = cuts("gz", ring_z, nz, wide_z, LANES)

    def cut(t, index, at):
        for c in at:
            t = jnp.where(index == c, 0.0, t)
        return t

    row_pair, lane_pair = row | 1, lane | 1
    even_row = even((wide_y, wide_z), 0)

    all_rows = slice(0, wide_y)
    own_part = slice(0, ny)
    rim_part = slice(ny, wide_y)

    def fine_k(i, part_=all_rows):
        inv_k[REACH + i, part_] = jnp.exp(-logs[REACH + i, part_])

    def fine_z(i, part_=all_rows):
        mine = inv_k[REACH + i, part_]
        t_z[DEGREE + i, part_] = cut(2.0 * inverse(mine + roll(mine, -1, 1)), lane[part_], cuts_z)

    def fine_y(i, at=slice(None)):
        mine = inv_k[REACH + i, :, at]
        t_y[DEGREE + i, :, at] = cut(2.0 * inverse(mine + roll(mine, -1, 0)), row[:, at], cuts_y)

    def fine_d_core(i):
        y, z = t_y[DEGREE + i, :, 0:nz], t_z[DEGREE + i, own_part]
        x = t_x[(REACH + i,) + core] + t_x[(REACH + i - 1,) + core]
        total = (y + roll(y, 1, 0))[:ny] + (z + roll(z, 1, 1))[:, :nz] + x
        inv_d[(DEGREE + i,) + core] = inverse(total + STORAGE)

    flag = {(step, side): get.astype(jnp.float32)
            for step in (1, 2) for _, _, get, side in slots_x(step)}

    def fine_x(i, part_=all_rows):
        t = 2.0 * inverse(inv_k[REACH + i, part_] + inv_k[REACH + i + 1, part_])
        if i == -1:
            t = t * flag[1, 0]
        if i == nx - 1:
            t = t * flag[1, 1]
        t_x[REACH + i, part_] = t

    def fine_d(i):
        y, z = t_y[DEGREE + i], t_z[DEGREE + i]
        total = (y + roll(y, 1, 0)) + (z + roll(z, 1, 1)) + (t_x[REACH + i] + t_x[REACH + i - 1])
        inv_d[DEGREE + i] = inverse(total + STORAGE)

    def coarse_yz(i):
        mine = c_inv_k[i]
        c_t_y[i] = cut(4.0 * inverse(mine + roll(mine, -2, 0)), row_pair, cuts_y)
        c_t_z[i] = cut(4.0 * inverse(mine + roll(mine, -2, 1)), lane_pair, cuts_z)

    def swap(a):
        return jnp.where(even_row, roll(a, -1, 0), roll(a, 1, 0))

    def coarse_x(i):
        if i < 0:
            mine = c_inv_k[0]
            c_t_x[0] = 4.0 * inverse(mine + swap(mine))
            return
        t = 4.0 * inverse(c_inv_k[i] + c_inv_k[i + 1])
        if i in (0, 2):
            step = i // 2 + 1
            t = t * jnp.where(even_row, flag[step, 0], flag[step, 1])
        c_t_x[i + 1] = t

    def coarse_d(i):
        y, z = c_t_y[i], c_t_z[i]
        total = (y + roll(y, 2, 0)) + (z + roll(z, 2, 1)) + (c_t_x[i] + c_t_x[i + 1])
        c_inv_d[i] = inverse(total + 8.0 * STORAGE)

    low_in.wait()
    high_in.wait()
    low = jnp.full((1, wide_z), low_ref[0])
    high = jnp.full((1, wide_z), high_ref[0])
    theta = (high + low) * 0.5
    delta = (high - low) * 0.5
    sigma = theta / delta
    rho = 1.0 / sigma
    inv_theta = 1.0 / theta
    keep, gain = [None], [None]
    for _ in range(DEGREE):
        rho_next = 1.0 / (2.0 * sigma - rho)
        keep.append(rho_next * rho)
        gain.append(2.0 * rho_next / delta)
        rho = rho_next

    def fine_first(i, at=(slice(None), slice(None))):
        dirs1[(DEGREE + i,) + at] = (srcs[(DEGREE + i,) + at] * inv_d[(DEGREE + i,) + at]
                                     * inv_theta[:, at[1]])

    def coarse_first(i, at=(slice(None), slice(None))):
        c_dirs1[(i,) + at] = c_res[(i,) + at] * c_inv_d[(i,) + at] * inv_theta[:, at[1]]

    fields = [None, dirs1, dirs2, dirs3]
    c_fields = [None, c_dirs1, c_dirs2, c_dirs3]

    def fine_turn(turn, i, small=False):
        ref, base = fields[turn], DEGREE + 1 - turn
        at = core if small else (all_rows, slice(0, wide_z))
        d = ref[base + i]
        y = t_y[DEGREE + i] * (d - roll(d, -1, 0))
        z = t_z[DEGREE + i] * (d - roll(d, -1, 1))
        flow = ((y - roll(y, 1, 0)) + (z - roll(z, 1, 1)))[at]
        d = d[at]
        r = (srcs if turn == 1 else res)[(DEGREE + i,) + at] - STORAGE * d - flow
        r = r - t_x[(REACH + i,) + at] * (d - ref[(base + i + 1,) + at])
        r = r - t_x[(REACH + i - 1,) + at] * (d - ref[(base + i - 1,) + at])
        later = keep[turn][:, at[1]] * d + gain[turn][:, at[1]] * (r * inv_d[(DEGREE + i,) + at])
        if turn < DEGREE:
            res[(DEGREE + i,) + at] = r
            fields[turn + 1][(base - 1 + i,) + at] = later
        else:
            part[i] = dirs1[(DEGREE + i,) + at] + dirs2[(DEGREE - 1 + i,) + at] + d
            last[i] = later

    def coarse_turn(turn, i, small=False):
        ref = c_fields[turn]
        at = core if small else (all_rows, slice(0, wide_z))
        d = ref[i]
        y = c_t_y[i] * (d - roll(d, -2, 0))
        z = c_t_z[i] * (d - roll(d, -2, 1))
        flow = ((y - roll(y, 2, 0)) + (z - roll(z, 2, 1)))[at]
        inner_side = swap(d)[at] if i == 0 else ref[(i - 1,) + at]
        d = d[at]
        r = c_res[(i,) + at] - 8.0 * STORAGE * d - flow
        r = r - c_t_x[(i + 1,) + at] * (d - ref[(i + 1,) + at])
        r = r - c_t_x[(i,) + at] * (d - inner_side)
        later = keep[turn][:, at[1]] * d + gain[turn][:, at[1]] * (r * c_inv_d[(i,) + at])
        if turn < DEGREE:
            c_res[(i,) + at] = r
            c_fields[turn + 1][(i,) + at] = later
        else:
            total = c_dirs1[(i,) + at] + c_dirs2[(i,) + at] + d + later
            top = even((ny, nz), 0)
            coarse[0] = jnp.where(top, total, roll(total, 1, 0))
            coarse[1] = jnp.where(top, roll(total, -1, 0), total)

    def unpack_rows(side, kind):
        for a in ring_y:
            place_rows(side, a, kind, got_rows[side, a["index"], kind], slice(0, nz))

    def spread(step, kind, near):
        left, right = packs[0, step - 1, kind], packs[1, step - 1, kind]
        top = even(left.shape, 0)
        if near:
            a = jnp.where(top, roll(left, -1, 0), roll(right, 1, 0))
        else:
            a = jnp.where(top, left, right)
        return jnp.concatenate([spread_lanes(a[:, :half]), a[:, half:]], axis=1)

    def spread_lanes(main):
        even_lane = even(main.shape, 1)
        return jnp.concatenate([jnp.where(even_lane, main, roll(main, 1, 1)),
                                jnp.where(even_lane, roll(main, -1, 1), main)], axis=1)

    def spread_far():
        left, right = got_far[0], got_far[1]
        first = even(left.shape, 0)
        upper = jnp.where(first, left, roll(right, 1, 0))
        lower = jnp.where(first, roll(left, -1, 0), right)
        return spread_lanes(jnp.concatenate([upper, lower], axis=0))

    def halo(i):
        return (-i, nx - 1 + i)

    mine = range(nx)
    inner = range(1, nx - 1)
    ends = (0, nx - 1)

    for i in mine:
        fine_k(i, own_part)
    for i in mine:
        fine_z(i, own_part)
    for i in range(nx - 1):
        fine_x(i, own_part)
    arrive(y_first)
    for i in inner:
        if ring_y:
            inv_k[REACH + i, rim_part, 0:nz] = jnp.exp(-logs[REACH + i, rim_part, 0:nz])
        fine_y(i, slice(0, nz))
        fine_d_core(i)
        fine_first(i, core)
    start(x_dir)
    arrive(packs_far)
    start(pass_y)
    start(pass_z)
    arrive(y_log)
    if ring_y:
        for i in mine:
            fine_k(i, rim_part)
        for i in mine:
            fine_z(i, rim_part)
        for i in range(nx - 1):
            fine_x(i, rim_part)
        keep_coarse(0, rim, own_coarse(0, rim))
    for i in mine:
        fine_y(i)
    for i in inner:
        fine_d(i)
    arrive(y_src)
    for i in inner:
        if ring_z:
            fine_first(i, beside)
        if ring_y:
            fine_first(i, rim)
    if ring_y:
        keep_coarse(1, rim, own_coarse(1, rim))
    coarse_yz(0)
    coarse_x(-1)

    arrive(x_log[1])
    arrive(rows)
    arrive(lanes)
    arrive(corner)
    for side in (0, 1):
        unpack_rows(side, 0)
        unpack_rows(side, 1)
        for b in ring_z:
            unpack_lanes(side, b)
    for i in halo(1) + halo(2):
        fine_k(i)
    for i in halo(1):
        fine_y(i)
        fine_z(i)
    for i in (-2, -1, nx - 1, nx):
        fine_x(i)
    for i in ends + halo(1):
        fine_d(i)
    for i in ends:
        fine_first(i)
    for i in inner:
        fine_turn(1, i)
    arrive(x_src[1])
    for i in halo(1):
        fine_first(i)
    for i in ends:
        fine_turn(1, i)
    for i in inner:
        fine_turn(2, i)

    arrive(packs_near)
    arrive(packs_edge)
    c_inv_k[1] = jnp.exp(-spread(1, 0, True))
    c_inv_k[2] = jnp.exp(-spread(1, 0, False))
    c_res[1] = spread(1, 1, True)
    c_res[2] = spread(1, 1, False)
    coarse_yz(1)
    coarse_x(0)
    coarse_x(1)
    coarse_yz(2)
    for i in (0, 1):
        coarse_d(i)
        coarse_first(i)
    coarse_turn(1, 0)

    arrive(x_log[3])
    for i in halo(3):
        fine_k(i)
    for i in halo(2):
        fine_y(i)
        fine_z(i)
    for i in (-3, nx + 1):
        fine_x(i)
    for i in halo(2):
        fine_d(i)
    arrive(x_src[2])
    for i in halo(2):
        fine_first(i)
    for i in halo(1):
        fine_turn(1, i)
    for i in ends:
        fine_turn(2, i)
    for i in inner:
        fine_turn(3, i, True)

    arrive(pass_z)
    for side in (0, 1):
        for b in ring_z:
            unpack_far(side, b)
    arrive(pass_y)
    c_inv_k[3] = jnp.exp(-spread(2, 0, True))
    c_inv_k[4] = jnp.exp(-spread(2, 0, False))
    c_res[(3,) + core] = spread_far()
    coarse_yz(3)
    coarse_x(2)
    coarse_x(3)
    for i in (2, 3):
        coarse_d(i)
    coarse_first(2)
    coarse_first(3, core)
    coarse_turn(1, 1)
    coarse_turn(1, 2, True)
    coarse_turn(2, 0)
    coarse_turn(2, 1, True)
    coarse_turn(3, 0, True)

    arrive(x_dir)
    for i in halo(2):
        fine_turn(1, i, True)
    for i in halo(1):
        fine_turn(2, i, True)
    for i in ends:
        fine_turn(3, i, True)

    for group in ([z_log, z_src, y_first, y_log, y_src, rows, corner, x_dir, packs_near, packs_edge, packs_far, pass_y, pass_z, lanes]
                  + list(x_log.values()) + list(x_src.values())):
        drain(group)


def shards(sizes, log_perm, source, low_bound, high_bound):
    nx, ny, nz = log_perm.shape
    wide_y = ny + ROWS * sides(sizes["gy"])
    wide_z = nz + LANES * sides(sizes["gz"])
    half = nz // 2
    f32 = lambda *shape: pltpu.VMEM(shape, jnp.float32)
    fine = lambda reach: f32(nx + 2 * reach, wide_y, wide_z)
    pairs = lambda n: f32(n, wide_y, wide_z)
    log_perm = pltpu.with_memory_space_constraint(log_perm, pltpu.HBM)
    source = pltpu.with_memory_space_constraint(source, pltpu.HBM)
    hbm = pl.BlockSpec(memory_space=pltpu.HBM)
    vmem = pl.BlockSpec(memory_space=pltpu.VMEM)
    whole = jax.ShapeDtypeStruct((nx, ny, nz), jnp.float32)
    messages = 96
    part, last, coarse = pl.pallas_call(
        functools.partial(kernel, sizes),
        out_shape=(whole, whole, jax.ShapeDtypeStruct((nx // 2, ny, nz), jnp.float32)),
        in_specs=[hbm] * 4,
        out_specs=(vmem,) * 3,
        scratch_shapes=[
            pltpu.SMEM((1,), jnp.float32),
            pltpu.SMEM((1,), jnp.float32),
            fine(REACH), fine(DEGREE),
            f32(2, 2, 2, wide_y, half + wide_z - nz),
            f32(2, ny, half + wide_z - nz),
            f32(2, max(1, sides(sizes["gy"])), 2, ROWS, nz),
            f32(2, max(1, sides(sizes["gy"])), 2, ROWS, nz),
            f32(2, max(1, sides(sizes["gz"])), ny, LANES),
            f32(2, 2, max(1, sides(sizes["gz"])), ny, LANES),
            f32(2, ny // 2, half),
            f32(2, ny // 2, half),
            f32(2, max(1, sides(sizes["gy"])), max(1, sides(sizes["gz"])), ROWS, LANES),
            f32(2, max(1, sides(sizes["gy"])), max(1, sides(sizes["gz"])), ROWS, LANES),
            fine(REACH), fine(REACH), fine(DEGREE), fine(DEGREE), fine(DEGREE), fine(DEGREE),
            fine(DEGREE), fine(DEGREE - 1), fine(DEGREE - 2),
            pairs(5), pairs(5), pairs(4), pairs(4), pairs(4), pairs(4), pairs(4), pairs(3), pairs(2),
            pltpu.SemaphoreType.DMA((4,)),
            pltpu.SemaphoreType.DMA((messages,)),
            pltpu.SemaphoreType.DMA((messages,)),
        ],
        compiler_params=pltpu.CompilerParams(
            collective_id=0, has_side_effects=True, vmem_limit_bytes=24 * 2**20),
    )(low_bound, high_bound, log_perm, source)
    fine_pressure = part + last
    return fine_pressure, fine_pressure - jnp.repeat(coarse, 2, axis=0)


def solution(mesh):
    sizes = {axis: mesh.shape[axis] for axis in AXES}
    spec = P(("groups", "gx"), "gy", "gz")
    return jax.shard_map(
        functools.partial(shards, sizes),
        mesh=mesh,
        in_specs=(spec, spec, P(), P()),
        out_specs=(spec, spec),
        check_vma=False,
    )
```

```python
import functools

import jax
import jax.numpy as jnp
from jax import lax
from jax.experimental import pallas as pl
from jax.experimental.pallas import tpu as pltpu
from jax.sharding import PartitionSpec as P

DEGREE = 3
REACH = DEGREE
STORAGE = 0.1
LANES = 128
ROWS = 8
MESH = pl.DeviceIdType.MESH
AXES = ("gx", "gy", "gz")


def roll(a, shift, axis):
    return pltpu.roll(a, shift % a.shape[axis], axis)


def iota(shape, axis):
    return lax.broadcasted_iota(jnp.int32, shape, axis)


def even(shape, axis):
    return iota(shape, axis) % 2 == 0


def pair_sum(a, axis):
    return a + jnp.where(even(a.shape, axis), roll(a, -1, axis), roll(a, 1, axis))


def pooled(a, b):
    return pair_sum(pair_sum(a + b, 0), 1)


def inverse(a):
    r = pl.reciprocal(a, approx=True)
    return r * (2.0 - a * r)


def pick(condition, a, b):
    if isinstance(condition, bool):
        return a if condition else b
    return jnp.where(condition, a, b)


def both(a, b):
    if a is True:
        return b
    return a if b is True else jnp.logical_and(a, b)


def when(condition, act):
    if condition is True:
        act()
    else:
        pl.when(condition)(act)


def sides(size):
    return min(size - 1, 2)


def kernel(sizes, low_hbm, high_hbm, log_hbm, src_hbm, part, last, coarse,
           low_ref, high_ref, logs, srcs, packs, own_pack, own_rows, got_rows, own_lanes, got_lanes,
           own_far, got_far, own_corner, got_corner,
           inv_k, t_x, t_y, t_z, u_z, inv_d, res, dirs1, dirs2, dirs3,
           c_inv_k, c_t_x, c_t_y, c_t_z, c_u_z, c_inv_d, c_res, c_dirs1, c_dirs2, c_dirs3,
           io_sem, send_sem, recv_sem):
    nx, ny, nz = log_hbm.shape
    half = nz // 2
    wide_y, wide_z = logs.shape[1:]
    me = {axis: lax.axis_index(axis) for axis in AXES}
    count_x = sizes["gx"]
    x = me["gx"]

    def slots_x(step):
        return [({"gx": x + step}, x + step < count_x, x >= step, 0),
                ({"gx": x - step}, x >= step, x + step < count_x, 1)]

    def ring(axis, length, tile):
        n, here = sizes[axis], me[axis]
        if n == 1:
            return []
        if n == 2:
            start = pl.multiple_of((1 - here) * (length - tile), tile)
            return [dict(to={axis: 1 - here}, send=True, get=True, start=start, place=length,
                         send_high=here == 0, get_high=here == 1, index=0)]
        return [dict(to={axis: here - 1}, send=here > 0, get=here < n - 1, start=0, place=length,
                     send_high=False, get_high=False, index=0),
                dict(to={axis: here + 1}, send=here < n - 1, get=here > 0, start=length - tile,
                     place=length + tile, send_high=True, get_high=True, index=1)]

    ring_y = ring("gy", ny, ROWS)
    ring_z = ring("gz", nz, LANES)

    def packed_start(b):
        if isinstance(b["start"], int):
            return b["start"] * (half - LANES) // (nz - LANES)
        return pl.multiple_of((1 - me["gz"]) * (half - LANES), LANES)

    used = []

    class Message:
        def __init__(self, to, send, get, source, target):
            index = len(used)
            used.append(index)
            self.send, self.get = send, get
            self.copy = lambda: pltpu.make_async_remote_copy(
                src_ref=source, dst_ref=target, send_sem=send_sem.at[index],
                recv_sem=recv_sem.at[index], device_id=to, device_id_type=MESH)

    def start(messages):
        for m in messages:
            when(m.send, lambda: m.copy().start())

    def arrive(messages):
        for m in messages:
            when(m.get, lambda: m.copy().wait_recv())

    def drain(messages):
        for m in messages:
            when(m.send, lambda: m.copy().wait_send())

    partners = [(to, send) for step in (1, 2) for to, send, _, _ in slots_x(step)]
    partners += [(r["to"], r["send"]) for r in ring_y + ring_z]
    partners += [({**a["to"], **b["to"]}, both(a["send"], b["send"])) for a in ring_y for b in ring_z]
    partners += [({**to, **a["to"]}, both(send, a["send"]))
                 for to, send, _, _ in slots_x(1) for a in ring_y]
    barrier = pltpu.get_barrier_semaphore()
    count = 0
    for to, send in partners:
        when(send, lambda: pl.semaphore_signal(barrier, inc=1, device_id=to, device_id_type=MESH))
        count = count + (1 if send is True else send.astype(jnp.int32))

    own = pl.ds(REACH, nx)
    own_s = pl.ds(DEGREE, nx)
    log_in = pltpu.make_async_copy(log_hbm, logs.at[own, 0:ny, 0:nz], io_sem.at[0])
    src_in = pltpu.make_async_copy(src_hbm, srcs.at[own_s, 0:ny, 0:nz], io_sem.at[1])
    low_in = pltpu.make_async_copy(low_hbm, low_ref, io_sem.at[2])
    high_in = pltpu.make_async_copy(high_hbm, high_ref, io_sem.at[3])
    for copy in (log_in, src_in, low_in, high_in):
        copy.start()

    def plane_z(hbm, ref, layers):
        return [Message(b["to"], b["send"], b["get"],
                        ref.at[layers, 0:ny, pl.ds(b["start"], LANES)],
                        ref.at[layers, 0:ny, pl.ds(b["place"], LANES)]) for b in ring_z]

    def plane_y(hbm, ref, base, first, count_):
        return [Message(a["to"], a["send"], a["get"],
                        ref.at[pl.ds(base + first, count_), pl.ds(a["start"], ROWS), 0:nz],
                        ref.at[pl.ds(base + first, count_), pl.ds(a["place"], ROWS), 0:nz])
                for a in ring_y]

    def plane_yz(hbm, ref, layers):
        return [Message({**a["to"], **b["to"]}, both(a["send"], b["send"]), both(a["get"], b["get"]),
                        ref.at[layers, pl.ds(a["start"], ROWS), pl.ds(b["start"], LANES)],
                        ref.at[layers, pl.ds(a["place"], ROWS), pl.ds(b["place"], LANES)])
                for a in ring_y for b in ring_z]

    def span(side, first, last_, base):
        many = last_ - first + 1
        if side == 0:
            return pl.ds(base + nx - last_, many), pl.ds(base - last_, many)
        return pl.ds(base + first - 1, many), pl.ds(base + nx + first - 1, many)

    def along(hbm, ref, base, first, last_):
        out = []
        for to, send, get, side in slots_x(1):
            mine, theirs = span(side, first, last_, base)
            out.append(Message(to, send, get, ref.at[mine, 0:ny, 0:nz], ref.at[theirs, 0:ny, 0:nz]))
        return out

    z_log = plane_z(log_hbm, logs, own)
    z_src = plane_z(src_hbm, srcs, own_s)
    y_first = plane_y(log_hbm, logs, REACH, 1, nx - 2)
    y_log = (plane_y(log_hbm, logs, REACH, 0, 1) + plane_y(log_hbm, logs, REACH, nx - 1, 1)
             + plane_yz(log_hbm, logs, own))
    y_src = plane_y(src_hbm, srcs, DEGREE, 0, nx) + plane_yz(src_hbm, srcs, own_s)
    x_log = {1: along(log_hbm, logs, REACH, 1, 2), 3: along(log_hbm, logs, REACH, 3, 3)}
    x_src = {i: along(src_hbm, srcs, DEGREE, i, i) for i in (1, 2)}
    x_dir = [Message(to, send, get, dirs1.at[DEGREE + (nx - DEGREE, DEGREE - 1)[side], 0:ny, 0:nz],
                     dirs1.at[DEGREE + (-DEGREE, nx - 1 + DEGREE)[side], 0:ny, 0:nz])
             for to, send, get, side in slots_x(1)]
    rows = [Message({**to, **a["to"]}, both(send, a["send"]), both(get, a["get"]),
                    own_rows.at[side, a["index"]], got_rows.at[side, a["index"]])
            for to, send, get, side in slots_x(1) for a in ring_y]
    lanes = [Message(to, both(send, b["get"]), both(get, b["get"]),
                     own_lanes.at[side, b["index"]], got_lanes.at[0, side, b["index"]])
             for to, send, get, side in slots_x(1) for b in ring_z]
    corner = [Message({**to, **a["to"]}, both(send, both(a["send"], b["get"])), both(get, both(a["get"], b["get"])),
                      own_corner.at[side, a["index"], b["index"]], got_corner.at[side, a["index"], b["index"]])
              for to, send, get, side in slots_x(1) for a in ring_y for b in ring_z]
    packs_near = [Message(to, send, get, own_pack.at[:, :, 0:half],
                          packs.at[side, 0, :, 0:ny, 0:half]) for to, send, get, side in slots_x(1)]
    packs_edge = [Message({**to, **a["to"]}, both(send, a["send"]), both(get, a["get"]),
                          own_pack.at[:, pl.ds(a["start"], ROWS), 0:half],
                          packs.at[side, 0, :, pl.ds(a["place"], ROWS), 0:half])
                  for to, send, get, side in slots_x(1) for a in ring_y]
    packs_far = [Message(to, send, get, own_pack.at[0, :, 0:half],
                         packs.at[side, 1, 0, 0:ny, 0:half]) for to, send, get, side in slots_x(2)]
    packs_far += [Message(to, send, get, own_far.at[side], got_far.at[side])
                  for to, send, get, side in slots_x(2)]
    far = [get for _, _, get, _ in slots_x(2)]
    pass_y = [Message(a["to"], both(a["send"], far[side]), both(a["get"], far[side]),
                      packs.at[side, 1, 0, pl.ds(a["start"], ROWS), 0:half],
                      packs.at[side, 1, 0, pl.ds(a["place"], ROWS), 0:half])
              for side in (0, 1) for a in ring_y]
    pass_z = [Message(b["to"], both(b["send"], far[side]), both(b["get"], far[side]),
                      packs.at[side, 1, 0, 0:ny, pl.ds(packed_start(b), LANES)],
                      got_lanes.at[1, side, b["index"]])
              for side in (0, 1) for b in ring_z]

    def pair_block(ref, base, at):
        a = pooled(ref[(base,) + at], ref[(base + 1,) + at])
        b = pooled(ref[(base + 2,) + at], ref[(base + 3,) + at])
        return jnp.where(even(a.shape, 0), a, b)

    tile_lane = iota((ny, LANES), 1)

    def pack_rows(side, a, kind, at):
        ref, base = ((logs, REACH), (srcs, DEGREE))[kind]

        def edge(i):
            layer = (nx - i, i - 1)[side]
            return ref[base + layer, pl.ds(a["start"], ROWS), at]
        high = a["send_high"]
        one, two = edge(1), edge(2)
        spot = iota(one.shape, 0)
        if kind == 0:
            three = edge(3)
            two = pick(high, roll(two, 5, 0), roll(two, 3, 0))
            three = pick(high, roll(three, 3, 0), roll(three, 5, 0))
            first = pick(high, spot - 5, 2 - spot) >= 0
            second = (spot == 3) | (spot == 4)
            return jnp.where(first, one, jnp.where(second, two, three))
        two = pick(high, roll(two, 6, 0), roll(two, 2, 0))
        first = pick(high, spot - 6, 1 - spot) >= 0
        return jnp.where(first, one, two)

    STRIP = 8

    def side_by_side(tiles, high):
        out = None
        for k, a in enumerate(tiles):
            a = pick(high, roll(a, STRIP * (k + 1), 1), roll(a, STRIP * k, 1))
            out = a if out is None else jnp.where(tile_lane[:a.shape[0]] >= STRIP * k, a, out)
        return out

    def strip(a, k, high):
        return pick(high, roll(a, -STRIP * (k + 1), 1), roll(a, -STRIP * k, 1))

    def tile_of(b):
        return (slice(b["place"], b["place"] + LANES),
                slice(half + b["place"] - nz, half + b["place"] - nz + LANES))

    def pack_lanes(side, b):
        at, at_pack = tile_of(b)
        tiles = [logs[REACH + (nx - i, i - 1)[side], 0:ny, at] for i in (1, 2, 3)]
        tiles += [srcs[DEGREE + (nx - i, i - 1)[side], 0:ny, at] for i in (1, 2)]
        tiles += [own_pack[kind, :, at_pack] for kind in (0, 1)]
        own_lanes[side, b["index"]] = side_by_side(tiles, b["get_high"])
        for a in ring_y:
            tiles = [pack_rows(side, a, kind, at) for kind in (0, 1)]
            tiles += [own_pack[kind, pl.ds(a["start"], ROWS), at_pack] for kind in (0, 1)]
            own_corner[side, a["index"], b["index"]] = side_by_side(tiles, b["get_high"])

    def unpack_far(side, b):
        tile = got_lanes[1, side, b["index"]]
        even_lane = even(tile.shape, 1)
        packs[side, 1, 0, 0:ny, tile_of(b)[1]] = pick(
            b["get_high"], jnp.where(even_lane, roll(tile, -1, 1), tile),
            jnp.where(even_lane, tile, roll(tile, 1, 1)))

    def unpack_lanes(side, b):
        got = got_lanes[0, side, b["index"]]
        at, at_pack = tile_of(b)
        high = b["get_high"]
        packs[side, 0, 0, 0:ny, at_pack] = strip(got, 5, high)
        packs[side, 0, 1, 0:ny, at_pack] = strip(got, 6, high)
        for i in (1, 2, 3):
            logs[REACH + (-i, nx - 1 + i)[side], 0:ny, at] = strip(got, i - 1, high)
        for i in (1, 2):
            srcs[DEGREE + (-i, nx - 1 + i)[side], 0:ny, at] = strip(got, i + 2, high)
        for a in ring_y:
            got = got_corner[side, a["index"], b["index"]]
            rows_at = slice(a["place"], a["place"] + ROWS)
            for kind in (0, 1):
                place_rows(side, a, kind, strip(got, kind, high), at)
                packs[side, 0, kind, rows_at, at_pack] = strip(got, kind + 2, high)

    def place_rows(side, a, kind, got, at):
        ref, base = ((logs, REACH), (srcs, DEGREE))[kind]
        rows_at = slice(a["place"], a["place"] + ROWS)
        shifts = ((3, 5), (5, 3)) if kind == 0 else ((2, 6),)
        ref[base + (-1, nx)[side], rows_at, at] = got
        for i, (if_high, if_low) in enumerate(shifts):
            layer = (-2 - i, nx + 1 + i)[side]
            ref[base + layer, rows_at, at] = pick(a["get_high"], roll(got, if_high, 0), roll(got, if_low, 0))

    core = (slice(0, ny), slice(0, nz))
    beside = (slice(0, ny), slice(nz, wide_z))
    rim = (slice(ny, wide_y), slice(0, wide_z))
    scales = (0.125, 1.0)
    whole = (logs, srcs)
    bases = (REACH, DEGREE)

    def own_coarse(kind, at):
        return pair_block(whole[kind], bases[kind], at) * scales[kind]

    def keep_coarse(kind, at, block):
        if kind == 0:
            c_inv_k[(0,) + at] = jnp.exp(-block)
        else:
            c_res[(0,) + at] = block

    def fold_lanes(a):
        return jnp.where(even((a.shape[0], half), 1), a[:, :half], a[:, half:nz])

    log_in.wait()
    block = own_coarse(0, core)
    own_pack[0, :, 0:half] = fold_lanes(block)
    keep_coarse(0, core, block)
    src_in.wait()
    block = own_coarse(1, core)
    flat = fold_lanes(block)
    own_pack[1, :, 0:half] = flat
    keep_coarse(1, core, block)
    upper, lower = flat[:ny // 2], flat[ny // 2:]
    upper_even = even(upper.shape, 0)
    own_far[0] = jnp.where(upper_even, roll(upper, -1, 0), lower)
    own_far[1] = jnp.where(upper_even, upper, roll(lower, 1, 0))
    for side in (0, 1):
        for a in ring_y:
            for kind in (0, 1):
                own_rows[side, a["index"], kind] = pack_rows(side, a, kind, slice(0, nz))

    pl.semaphore_wait(barrier, count)
    start(z_log)
    start(z_src)
    start(y_first)
    start(packs_far)
    start(x_log[1])
    start(rows)
    start(y_log)
    start(y_src)

    arrive(z_log)
    arrive(z_src)
    if ring_z:
        for kind in (0, 1):
            block = own_coarse(kind, beside)
            own_pack[kind, :, half:] = block
            keep_coarse(kind, beside, block)
    for side in (0, 1):
        for b in ring_z:
            pack_lanes(side, b)
    start(lanes)
    start(corner)
    start(x_src[1])
    start(packs_edge)
    start(packs_near)
    start(x_log[3])
    start(x_src[2])

    def clear(ref, *at):
        ref[at] = jnp.zeros_like(ref[at])

    if ring_y and ring_z:
        for side in (0, 1):
            clear(packs, side, 1, 0, slice(ny, wide_y), slice(half, packs.shape[4]))
    for step in (1, 2):
        for _, _, get, side in slots_x(step):
            @pl.when(jnp.logical_not(get))
            def _():
                clear(packs, side, step - 1)
                clear(got_lanes, step - 1, side)
                if step == 2:
                    clear(got_far, side)
                if step == 1:
                    clear(got_rows, side)
                    clear(got_corner, side)
                    for i in range(1, DEGREE + 1):
                        layer = (-i, nx - 1 + i)[side]
                        clear(logs, REACH + layer)
                        clear(srcs, DEGREE + layer)
                    clear(dirs1, DEGREE + layer)
    for a in ring_y:
        if a["get"] is not True:
            @pl.when(jnp.logical_not(a["get"]))
            def _():
                at = slice(a["place"], a["place"] + ROWS)
                for layer in range(nx + 2 * REACH):
                    clear(logs, layer, at)
                for layer in range(nx + 2 * DEGREE):
                    clear(srcs, layer, at)
                for side in (0, 1):
                    for step in (1, 2):
                        clear(packs, side, step - 1, slice(None), at)
                    clear(got_rows, side, a["index"])
                    clear(got_corner, side, a["index"])

    row = iota((wide_y, wide_z), 0)
    lane = iota((wide_y, wide_z), 1)

    def cuts(axis, ring_, length, total, tile):
        n, here = sizes[axis], me[axis]
        if n == 1:
            return [total - 1]
        if n == 2:
            return [jnp.where(here == 0, total - 1, length - 1)]
        return [length + tile - 1, jnp.where(here < n - 1, -1, length - 1),
                jnp.where(here > 0, -1, total - 1)]

    cuts_y = cuts("gy", ring_y, ny, wide_y, ROWS)
    cuts_z = cuts("gz", ring_z, nz, wide_z, LANES)

    def cut(t, index, at):
        for c in at:
            t = jnp.where(index == c, 0.0, t)
        return t

    row_pair, lane_pair = row | 1, lane | 1
    even_row = even((wide_y, wide_z), 0)

    all_rows = slice(0, wide_y)
    own_part = slice(0, ny)
    rim_part = slice(ny, wide_y)

    def fine_k(i, part_=all_rows):
        inv_k[REACH + i, part_] = jnp.exp(-logs[REACH + i, part_])

    def fine_z(i, part_=all_rows):
        mine = inv_k[REACH + i, part_]
        t_z[DEGREE + i, part_] = cut(2.0 * inverse(mine + roll(mine, -1, 1)), lane[part_], cuts_z)

    def fine_y(i, at=slice(None)):
        mine = inv_k[REACH + i, :, at]
        t_y[DEGREE + i, :, at] = cut(2.0 * inverse(mine + roll(mine, -1, 0)), row[:, at], cuts_y)

    def fine_d_core(i):
        y, z = t_y[DEGREE + i, :, 0:nz], t_z[DEGREE + i, own_part]
        x = t_x[(REACH + i,) + core] + t_x[(REACH + i - 1,) + core]
        back = roll(z, 1, 1)
        u_z[DEGREE + i, own_part] = back
        total = (y + roll(y, 1, 0))[:ny] + (z + back)[:, :nz] + x
        inv_d[(DEGREE + i,) + core] = inverse(total + STORAGE)

    flag = {(step, side): get.astype(jnp.float32)
            for step in (1, 2) for _, _, get, side in slots_x(step)}

    def fine_x(i, part_=all_rows):
        t = 2.0 * inverse(inv_k[REACH + i, part_] + inv_k[REACH + i + 1, part_])
        if i == -1:
            t = t * flag[1, 0]
        if i == nx - 1:
            t = t * flag[1, 1]
        t_x[REACH + i, part_] = t

    def fine_d(i):
        y, z = t_y[DEGREE + i], t_z[DEGREE + i]
        back = roll(z, 1, 1)
        u_z[DEGREE + i] = back
        total = (y + roll(y, 1, 0)) + (z + back) + (t_x[REACH + i] + t_x[REACH + i - 1])
        inv_d[DEGREE + i] = inverse(total + STORAGE)

    def coarse_yz(i):
        mine = c_inv_k[i]
        c_t_y[i] = cut(4.0 * inverse(mine + roll(mine, -2, 0)), row_pair, cuts_y)
        c_t_z[i] = cut(4.0 * inverse(mine + roll(mine, -2, 1)), lane_pair, cuts_z)

    def swap(a):
        return jnp.where(even_row, roll(a, -1, 0), roll(a, 1, 0))

    def coarse_x(i):
        if i < 0:
            mine = c_inv_k[0]
            c_t_x[0] = 4.0 * inverse(mine + swap(mine))
            return
        t = 4.0 * inverse(c_inv_k[i] + c_inv_k[i + 1])
        if i in (0, 2):
            step = i // 2 + 1
            t = t * jnp.where(even_row, flag[step, 0], flag[step, 1])
        c_t_x[i + 1] = t

    def coarse_d(i):
        y, z = c_t_y[i], c_t_z[i]
        back = roll(z, 2, 1)
        c_u_z[i] = back
        total = (y + roll(y, 2, 0)) + (z + back) + (c_t_x[i] + c_t_x[i + 1])
        c_inv_d[i] = inverse(total + 8.0 * STORAGE)

    low_in.wait()
    high_in.wait()
    low = jnp.full((1, wide_z), low_ref[0])
    high = jnp.full((1, wide_z), high_ref[0])
    theta = (high + low) * 0.5
    delta = (high - low) * 0.5
    sigma = theta / delta
    rho = 1.0 / sigma
    inv_theta = 1.0 / theta
    keep, gain = [None], [None]
    for _ in range(DEGREE):
        rho_next = 1.0 / (2.0 * sigma - rho)
        keep.append(rho_next * rho)
        gain.append(2.0 * rho_next / delta)
        rho = rho_next

    def fine_first(i, at=(slice(None), slice(None))):
        dirs1[(DEGREE + i,) + at] = (srcs[(DEGREE + i,) + at] * inv_d[(DEGREE + i,) + at]
                                     * inv_theta[:, at[1]])

    def coarse_first(i, at=(slice(None), slice(None))):
        c_dirs1[(i,) + at] = c_res[(i,) + at] * c_inv_d[(i,) + at] * inv_theta[:, at[1]]

    fields = [None, dirs1, dirs2, dirs3]
    c_fields = [None, c_dirs1, c_dirs2, c_dirs3]

    def flows(d, y, z, u, k):
        y = y * (d - roll(d, -k, 0))
        return (y - roll(y, k, 0)) + (z * (d - roll(d, -k, 1)) + u * (d - roll(d, k, 1)))

    def core_flows(d, y, z, u, k):
        dy, dz = d[:, :nz], d[:ny]
        y = y[:, :nz] * (dy - roll(dy, -k, 0))
        z = (z[:ny] * (dz - roll(dz, -k, 1)) + u[:ny] * (dz - roll(dz, k, 1)))[:, :nz]
        return (y - roll(y, k, 0))[:ny] + z

    def fine_turn(turn, i, small=False):
        ref, base = fields[turn], DEGREE + 1 - turn
        at = core if small else (all_rows, slice(0, wide_z))
        d = ref[base + i]
        flow = (core_flows if small else flows)(d, t_y[DEGREE + i], t_z[DEGREE + i], u_z[DEGREE + i], 1)
        d = d[at]
        r = (srcs if turn == 1 else res)[(DEGREE + i,) + at] - STORAGE * d - flow
        r = r - t_x[(REACH + i,) + at] * (d - ref[(base + i + 1,) + at])
        r = r - t_x[(REACH + i - 1,) + at] * (d - ref[(base + i - 1,) + at])
        later = keep[turn][:, at[1]] * d + gain[turn][:, at[1]] * (r * inv_d[(DEGREE + i,) + at])
        if turn < DEGREE:
            res[(DEGREE + i,) + at] = r
            fields[turn + 1][(base - 1 + i,) + at] = later
        else:
            part[i] = dirs1[(DEGREE + i,) + at] + dirs2[(DEGREE - 1 + i,) + at] + d
            last[i] = later

    def coarse_turn(turn, i, small=False):
        ref = c_fields[turn]
        at = core if small else (all_rows, slice(0, wide_z))
        d = ref[i]
        flow = (core_flows if small else flows)(d, c_t_y[i], c_t_z[i], c_u_z[i], 2)
        d = d[at]
        if i > 0:
            inner_side = ref[(i - 1,) + at]
        else:
            inner_side = jnp.where(even(d.shape, 0), roll(d, -1, 0), roll(d, 1, 0))
        r = c_res[(i,) + at] - 8.0 * STORAGE * d - flow
        r = r - c_t_x[(i + 1,) + at] * (d - ref[(i + 1,) + at])
        r = r - c_t_x[(i,) + at] * (d - inner_side)
        later = keep[turn][:, at[1]] * d + gain[turn][:, at[1]] * (r * c_inv_d[(i,) + at])
        if turn < DEGREE:
            c_res[(i,) + at] = r
            c_fields[turn + 1][(i,) + at] = later
        else:
            total = c_dirs1[(i,) + at] + c_dirs2[(i,) + at] + d + later
            top = even((ny, nz), 0)
            coarse[0] = jnp.where(top, total, roll(total, 1, 0))
            coarse[1] = jnp.where(top, roll(total, -1, 0), total)

    def unpack_rows(side, kind):
        for a in ring_y:
            place_rows(side, a, kind, got_rows[side, a["index"], kind], slice(0, nz))

    def spread(step, kind, near):
        left, right = packs[0, step - 1, kind], packs[1, step - 1, kind]
        top = even(left.shape, 0)
        if near:
            a = jnp.where(top, roll(left, -1, 0), roll(right, 1, 0))
        else:
            a = jnp.where(top, left, right)
        return jnp.concatenate([spread_lanes(a[:, :half]), a[:, half:]], axis=1)

    def spread_lanes(main):
        even_lane = even(main.shape, 1)
        return jnp.concatenate([jnp.where(even_lane, main, roll(main, 1, 1)),
                                jnp.where(even_lane, roll(main, -1, 1), main)], axis=1)

    def spread_far():
        left, right = got_far[0], got_far[1]
        first = even(left.shape, 0)
        upper = jnp.where(first, left, roll(right, 1, 0))
        lower = jnp.where(first, roll(left, -1, 0), right)
        return spread_lanes(jnp.concatenate([upper, lower], axis=0))

    def halo(i):
        return (-i, nx - 1 + i)

    mine = range(nx)
    inner = range(1, nx - 1)
    ends = (0, nx - 1)

    for i in mine:
        fine_k(i, own_part)
    for i in mine:
        fine_z(i, own_part)
    for i in range(nx - 1):
        fine_x(i, own_part)
    arrive(y_first)
    for i in inner:
        if ring_y:
            inv_k[REACH + i, rim_part, 0:nz] = jnp.exp(-logs[REACH + i, rim_part, 0:nz])
        fine_y(i, slice(0, nz))
        fine_d_core(i)
        fine_first(i, core)
    start(x_dir)
    arrive(packs_far)
    start(pass_y)
    start(pass_z)
    arrive(y_log)
    if ring_y:
        for i in mine:
            fine_k(i, rim_part)
        for i in mine:
            fine_z(i, rim_part)
        for i in range(nx - 1):
            fine_x(i, rim_part)
        keep_coarse(0, rim, own_coarse(0, rim))
    for i in mine:
        fine_y(i)
    for i in inner:
        fine_d(i)
    arrive(y_src)
    for i in inner:
        if ring_z:
            fine_first(i, beside)
        if ring_y:
            fine_first(i, rim)
    if ring_y:
        keep_coarse(1, rim, own_coarse(1, rim))
    coarse_yz(0)
    coarse_x(-1)

    arrive(x_log[1])
    arrive(rows)
    arrive(lanes)
    arrive(corner)
    for side in (0, 1):
        unpack_rows(side, 0)
        unpack_rows(side, 1)
        for b in ring_z:
            unpack_lanes(side, b)
    for i in halo(1) + halo(2):
        fine_k(i)
    for i in halo(1):
        fine_y(i)
        fine_z(i)
    for i in (-2, -1, nx - 1, nx):
        fine_x(i)
    for i in ends + halo(1):
        fine_d(i)
    for i in ends:
        fine_first(i)
    for i in inner:
        fine_turn(1, i)
    arrive(x_src[1])
    for i in halo(1):
        fine_first(i)
    for i in ends:
        fine_turn(1, i)
    for i in inner:
        fine_turn(2, i)

    arrive(packs_near)
    arrive(packs_edge)
    c_inv_k[1] = jnp.exp(-spread(1, 0, True))
    c_inv_k[2] = jnp.exp(-spread(1, 0, False))
    c_res[1] = spread(1, 1, True)
    c_res[2] = spread(1, 1, False)
    coarse_yz(1)
    coarse_x(0)
    coarse_x(1)
    coarse_yz(2)
    for i in (0, 1):
        coarse_d(i)
        coarse_first(i)
    coarse_turn(1, 0)

    arrive(pass_z)
    for side in (0, 1):
        for b in ring_z:
            unpack_far(side, b)
    arrive(pass_y)
    c_inv_k[3] = jnp.exp(-spread(2, 0, True))
    c_inv_k[4] = jnp.exp(-spread(2, 0, False))
    c_res[(3,) + core] = spread_far()
    coarse_yz(3)
    coarse_x(2)
    coarse_x(3)
    for i in (2, 3):
        coarse_d(i)
    coarse_first(2)
    coarse_first(3, core)
    coarse_turn(1, 1)
    coarse_turn(1, 2, True)
    coarse_turn(2, 0)
    coarse_turn(2, 1, True)
    coarse_turn(3, 0, True)

    arrive(x_log[3])
    for i in halo(3):
        fine_k(i)
    for i in halo(2):
        fine_y(i)
        fine_z(i)
    for i in (-3, nx + 1):
        fine_x(i)
    for i in halo(2):
        fine_d(i)
    arrive(x_src[2])
    for i in halo(2):
        fine_first(i)
    for i in halo(1):
        fine_turn(1, i)
    for i in ends:
        fine_turn(2, i)
    for i in inner:
        fine_turn(3, i, True)

    for group in ([z_log, z_src, y_first, y_log, y_src, rows, corner, x_dir, packs_near, packs_edge, packs_far, pass_y, pass_z, lanes]
                  + list(x_log.values()) + list(x_src.values())):
        drain(group)

    arrive(x_dir)
    for i in halo(2):
        fine_turn(1, i, True)
    for i in halo(1):
        fine_turn(2, i, True)
    for i in ends:
        fine_turn(3, i, True)


def shards(sizes, log_perm, source, low_bound, high_bound):
    nx, ny, nz = log_perm.shape
    wide_y = ny + ROWS * sides(sizes["gy"])
    wide_z = nz + LANES * sides(sizes["gz"])
    half = nz // 2
    f32 = lambda *shape: pltpu.VMEM(shape, jnp.float32)
    fine = lambda reach: f32(nx + 2 * reach, wide_y, wide_z)
    pairs = lambda n: f32(n, wide_y, wide_z)
    log_perm = pltpu.with_memory_space_constraint(log_perm, pltpu.HBM)
    source = pltpu.with_memory_space_constraint(source, pltpu.HBM)
    hbm = pl.BlockSpec(memory_space=pltpu.HBM)
    vmem = pl.BlockSpec(memory_space=pltpu.VMEM)
    whole = jax.ShapeDtypeStruct((nx, ny, nz), jnp.float32)
    messages = 96
    part, last, coarse = pl.pallas_call(
        functools.partial(kernel, sizes),
        out_shape=(whole, whole, jax.ShapeDtypeStruct((nx // 2, ny, nz), jnp.float32)),
        in_specs=[hbm] * 4,
        out_specs=(vmem,) * 3,
        scratch_shapes=[
            pltpu.SMEM((1,), jnp.float32),
            pltpu.SMEM((1,), jnp.float32),
            fine(REACH), fine(DEGREE),
            f32(2, 2, 2, wide_y, half + wide_z - nz),
            f32(2, ny, half + wide_z - nz),
            f32(2, max(1, sides(sizes["gy"])), 2, ROWS, nz),
            f32(2, max(1, sides(sizes["gy"])), 2, ROWS, nz),
            f32(2, max(1, sides(sizes["gz"])), ny, LANES),
            f32(2, 2, max(1, sides(sizes["gz"])), ny, LANES),
            f32(2, ny // 2, half),
            f32(2, ny // 2, half),
            f32(2, max(1, sides(sizes["gy"])), max(1, sides(sizes["gz"])), ROWS, LANES),
            f32(2, max(1, sides(sizes["gy"])), max(1, sides(sizes["gz"])), ROWS, LANES),
            fine(REACH), fine(REACH), fine(DEGREE), fine(DEGREE), fine(DEGREE), fine(DEGREE), fine(DEGREE),
            fine(DEGREE), fine(DEGREE - 1), fine(DEGREE - 2),
            pairs(5), pairs(5), pairs(4), pairs(4), pairs(4), pairs(4), pairs(4), pairs(4), pairs(3), pairs(2),
            pltpu.SemaphoreType.DMA((4,)),
            pltpu.SemaphoreType.DMA((messages,)),
            pltpu.SemaphoreType.DMA((messages,)),
        ],
        compiler_params=pltpu.CompilerParams(
            collective_id=0, has_side_effects=True, vmem_limit_bytes=24 * 2**20),
    )(low_bound, high_bound, log_perm, source)
    fine_pressure = part + last
    return fine_pressure, fine_pressure - jnp.repeat(coarse, 2, axis=0)


def solution(mesh):
    sizes = {axis: mesh.shape[axis] for axis in AXES}
    spec = P(("groups", "gx"), "gy", "gz")
    return jax.shard_map(
        functools.partial(shards, sizes),
        mesh=mesh,
        in_specs=(spec, spec, P(), P()),
        out_specs=(spec, spec),
        check_vma=False,
    )
```

```python
import functools

import jax
import jax.numpy as jnp
from jax import lax
from jax.experimental import pallas as pl
from jax.experimental.pallas import tpu as pltpu
from jax.sharding import PartitionSpec as P

DEGREE = 3
REACH = DEGREE
STORAGE = 0.1
LANES = 128
ROWS = 8
MESH = pl.DeviceIdType.MESH
AXES = ("gx", "gy", "gz")


def roll(a, shift, axis):
    return pltpu.roll(a, shift % a.shape[axis], axis)


def iota(shape, axis):
    return lax.broadcasted_iota(jnp.int32, shape, axis)


def even(shape, axis):
    return iota(shape, axis) % 2 == 0


def pair_sum(a, axis):
    return a + jnp.where(even(a.shape, axis), roll(a, -1, axis), roll(a, 1, axis))


def pooled(a, b):
    return pair_sum(pair_sum(a + b, 0), 1)


def inverse(a):
    r = pl.reciprocal(a, approx=True)
    return r * (2.0 - a * r)


def pick(condition, a, b):
    if isinstance(condition, bool):
        return a if condition else b
    return jnp.where(condition, a, b)


def both(a, b):
    if a is True:
        return b
    return a if b is True else jnp.logical_and(a, b)


def when(condition, act):
    if condition is True:
        act()
    else:
        pl.when(condition)(act)


def sides(size):
    return min(size - 1, 2)


def kernel(sizes, low_hbm, high_hbm, log_hbm, src_hbm, part, last, coarse,
           low_ref, high_ref, logs, srcs, packs, own_pack, own_rows, got_rows, own_lanes, got_lanes,
           own_far, got_far, own_corner, got_corner,
           inv_k, t_x, t_y, t_z, u_z, inv_d, res, dirs1, dirs2, dirs3,
           c_inv_k, c_t_x, c_t_y, c_t_z, c_u_z, c_inv_d, c_res, c_dirs1, c_dirs2, c_dirs3,
           io_sem, send_sem, recv_sem):
    nx, ny, nz = log_hbm.shape
    half = nz // 2
    wide_y, wide_z = logs.shape[1:]
    me = {axis: lax.axis_index(axis) for axis in AXES}
    count_x = sizes["gx"]
    x = me["gx"]

    def slots_x(step):
        return [({"gx": x + step}, x + step < count_x, x >= step, 0),
                ({"gx": x - step}, x >= step, x + step < count_x, 1)]

    def ring(axis, length, tile):
        n, here = sizes[axis], me[axis]
        if n == 1:
            return []
        if n == 2:
            start = pl.multiple_of((1 - here) * (length - tile), tile)
            return [dict(to={axis: 1 - here}, send=True, get=True, start=start, place=length,
                         send_high=here == 0, get_high=here == 1, index=0)]
        return [dict(to={axis: here - 1}, send=here > 0, get=here < n - 1, start=0, place=length,
                     send_high=False, get_high=False, index=0),
                dict(to={axis: here + 1}, send=here < n - 1, get=here > 0, start=length - tile,
                     place=length + tile, send_high=True, get_high=True, index=1)]

    ring_y = ring("gy", ny, ROWS)
    ring_z = ring("gz", nz, LANES)

    def packed_start(b):
        if isinstance(b["start"], int):
            return b["start"] * (half - LANES) // (nz - LANES)
        return pl.multiple_of((1 - me["gz"]) * (half - LANES), LANES)

    used = []

    class Message:
        def __init__(self, to, send, get, source, target):
            index = len(used)
            used.append(index)
            self.send, self.get = send, get
            self.copy = lambda: pltpu.make_async_remote_copy(
                src_ref=source, dst_ref=target, send_sem=send_sem.at[index],
                recv_sem=recv_sem.at[index], device_id=to, device_id_type=MESH)

    def start(messages):
        for m in messages:
            when(m.send, lambda: m.copy().start())

    def arrive(messages):
        for m in messages:
            when(m.get, lambda: m.copy().wait_recv())

    def drain(messages):
        for m in messages:
            when(m.send, lambda: m.copy().wait_send())

    partners = [({**to, **a["to"]}, both(send, a["send"]))
                for to, send, _, _ in slots_x(1) for a in ring_y]
    partners += [(to, send) for step in (2, 1) for to, send, _, _ in slots_x(step)]
    partners += [({**a["to"], **b["to"]}, both(a["send"], b["send"])) for a in ring_y for b in ring_z]
    partners += [(r["to"], r["send"]) for r in ring_y + ring_z]
    barrier = pltpu.get_barrier_semaphore()
    count = 0
    for to, send in partners:
        when(send, lambda: pl.semaphore_signal(barrier, inc=1, device_id=to, device_id_type=MESH))
        count = count + (1 if send is True else send.astype(jnp.int32))

    own = pl.ds(REACH, nx)
    own_s = pl.ds(DEGREE, nx)
    log_in = pltpu.make_async_copy(log_hbm, logs.at[own, 0:ny, 0:nz], io_sem.at[0])
    src_in = pltpu.make_async_copy(src_hbm, srcs.at[own_s, 0:ny, 0:nz], io_sem.at[1])
    low_in = pltpu.make_async_copy(low_hbm, low_ref, io_sem.at[2])
    high_in = pltpu.make_async_copy(high_hbm, high_ref, io_sem.at[3])
    for copy in (log_in, src_in, low_in, high_in):
        copy.start()

    def plane_z(hbm, ref, layers):
        return [Message(b["to"], b["send"], b["get"],
                        ref.at[layers, 0:ny, pl.ds(b["start"], LANES)],
                        ref.at[layers, 0:ny, pl.ds(b["place"], LANES)]) for b in ring_z]

    def plane_y(hbm, ref, base, first, count_):
        return [Message(a["to"], a["send"], a["get"],
                        ref.at[pl.ds(base + first, count_), pl.ds(a["start"], ROWS), 0:nz],
                        ref.at[pl.ds(base + first, count_), pl.ds(a["place"], ROWS), 0:nz])
                for a in ring_y]

    def plane_yz(hbm, ref, layers):
        return [Message({**a["to"], **b["to"]}, both(a["send"], b["send"]), both(a["get"], b["get"]),
                        ref.at[layers, pl.ds(a["start"], ROWS), pl.ds(b["start"], LANES)],
                        ref.at[layers, pl.ds(a["place"], ROWS), pl.ds(b["place"], LANES)])
                for a in ring_y for b in ring_z]

    def span(side, first, last_, base):
        many = last_ - first + 1
        if side == 0:
            return pl.ds(base + nx - last_, many), pl.ds(base - last_, many)
        return pl.ds(base + first - 1, many), pl.ds(base + nx + first - 1, many)

    def along(hbm, ref, base, first, last_):
        out = []
        for to, send, get, side in slots_x(1):
            mine, theirs = span(side, first, last_, base)
            out.append(Message(to, send, get, ref.at[mine, 0:ny, 0:nz], ref.at[theirs, 0:ny, 0:nz]))
        return out

    z_log = plane_z(log_hbm, logs, own)
    z_src = plane_z(src_hbm, srcs, own_s)
    y_first = plane_y(log_hbm, logs, REACH, 1, nx - 2)
    y_log = (plane_y(log_hbm, logs, REACH, 0, 1) + plane_y(log_hbm, logs, REACH, nx - 1, 1)
             + plane_yz(log_hbm, logs, own))
    y_src = plane_y(src_hbm, srcs, DEGREE, 0, nx) + plane_yz(src_hbm, srcs, own_s)
    x_log = {1: along(log_hbm, logs, REACH, 1, 2), 3: along(log_hbm, logs, REACH, 3, 3)}
    x_src = {i: along(src_hbm, srcs, DEGREE, i, i) for i in (1, 2)}
    x_dir = [Message(to, send, get, dirs1.at[DEGREE + (nx - DEGREE, DEGREE - 1)[side], 0:ny, 0:nz],
                     dirs1.at[DEGREE + (-DEGREE, nx - 1 + DEGREE)[side], 0:ny, 0:nz])
             for to, send, get, side in slots_x(1)]
    rows = [Message({**to, **a["to"]}, both(send, a["send"]), both(get, a["get"]),
                    own_rows.at[side, a["index"]], got_rows.at[side, a["index"]])
            for to, send, get, side in slots_x(1) for a in ring_y]
    lanes = [Message(to, both(send, b["get"]), both(get, b["get"]),
                     own_lanes.at[side, b["index"]], got_lanes.at[0, side, b["index"]])
             for to, send, get, side in slots_x(1) for b in ring_z]
    corner = [Message({**to, **a["to"]}, both(send, both(a["send"], b["get"])), both(get, both(a["get"], b["get"])),
                      own_corner.at[side, a["index"], b["index"]], got_corner.at[side, a["index"], b["index"]])
              for to, send, get, side in slots_x(1) for a in ring_y for b in ring_z]
    packs_near = [Message(to, send, get, own_pack.at[:, :, 0:half],
                          packs.at[side, 0, :, 0:ny, 0:half]) for to, send, get, side in slots_x(1)]
    packs_edge = [Message({**to, **a["to"]}, both(send, a["send"]), both(get, a["get"]),
                          own_pack.at[:, pl.ds(a["start"], ROWS), 0:half],
                          packs.at[side, 0, :, pl.ds(a["place"], ROWS), 0:half])
                  for to, send, get, side in slots_x(1) for a in ring_y]
    packs_far = [Message(to, send, get, own_pack.at[0, :, 0:half],
                         packs.at[side, 1, 0, 0:ny, 0:half]) for to, send, get, side in slots_x(2)]
    packs_far += [Message(to, send, get, own_far.at[side], got_far.at[side])
                  for to, send, get, side in slots_x(2)]
    far = [get for _, _, get, _ in slots_x(2)]
    pass_y = [Message(a["to"], both(a["send"], far[side]), both(a["get"], far[side]),
                      packs.at[side, 1, 0, pl.ds(a["start"], ROWS), 0:half],
                      packs.at[side, 1, 0, pl.ds(a["place"], ROWS), 0:half])
              for side in (0, 1) for a in ring_y]
    pass_z = [Message(b["to"], both(b["send"], far[side]), both(b["get"], far[side]),
                      packs.at[side, 1, 0, 0:ny, pl.ds(packed_start(b), LANES)],
                      got_lanes.at[1, side, b["index"]])
              for side in (0, 1) for b in ring_z]

    def pair_block(ref, base, at):
        a = pooled(ref[(base,) + at], ref[(base + 1,) + at])
        b = pooled(ref[(base + 2,) + at], ref[(base + 3,) + at])
        return jnp.where(even(a.shape, 0), a, b)

    tile_lane = iota((ny, LANES), 1)

    def pack_rows(side, a, kind, at):
        ref, base = ((logs, REACH), (srcs, DEGREE))[kind]

        def edge(i):
            layer = (nx - i, i - 1)[side]
            return ref[base + layer, pl.ds(a["start"], ROWS), at]
        high = a["send_high"]
        one, two = edge(1), edge(2)
        spot = iota(one.shape, 0)
        if kind == 0:
            three = edge(3)
            two = pick(high, roll(two, 5, 0), roll(two, 3, 0))
            three = pick(high, roll(three, 3, 0), roll(three, 5, 0))
            first = pick(high, spot - 5, 2 - spot) >= 0
            second = (spot == 3) | (spot == 4)
            return jnp.where(first, one, jnp.where(second, two, three))
        two = pick(high, roll(two, 6, 0), roll(two, 2, 0))
        first = pick(high, spot - 6, 1 - spot) >= 0
        return jnp.where(first, one, two)

    STRIP = 8

    def side_by_side(tiles, high):
        out = None
        for k, a in enumerate(tiles):
            a = pltpu.roll(a, STRIP * k + pick(high, STRIP, 0), 1)
            out = a if out is None else jnp.where(tile_lane[:a.shape[0]] >= STRIP * k, a, out)
        return out

    def strip(a, k, high):
        return pltpu.roll(a, LANES - STRIP * k - pick(high, STRIP, 0), 1)

    def tile_of(b):
        return (slice(b["place"], b["place"] + LANES),
                slice(half + b["place"] - nz, half + b["place"] - nz + LANES))

    def pack_lanes(side, b):
        at, at_pack = tile_of(b)
        tiles = [logs[REACH + (nx - i, i - 1)[side], 0:ny, at] for i in (1, 2, 3)]
        tiles += [srcs[DEGREE + (nx - i, i - 1)[side], 0:ny, at] for i in (1, 2)]
        tiles += [own_pack[kind, :, at_pack] for kind in (0, 1)]
        own_lanes[side, b["index"]] = side_by_side(tiles, b["get_high"])

    def pack_corner(side, b):
        at, at_pack = tile_of(b)
        for a in ring_y:
            tiles = [pack_rows(side, a, kind, at) for kind in (0, 1)]
            tiles += [own_pack[kind, pl.ds(a["start"], ROWS), at_pack] for kind in (0, 1)]
            own_corner[side, a["index"], b["index"]] = side_by_side(tiles, b["get_high"])

    def unpack_far(side, b):
        tile = got_lanes[1, side, b["index"]]
        even_lane = even(tile.shape, 1)
        packs[side, 1, 0, 0:ny, tile_of(b)[1]] = pick(
            b["get_high"], jnp.where(even_lane, roll(tile, -1, 1), tile),
            jnp.where(even_lane, tile, roll(tile, 1, 1)))

    def unpack_lanes(side, b):
        got = got_lanes[0, side, b["index"]]
        at, at_pack = tile_of(b)
        high = b["get_high"]
        packs[side, 0, 0, 0:ny, at_pack] = strip(got, 5, high)
        packs[side, 0, 1, 0:ny, at_pack] = strip(got, 6, high)
        for i in (1, 2, 3):
            logs[REACH + (-i, nx - 1 + i)[side], 0:ny, at] = strip(got, i - 1, high)
        for i in (1, 2):
            srcs[DEGREE + (-i, nx - 1 + i)[side], 0:ny, at] = strip(got, i + 2, high)
        for a in ring_y:
            got = got_corner[side, a["index"], b["index"]]
            rows_at = slice(a["place"], a["place"] + ROWS)
            for kind in (0, 1):
                place_rows(side, a, kind, strip(got, kind, high), at)
                packs[side, 0, kind, rows_at, at_pack] = strip(got, kind + 2, high)

    def place_rows(side, a, kind, got, at):
        ref, base = ((logs, REACH), (srcs, DEGREE))[kind]
        rows_at = slice(a["place"], a["place"] + ROWS)
        shifts = ((3, 5), (5, 3)) if kind == 0 else ((2, 6),)
        ref[base + (-1, nx)[side], rows_at, at] = got
        for i, (if_high, if_low) in enumerate(shifts):
            layer = (-2 - i, nx + 1 + i)[side]
            ref[base + layer, rows_at, at] = pick(a["get_high"], roll(got, if_high, 0), roll(got, if_low, 0))

    core = (slice(0, ny), slice(0, nz))
    beside = (slice(0, ny), slice(nz, wide_z))
    rim = (slice(ny, wide_y), slice(0, wide_z))
    scales = (0.125, 1.0)
    whole = (logs, srcs)
    bases = (REACH, DEGREE)

    def own_coarse(kind, at):
        return pair_block(whole[kind], bases[kind], at) * scales[kind]

    def keep_coarse(kind, at, block):
        if kind == 0:
            c_inv_k[(0,) + at] = jnp.exp(-block)
        else:
            c_res[(0,) + at] = block

    def fold_lanes(a):
        return jnp.where(even((a.shape[0], half), 1), a[:, :half], a[:, half:nz])

    log_in.wait()
    block = own_coarse(0, core)
    own_pack[0, :, 0:half] = fold_lanes(block)
    keep_coarse(0, core, block)
    src_in.wait()
    block = own_coarse(1, core)
    flat = fold_lanes(block)
    own_pack[1, :, 0:half] = flat
    keep_coarse(1, core, block)
    upper, lower = flat[:ny // 2], flat[ny // 2:]
    upper_even = even(upper.shape, 0)
    own_far[0] = jnp.where(upper_even, roll(upper, -1, 0), lower)
    own_far[1] = jnp.where(upper_even, upper, roll(lower, 1, 0))
    for side in (0, 1):
        for a in ring_y:
            for kind in (0, 1):
                own_rows[side, a["index"], kind] = pack_rows(side, a, kind, slice(0, nz))

    pl.semaphore_wait(barrier, count)
    start(z_log)
    start(z_src)
    start(y_first)
    start(packs_far)
    start(x_log[1])
    start(rows)
    start(y_log)
    start(y_src)

    arrive(z_log)
    arrive(z_src)
    if ring_z:
        for kind in (0, 1):
            block = own_coarse(kind, beside)
            own_pack[kind, :, half:] = block
            keep_coarse(kind, beside, block)
    for side in (0, 1):
        for b in ring_z:
            pack_corner(side, b)
    start(corner)
    for side in (0, 1):
        for b in ring_z:
            pack_lanes(side, b)
    start(lanes)
    start(x_src[1])
    start(packs_edge)
    start(packs_near)
    start(x_log[3])
    start(x_src[2])

    def clear(ref, *at):
        ref[at] = jnp.zeros_like(ref[at])

    if ring_y and ring_z:
        for side in (0, 1):
            clear(packs, side, 1, 0, slice(ny, wide_y), slice(half, packs.shape[4]))
    for step in (1, 2):
        for _, _, get, side in slots_x(step):
            @pl.when(jnp.logical_not(get))
            def _():
                clear(packs, side, step - 1)
                clear(got_lanes, step - 1, side)
                if step == 2:
                    clear(got_far, side)
                if step == 1:
                    clear(got_rows, side)
                    clear(got_corner, side)
                    for i in range(1, DEGREE + 1):
                        layer = (-i, nx - 1 + i)[side]
                        clear(logs, REACH + layer)
                        clear(srcs, DEGREE + layer)
                    clear(dirs1, DEGREE + layer)
    for a in ring_y:
        if a["get"] is not True:
            @pl.when(jnp.logical_not(a["get"]))
            def _():
                at = slice(a["place"], a["place"] + ROWS)
                for layer in range(nx + 2 * REACH):
                    clear(logs, layer, at)
                for layer in range(nx + 2 * DEGREE):
                    clear(srcs, layer, at)
                for side in (0, 1):
                    for step in (1, 2):
                        clear(packs, side, step - 1, slice(None), at)
                    clear(got_rows, side, a["index"])
                    clear(got_corner, side, a["index"])

    row = iota((wide_y, wide_z), 0)
    lane = iota((wide_y, wide_z), 1)

    def cuts(axis, ring_, length, total, tile):
        n, here = sizes[axis], me[axis]
        if n == 1:
            return [total - 1]
        if n == 2:
            return [jnp.where(here == 0, total - 1, length - 1)]
        return [length + tile - 1, jnp.where(here < n - 1, -1, length - 1),
                jnp.where(here > 0, -1, total - 1)]

    cuts_y = cuts("gy", ring_y, ny, wide_y, ROWS)
    cuts_z = cuts("gz", ring_z, nz, wide_z, LANES)

    def cut(t, index, at):
        for c in at:
            t = jnp.where(index == c, 0.0, t)
        return t

    row_pair, lane_pair = row | 1, lane | 1
    even_row = even((wide_y, wide_z), 0)

    all_rows = slice(0, wide_y)
    own_part = slice(0, ny)
    rim_part = slice(ny, wide_y)

    def fine_k(i, part_=all_rows):
        inv_k[REACH + i, part_] = jnp.exp(-logs[REACH + i, part_])

    def fine_z(i, part_=all_rows):
        mine = inv_k[REACH + i, part_]
        t_z[DEGREE + i, part_] = cut(2.0 * inverse(mine + roll(mine, -1, 1)), lane[part_], cuts_z)

    def fine_y(i, at=slice(None)):
        mine = inv_k[REACH + i, :, at]
        t_y[DEGREE + i, :, at] = cut(2.0 * inverse(mine + roll(mine, -1, 0)), row[:, at], cuts_y)

    def fine_d_core(i):
        y, z = t_y[DEGREE + i, :, 0:nz], t_z[DEGREE + i, own_part]
        x = t_x[(REACH + i,) + core] + t_x[(REACH + i - 1,) + core]
        back = roll(z, 1, 1)
        u_z[DEGREE + i, own_part] = back
        total = (y + roll(y, 1, 0))[:ny] + (z + back)[:, :nz] + x
        inv_d[(DEGREE + i,) + core] = inverse(total + STORAGE)

    flag = {(step, side): get.astype(jnp.float32)
            for step in (1, 2) for _, _, get, side in slots_x(step)}

    def fine_x(i, part_=all_rows):
        t = 2.0 * inverse(inv_k[REACH + i, part_] + inv_k[REACH + i + 1, part_])
        if i == -1:
            t = t * flag[1, 0]
        if i == nx - 1:
            t = t * flag[1, 1]
        t_x[REACH + i, part_] = t

    def fine_d(i):
        y, z = t_y[DEGREE + i], t_z[DEGREE + i]
        back = roll(z, 1, 1)
        u_z[DEGREE + i] = back
        total = (y + roll(y, 1, 0)) + (z + back) + (t_x[REACH + i] + t_x[REACH + i - 1])
        inv_d[DEGREE + i] = inverse(total + STORAGE)

    def coarse_yz(i):
        mine = c_inv_k[i]
        c_t_y[i] = cut(4.0 * inverse(mine + roll(mine, -2, 0)), row_pair, cuts_y)
        c_t_z[i] = cut(4.0 * inverse(mine + roll(mine, -2, 1)), lane_pair, cuts_z)

    def swap(a):
        return jnp.where(even_row, roll(a, -1, 0), roll(a, 1, 0))

    def coarse_x(i):
        if i < 0:
            mine = c_inv_k[0]
            c_t_x[0] = 4.0 * inverse(mine + swap(mine))
            return
        t = 4.0 * inverse(c_inv_k[i] + c_inv_k[i + 1])
        if i in (0, 2):
            step = i // 2 + 1
            t = t * jnp.where(even_row, flag[step, 0], flag[step, 1])
        c_t_x[i + 1] = t

    def coarse_d(i):
        y, z = c_t_y[i], c_t_z[i]
        back = roll(z, 2, 1)
        c_u_z[i] = back
        total = (y + roll(y, 2, 0)) + (z + back) + (c_t_x[i] + c_t_x[i + 1])
        c_inv_d[i] = inverse(total + 8.0 * STORAGE)

    low_in.wait()
    high_in.wait()
    low = jnp.full((1, wide_z), low_ref[0])
    high = jnp.full((1, wide_z), high_ref[0])
    theta = (high + low) * 0.5
    delta = (high - low) * 0.5
    sigma = theta / delta
    rho = 1.0 / sigma
    inv_theta = 1.0 / theta
    keep, gain = [None], [None]
    for _ in range(DEGREE):
        rho_next = 1.0 / (2.0 * sigma - rho)
        keep.append(rho_next * rho)
        gain.append(2.0 * rho_next / delta)
        rho = rho_next

    def fine_first(i, at=(slice(None), slice(None))):
        dirs1[(DEGREE + i,) + at] = (srcs[(DEGREE + i,) + at] * inv_d[(DEGREE + i,) + at]
                                     * inv_theta[:, at[1]])

    def coarse_first(i, at=(slice(None), slice(None))):
        c_dirs1[(i,) + at] = c_res[(i,) + at] * c_inv_d[(i,) + at] * inv_theta[:, at[1]]

    fields = [None, dirs1, dirs2, dirs3]
    c_fields = [None, c_dirs1, c_dirs2, c_dirs3]

    def flows(d, y, z, u, k):
        y = y * (d - roll(d, -k, 0))
        return (y - roll(y, k, 0)) + (z * (d - roll(d, -k, 1)) + u * (d - roll(d, k, 1)))

    def core_flows(d, y, z, u, k):
        dy, dz = d[:, :nz], d[:ny]
        y = y[:, :nz] * (dy - roll(dy, -k, 0))
        z = (z[:ny] * (dz - roll(dz, -k, 1)) + u[:ny] * (dz - roll(dz, k, 1)))[:, :nz]
        return (y - roll(y, k, 0))[:ny] + z

    def fine_turn(turn, i, small=False):
        ref, base = fields[turn], DEGREE + 1 - turn
        at = core if small else (all_rows, slice(0, wide_z))
        d = ref[base + i]
        flow = (core_flows if small else flows)(d, t_y[DEGREE + i], t_z[DEGREE + i], u_z[DEGREE + i], 1)
        d = d[at]
        r = (srcs if turn == 1 else res)[(DEGREE + i,) + at] - STORAGE * d - flow
        r = r - t_x[(REACH + i,) + at] * (d - ref[(base + i + 1,) + at])
        r = r - t_x[(REACH + i - 1,) + at] * (d - ref[(base + i - 1,) + at])
        later = keep[turn][:, at[1]] * d + gain[turn][:, at[1]] * (r * inv_d[(DEGREE + i,) + at])
        if turn < DEGREE:
            res[(DEGREE + i,) + at] = r
            fields[turn + 1][(base - 1 + i,) + at] = later
        else:
            part[i] = dirs1[(DEGREE + i,) + at] + dirs2[(DEGREE - 1 + i,) + at] + d
            last[i] = later

    def coarse_turn(turn, i, small=False):
        ref = c_fields[turn]
        at = core if small else (all_rows, slice(0, wide_z))
        d = ref[i]
        flow = (core_flows if small else flows)(d, c_t_y[i], c_t_z[i], c_u_z[i], 2)
        d = d[at]
        if i > 0:
            inner_side = ref[(i - 1,) + at]
        else:
            inner_side = jnp.where(even(d.shape, 0), roll(d, -1, 0), roll(d, 1, 0))
        r = c_res[(i,) + at] - 8.0 * STORAGE * d - flow
        r = r - c_t_x[(i + 1,) + at] * (d - ref[(i + 1,) + at])
        r = r - c_t_x[(i,) + at] * (d - inner_side)
        later = keep[turn][:, at[1]] * d + gain[turn][:, at[1]] * (r * c_inv_d[(i,) + at])
        if turn < DEGREE:
            c_res[(i,) + at] = r
            c_fields[turn + 1][(i,) + at] = later
        else:
            total = c_dirs1[(i,) + at] + c_dirs2[(i,) + at] + d + later
            top = even((ny, nz), 0)
            coarse[0] = jnp.where(top, total, roll(total, 1, 0))
            coarse[1] = jnp.where(top, roll(total, -1, 0), total)

    def unpack_rows(side, kind):
        for a in ring_y:
            place_rows(side, a, kind, got_rows[side, a["index"], kind], slice(0, nz))

    def spread(step, kind, near):
        left, right = packs[0, step - 1, kind], packs[1, step - 1, kind]
        top = even(left.shape, 0)
        if near:
            a = jnp.where(top, roll(left, -1, 0), roll(right, 1, 0))
        else:
            a = jnp.where(top, left, right)
        return jnp.concatenate([spread_lanes(a[:, :half]), a[:, half:]], axis=1)

    def spread_lanes(main):
        even_lane = even(main.shape, 1)
        return jnp.concatenate([jnp.where(even_lane, main, roll(main, 1, 1)),
                                jnp.where(even_lane, roll(main, -1, 1), main)], axis=1)

    def spread_far():
        left, right = got_far[0], got_far[1]
        first = even(left.shape, 0)
        upper = jnp.where(first, left, roll(right, 1, 0))
        lower = jnp.where(first, roll(left, -1, 0), right)
        return spread_lanes(jnp.concatenate([upper, lower], axis=0))

    def halo(i):
        return (-i, nx - 1 + i)

    mine = range(nx)
    inner = range(1, nx - 1)
    ends = (0, nx - 1)

    for i in mine:
        fine_k(i, own_part)
    for i in mine:
        fine_z(i, own_part)
    for i in range(nx - 1):
        fine_x(i, own_part)
    arrive(y_first)
    for i in inner:
        if ring_y:
            inv_k[REACH + i, rim_part, 0:nz] = jnp.exp(-logs[REACH + i, rim_part, 0:nz])
        fine_y(i, slice(0, nz))
        fine_d_core(i)
        fine_first(i, core)
    start(x_dir)
    arrive(packs_far)
    start(pass_y)
    start(pass_z)
    arrive(y_log)
    if ring_y:
        for i in mine:
            fine_k(i, rim_part)
        for i in mine:
            fine_z(i, rim_part)
        for i in range(nx - 1):
            fine_x(i, rim_part)
        keep_coarse(0, rim, own_coarse(0, rim))
    for i in mine:
        fine_y(i)
    for i in inner:
        fine_d(i)
    arrive(y_src)
    for i in inner:
        if ring_z:
            fine_first(i, beside)
        if ring_y:
            fine_first(i, rim)
    if ring_y:
        keep_coarse(1, rim, own_coarse(1, rim))
    coarse_yz(0)
    coarse_x(-1)

    arrive(x_log[1])
    arrive(rows)
    arrive(lanes)
    arrive(corner)
    for side in (0, 1):
        unpack_rows(side, 0)
        unpack_rows(side, 1)
        for b in ring_z:
            unpack_lanes(side, b)
    for i in halo(1) + halo(2):
        fine_k(i)
    for i in halo(1):
        fine_y(i)
        fine_z(i)
    for i in (-2, -1, nx - 1, nx):
        fine_x(i)
    for i in ends + halo(1):
        fine_d(i)
    for i in ends:
        fine_first(i)
    for i in inner:
        fine_turn(1, i)
    arrive(x_src[1])
    for i in halo(1):
        fine_first(i)
    for i in ends:
        fine_turn(1, i)
    for i in inner:
        fine_turn(2, i)

    arrive(packs_near)
    arrive(packs_edge)
    c_inv_k[1] = jnp.exp(-spread(1, 0, True))
    c_inv_k[2] = jnp.exp(-spread(1, 0, False))
    c_res[1] = spread(1, 1, True)
    c_res[2] = spread(1, 1, False)
    coarse_yz(1)
    coarse_x(0)
    coarse_x(1)
    coarse_yz(2)
    for i in (0, 1):
        coarse_d(i)
        coarse_first(i)
    coarse_turn(1, 0)

    arrive(pass_z)
    for side in (0, 1):
        for b in ring_z:
            unpack_far(side, b)
    arrive(pass_y)
    c_inv_k[3] = jnp.exp(-spread(2, 0, True))
    c_inv_k[4] = jnp.exp(-spread(2, 0, False))
    c_res[(3,) + core] = spread_far()
    coarse_yz(3)
    coarse_x(2)
    coarse_x(3)
    for i in (2, 3):
        coarse_d(i)
    coarse_first(2)
    coarse_first(3, core)
    coarse_turn(1, 1)
    coarse_turn(1, 2, True)
    coarse_turn(2, 0)
    coarse_turn(2, 1, True)
    coarse_turn(3, 0, True)

    arrive(x_log[3])
    for i in halo(3):
        fine_k(i)
    for i in halo(2):
        fine_y(i)
        fine_z(i)
    for i in (-3, nx + 1):
        fine_x(i)
    for i in halo(2):
        fine_d(i)
    arrive(x_src[2])
    for i in halo(2):
        fine_first(i)
    for i in halo(1):
        fine_turn(1, i)
    for i in ends:
        fine_turn(2, i)
    for i in inner:
        fine_turn(3, i, True)

    for group in ([z_log, z_src, y_first, y_log, y_src, rows, corner, x_dir, packs_near, packs_edge, packs_far, pass_y, pass_z, lanes]
                  + list(x_log.values()) + list(x_src.values())):
        drain(group)

    arrive(x_dir)
    for i in halo(2):
        fine_turn(1, i, True)
    for i in halo(1):
        fine_turn(2, i, True)
    for i in ends:
        fine_turn(3, i, True)


def shards(sizes, log_perm, source, low_bound, high_bound):
    nx, ny, nz = log_perm.shape
    wide_y = ny + ROWS * sides(sizes["gy"])
    wide_z = nz + LANES * sides(sizes["gz"])
    half = nz // 2
    f32 = lambda *shape: pltpu.VMEM(shape, jnp.float32)
    fine = lambda reach: f32(nx + 2 * reach, wide_y, wide_z)
    pairs = lambda n: f32(n, wide_y, wide_z)
    log_perm = pltpu.with_memory_space_constraint(log_perm, pltpu.HBM)
    source = pltpu.with_memory_space_constraint(source, pltpu.HBM)
    hbm = pl.BlockSpec(memory_space=pltpu.HBM)
    vmem = pl.BlockSpec(memory_space=pltpu.VMEM)
    whole = jax.ShapeDtypeStruct((nx, ny, nz), jnp.float32)
    messages = 96
    part, last, coarse = pl.pallas_call(
        functools.partial(kernel, sizes),
        out_shape=(whole, whole, jax.ShapeDtypeStruct((nx // 2, ny, nz), jnp.float32)),
        in_specs=[hbm] * 4,
        out_specs=(vmem,) * 3,
        scratch_shapes=[
            pltpu.SMEM((1,), jnp.float32),
            pltpu.SMEM((1,), jnp.float32),
            fine(REACH), fine(DEGREE),
            f32(2, 2, 2, wide_y, half + wide_z - nz),
            f32(2, ny, half + wide_z - nz),
            f32(2, max(1, sides(sizes["gy"])), 2, ROWS, nz),
            f32(2, max(1, sides(sizes["gy"])), 2, ROWS, nz),
            f32(2, max(1, sides(sizes["gz"])), ny, LANES),
            f32(2, 2, max(1, sides(sizes["gz"])), ny, LANES),
            f32(2, ny // 2, half),
            f32(2, ny // 2, half),
            f32(2, max(1, sides(sizes["gy"])), max(1, sides(sizes["gz"])), ROWS, LANES),
            f32(2, max(1, sides(sizes["gy"])), max(1, sides(sizes["gz"])), ROWS, LANES),
            fine(REACH), fine(REACH), fine(DEGREE), fine(DEGREE), fine(DEGREE), fine(DEGREE), fine(DEGREE),
            fine(DEGREE), fine(DEGREE - 1), fine(DEGREE - 2),
            pairs(5), pairs(5), pairs(4), pairs(4), pairs(4), pairs(4), pairs(4), pairs(4), pairs(3), pairs(2),
            pltpu.SemaphoreType.DMA((4,)),
            pltpu.SemaphoreType.DMA((messages,)),
            pltpu.SemaphoreType.DMA((messages,)),
        ],
        compiler_params=pltpu.CompilerParams(
            collective_id=0, has_side_effects=True, vmem_limit_bytes=24 * 2**20),
    )(low_bound, high_bound, log_perm, source)
    fine_pressure = part + last
    return fine_pressure, fine_pressure - jnp.repeat(coarse, 2, axis=0)


def solution(mesh):
    sizes = {axis: mesh.shape[axis] for axis in AXES}
    spec = P(("groups", "gx"), "gy", "gz")
    return jax.shard_map(
        functools.partial(shards, sizes),
        mesh=mesh,
        in_specs=(spec, spec, P(), P()),
        out_specs=(spec, spec),
        check_vma=False,
    )
```

```python
import functools

import jax
import jax.numpy as jnp
from jax import lax
from jax.experimental import pallas as pl
from jax.experimental.pallas import tpu as pltpu
from jax.sharding import PartitionSpec as P

DEGREE = 3
REACH = DEGREE
STORAGE = 0.1
LANES = 128
ROWS = 8
MESH = pl.DeviceIdType.MESH
AXES = ("gx", "gy", "gz")


def roll(a, shift, axis):
    return pltpu.roll(a, shift % a.shape[axis], axis)


def iota(shape, axis):
    return lax.broadcasted_iota(jnp.int32, shape, axis)


def even(shape, axis):
    return iota(shape, axis) % 2 == 0


def pair_sum(a, axis):
    return a + jnp.where(even(a.shape, axis), roll(a, -1, axis), roll(a, 1, axis))


def pooled(a, b):
    return pair_sum(pair_sum(a + b, 0), 1)


def inverse(a):
    r = pl.reciprocal(a, approx=True)
    return r * (2.0 - a * r)


def pick(condition, a, b):
    if isinstance(condition, bool):
        return a if condition else b
    return jnp.where(condition, a, b)


def both(a, b):
    if a is True:
        return b
    return a if b is True else jnp.logical_and(a, b)


def when(condition, act):
    if condition is True:
        act()
    else:
        pl.when(condition)(act)


def sides(size):
    return min(size - 1, 2)


def kernel(sizes, low_hbm, high_hbm, log_hbm, src_hbm, part, last, coarse,
           low_ref, high_ref, logs, srcs, packs, own_pack, own_rows, got_rows, own_lanes, got_lanes,
           own_far, got_far, own_corner, got_corner,
           inv_k, t_x, t_y, t_z, u_z, inv_d, res, dirs1, dirs2, dirs3,
           c_inv_k, c_t_x, c_t_y, c_t_z, c_u_z, c_inv_d, c_res, c_dirs1, c_dirs2, c_dirs3,
           io_sem, send_sem, recv_sem):
    nx, ny, nz = log_hbm.shape
    half = nz // 2
    wide_y, wide_z = logs.shape[1:]
    me = {axis: lax.axis_index(axis) for axis in AXES}
    count_x = sizes["gx"]
    x = me["gx"]

    def slots_x(step):
        return [({"gx": x + step}, x + step < count_x, x >= step, 0),
                ({"gx": x - step}, x >= step, x + step < count_x, 1)]

    def ring(axis, length, tile):
        n, here = sizes[axis], me[axis]
        if n == 1:
            return []
        if n == 2:
            start = pl.multiple_of((1 - here) * (length - tile), tile)
            return [dict(to={axis: 1 - here}, send=True, get=True, start=start, place=length,
                         send_high=here == 0, get_high=here == 1, index=0)]
        return [dict(to={axis: here - 1}, send=here > 0, get=here < n - 1, start=0, place=length,
                     send_high=False, get_high=False, index=0),
                dict(to={axis: here + 1}, send=here < n - 1, get=here > 0, start=length - tile,
                     place=length + tile, send_high=True, get_high=True, index=1)]

    ring_y = ring("gy", ny, ROWS)
    ring_z = ring("gz", nz, LANES)

    def packed_start(b):
        if isinstance(b["start"], int):
            return b["start"] * (half - LANES) // (nz - LANES)
        return pl.multiple_of((1 - me["gz"]) * (half - LANES), LANES)

    used = []

    class Message:
        def __init__(self, to, send, get, source, target):
            index = len(used)
            used.append(index)
            self.send, self.get = send, get
            self.copy = lambda: pltpu.make_async_remote_copy(
                src_ref=source, dst_ref=target, send_sem=send_sem.at[index],
                recv_sem=recv_sem.at[index], device_id=to, device_id_type=MESH)

    def start(messages):
        for m in messages:
            when(m.send, lambda: m.copy().start())

    def arrive(messages):
        for m in messages:
            when(m.get, lambda: m.copy().wait_recv())

    def drain(messages):
        for m in messages:
            when(m.send, lambda: m.copy().wait_send())

    partners = [({**to, **a["to"]}, both(send, a["send"]))
                for to, send, _, _ in slots_x(1) for a in ring_y]
    partners += [(to, send) for step in (2, 1) for to, send, _, _ in slots_x(step)]
    partners += [({**a["to"], **b["to"]}, both(a["send"], b["send"])) for a in ring_y for b in ring_z]
    partners += [(r["to"], r["send"]) for r in ring_y + ring_z]
    barrier = pltpu.get_barrier_semaphore()
    count = 0
    for to, send in partners:
        when(send, lambda: pl.semaphore_signal(barrier, inc=1, device_id=to, device_id_type=MESH))
        count = count + (1 if send is True else send.astype(jnp.int32))

    own = pl.ds(REACH, nx)
    own_s = pl.ds(DEGREE, nx)
    log_in = pltpu.make_async_copy(log_hbm, logs.at[own, 0:ny, 0:nz], io_sem.at[0])
    src_in = pltpu.make_async_copy(src_hbm, srcs.at[own_s, 0:ny, 0:nz], io_sem.at[1])
    low_in = pltpu.make_async_copy(low_hbm, low_ref, io_sem.at[2])
    high_in = pltpu.make_async_copy(high_hbm, high_ref, io_sem.at[3])
    for copy in (log_in, src_in, low_in, high_in):
        copy.start()

    def plane_z(hbm, ref, layers):
        return [Message(b["to"], b["send"], b["get"],
                        ref.at[layers, 0:ny, pl.ds(b["start"], LANES)],
                        ref.at[layers, 0:ny, pl.ds(b["place"], LANES)]) for b in ring_z]

    def plane_y(hbm, ref, base, first, count_):
        return [Message(a["to"], a["send"], a["get"],
                        ref.at[pl.ds(base + first, count_), pl.ds(a["start"], ROWS), 0:nz],
                        ref.at[pl.ds(base + first, count_), pl.ds(a["place"], ROWS), 0:nz])
                for a in ring_y]

    def plane_yz(hbm, ref, layers):
        return [Message({**a["to"], **b["to"]}, both(a["send"], b["send"]), both(a["get"], b["get"]),
                        ref.at[layers, pl.ds(a["start"], ROWS), pl.ds(b["start"], LANES)],
                        ref.at[layers, pl.ds(a["place"], ROWS), pl.ds(b["place"], LANES)])
                for a in ring_y for b in ring_z]

    def span(side, first, last_, base):
        many = last_ - first + 1
        if side == 0:
            return pl.ds(base + nx - last_, many), pl.ds(base - last_, many)
        return pl.ds(base + first - 1, many), pl.ds(base + nx + first - 1, many)

    def along(hbm, ref, base, first, last_):
        out = []
        for to, send, get, side in slots_x(1):
            mine, theirs = span(side, first, last_, base)
            out.append(Message(to, send, get, ref.at[mine, 0:ny, 0:nz], ref.at[theirs, 0:ny, 0:nz]))
        return out

    z_log = plane_z(log_hbm, logs, own)
    z_src = plane_z(src_hbm, srcs, own_s)
    y_first = plane_y(log_hbm, logs, REACH, 1, nx - 2)
    y_log = (plane_y(log_hbm, logs, REACH, 0, 1) + plane_y(log_hbm, logs, REACH, nx - 1, 1)
             + plane_yz(log_hbm, logs, own))
    y_src = plane_y(src_hbm, srcs, DEGREE, 0, nx) + plane_yz(src_hbm, srcs, own_s)
    x_log = {1: along(log_hbm, logs, REACH, 1, 2), 3: along(log_hbm, logs, REACH, 3, 3)}
    x_src = {i: along(src_hbm, srcs, DEGREE, i, i) for i in (1, 2)}
    x_dir = [Message(to, send, get, dirs1.at[DEGREE + (nx - DEGREE, DEGREE - 1)[side], 0:ny, 0:nz],
                     dirs1.at[DEGREE + (-DEGREE, nx - 1 + DEGREE)[side], 0:ny, 0:nz])
             for to, send, get, side in slots_x(1)]
    rows = [Message({**to, **a["to"]}, both(send, a["send"]), both(get, a["get"]),
                    own_rows.at[side, a["index"]], got_rows.at[side, a["index"]])
            for to, send, get, side in slots_x(1) for a in ring_y]
    lanes = [Message(to, both(send, b["get"]), both(get, b["get"]),
                     own_lanes.at[side, b["index"]], got_lanes.at[0, side, b["index"]])
             for to, send, get, side in slots_x(1) for b in ring_z]
    corner = [Message({**to, **a["to"]}, both(send, both(a["send"], b["get"])), both(get, both(a["get"], b["get"])),
                      own_corner.at[side, a["index"], b["index"]], got_corner.at[side, a["index"], b["index"]])
              for to, send, get, side in slots_x(1) for a in ring_y for b in ring_z]
    packs_near = [Message(to, send, get, own_pack.at[:, :, 0:half],
                          packs.at[side, 0, :, 0:ny, 0:half]) for to, send, get, side in slots_x(1)]
    packs_edge = [Message({**to, **a["to"]}, both(send, a["send"]), both(get, a["get"]),
                          own_pack.at[:, pl.ds(a["start"], ROWS), 0:half],
                          packs.at[side, 0, :, pl.ds(a["place"], ROWS), 0:half])
                  for to, send, get, side in slots_x(1) for a in ring_y]
    packs_far = [Message(to, send, get, own_pack.at[0, :, 0:half],
                         packs.at[side, 1, 0, 0:ny, 0:half]) for to, send, get, side in slots_x(2)]
    packs_far += [Message(to, send, get, own_far.at[side], got_far.at[side])
                  for to, send, get, side in slots_x(2)]
    far = [get for _, _, get, _ in slots_x(2)]
    pass_y = [Message(a["to"], both(a["send"], far[side]), both(a["get"], far[side]),
                      packs.at[side, 1, 0, pl.ds(a["start"], ROWS), 0:half],
                      packs.at[side, 1, 0, pl.ds(a["place"], ROWS), 0:half])
              for side in (0, 1) for a in ring_y]
    pass_z = [Message(b["to"], both(b["send"], far[side]), both(b["get"], far[side]),
                      packs.at[side, 1, 0, 0:ny, pl.ds(packed_start(b), LANES)],
                      got_lanes.at[1, side, b["index"]])
              for side in (0, 1) for b in ring_z]

    def pair_block(ref, base, at):
        a = pooled(ref[(base,) + at], ref[(base + 1,) + at])
        b = pooled(ref[(base + 2,) + at], ref[(base + 3,) + at])
        return jnp.where(even(a.shape, 0), a, b)

    tile_lane = iota((ny, LANES), 1)

    def pack_rows(side, a, kind, at):
        ref, base = ((logs, REACH), (srcs, DEGREE))[kind]

        def edge(i):
            layer = (nx - i, i - 1)[side]
            return ref[base + layer, pl.ds(a["start"], ROWS), at]
        high = a["send_high"]
        one, two = edge(1), edge(2)
        spot = iota(one.shape, 0)
        if kind == 0:
            three = edge(3)
            two = pick(high, roll(two, 5, 0), roll(two, 3, 0))
            three = pick(high, roll(three, 3, 0), roll(three, 5, 0))
            first = pick(high, spot - 5, 2 - spot) >= 0
            second = (spot == 3) | (spot == 4)
            return jnp.where(first, one, jnp.where(second, two, three))
        two = pick(high, roll(two, 6, 0), roll(two, 2, 0))
        first = pick(high, spot - 6, 1 - spot) >= 0
        return jnp.where(first, one, two)

    STRIP = 8

    def side_by_side(tiles, high):
        out = None
        for k, a in enumerate(tiles):
            a = pltpu.roll(a, STRIP * k + pick(high, STRIP, 0), 1)
            out = a if out is None else jnp.where(tile_lane[:a.shape[0]] >= STRIP * k, a, out)
        return out

    def strip(a, k, high):
        return pltpu.roll(a, LANES - STRIP * k - pick(high, STRIP, 0), 1)

    def tile_of(b):
        return (slice(b["place"], b["place"] + LANES),
                slice(half + b["place"] - nz, half + b["place"] - nz + LANES))

    def pack_lanes(side, b):
        at, at_pack = tile_of(b)
        tiles = [logs[REACH + (nx - i, i - 1)[side], 0:ny, at] for i in (1, 2, 3)]
        tiles += [srcs[DEGREE + (nx - i, i - 1)[side], 0:ny, at] for i in (1, 2)]
        tiles += [own_pack[kind, :, at_pack] for kind in (0, 1)]
        own_lanes[side, b["index"]] = side_by_side(tiles, b["get_high"])

    def pack_corner(side, b):
        at, at_pack = tile_of(b)
        for a in ring_y:
            tiles = [pack_rows(side, a, kind, at) for kind in (0, 1)]
            tiles += [own_pack[kind, pl.ds(a["start"], ROWS), at_pack] for kind in (0, 1)]
            own_corner[side, a["index"], b["index"]] = side_by_side(tiles, b["get_high"])

    def unpack_far(side, b):
        tile = got_lanes[1, side, b["index"]]
        even_lane = even(tile.shape, 1)
        packs[side, 1, 0, 0:ny, tile_of(b)[1]] = pick(
            b["get_high"], jnp.where(even_lane, roll(tile, -1, 1), tile),
            jnp.where(even_lane, tile, roll(tile, 1, 1)))

    def unpack_lanes(side, b):
        got = got_lanes[0, side, b["index"]]
        at, at_pack = tile_of(b)
        high = b["get_high"]
        packs[side, 0, 0, 0:ny, at_pack] = strip(got, 5, high)
        packs[side, 0, 1, 0:ny, at_pack] = strip(got, 6, high)
        for i in (1, 2, 3):
            logs[REACH + (-i, nx - 1 + i)[side], 0:ny, at] = strip(got, i - 1, high)
        for i in (1, 2):
            srcs[DEGREE + (-i, nx - 1 + i)[side], 0:ny, at] = strip(got, i + 2, high)
        for a in ring_y:
            got = got_corner[side, a["index"], b["index"]]
            rows_at = slice(a["place"], a["place"] + ROWS)
            for kind in (0, 1):
                place_rows(side, a, kind, strip(got, kind, high), at)
                packs[side, 0, kind, rows_at, at_pack] = strip(got, kind + 2, high)

    def place_rows(side, a, kind, got, at):
        ref, base = ((logs, REACH), (srcs, DEGREE))[kind]
        rows_at = slice(a["place"], a["place"] + ROWS)
        shifts = ((3, 5), (5, 3)) if kind == 0 else ((2, 6),)
        ref[base + (-1, nx)[side], rows_at, at] = got
        for i, (if_high, if_low) in enumerate(shifts):
            layer = (-2 - i, nx + 1 + i)[side]
            ref[base + layer, rows_at, at] = pick(a["get_high"], roll(got, if_high, 0), roll(got, if_low, 0))

    core = (slice(0, ny), slice(0, nz))
    beside = (slice(0, ny), slice(nz, wide_z))
    rim = (slice(ny, wide_y), slice(0, wide_z))
    scales = (0.125, 1.0)
    whole = (logs, srcs)
    bases = (REACH, DEGREE)

    def own_coarse(kind, at):
        return pair_block(whole[kind], bases[kind], at) * scales[kind]

    def keep_coarse(kind, at, block):
        if kind == 0:
            c_inv_k[(0,) + at] = jnp.exp(-block)
        else:
            c_res[(0,) + at] = block

    def fold_lanes(a):
        return jnp.where(even((a.shape[0], half), 1), a[:, :half], a[:, half:nz])

    log_in.wait()
    block = own_coarse(0, core)
    own_pack[0, :, 0:half] = fold_lanes(block)
    keep_coarse(0, core, block)
    src_in.wait()
    block = own_coarse(1, core)
    flat = fold_lanes(block)
    own_pack[1, :, 0:half] = flat
    keep_coarse(1, core, block)
    upper, lower = flat[:ny // 2], flat[ny // 2:]
    upper_even = even(upper.shape, 0)
    own_far[0] = jnp.where(upper_even, roll(upper, -1, 0), lower)
    own_far[1] = jnp.where(upper_even, upper, roll(lower, 1, 0))
    for side in (0, 1):
        for a in ring_y:
            for kind in (0, 1):
                own_rows[side, a["index"], kind] = pack_rows(side, a, kind, slice(0, nz))

    pl.semaphore_wait(barrier, count)
    start(z_log)
    start(z_src)
    start(y_first)
    start(packs_far)
    start(x_log[1])
    start(rows)
    start(y_log)
    start(y_src)

    for i in range(nx):
        inv_k[(REACH + i,) + core] = jnp.exp(-logs[(REACH + i,) + core])
    for i in range(nx - 1):
        t_x[(REACH + i,) + core] = 2.0 * inverse(inv_k[(REACH + i,) + core] + inv_k[(REACH + i + 1,) + core])
    arrive(z_log)
    arrive(z_src)
    if ring_z:
        for kind in (0, 1):
            block = own_coarse(kind, beside)
            own_pack[kind, :, half:] = block
            keep_coarse(kind, beside, block)
    for side in (0, 1):
        for b in ring_z:
            pack_corner(side, b)
    start(corner)
    for side in (0, 1):
        for b in ring_z:
            pack_lanes(side, b)
    start(lanes)
    start(x_src[1])
    start(packs_edge)
    start(packs_near)
    start(x_log[3])
    start(x_src[2])

    def clear(ref, *at):
        ref[at] = jnp.zeros_like(ref[at])

    if ring_y and ring_z:
        for side in (0, 1):
            clear(packs, side, 1, 0, slice(ny, wide_y), slice(half, packs.shape[4]))
    for step in (1, 2):
        for _, _, get, side in slots_x(step):
            @pl.when(jnp.logical_not(get))
            def _():
                clear(packs, side, step - 1)
                clear(got_lanes, step - 1, side)
                if step == 2:
                    clear(got_far, side)
                if step == 1:
                    clear(got_rows, side)
                    clear(got_corner, side)
                    for i in range(1, DEGREE + 1):
                        layer = (-i, nx - 1 + i)[side]
                        clear(logs, REACH + layer)
                        clear(srcs, DEGREE + layer)
                    clear(dirs1, DEGREE + layer)
    for a in ring_y:
        if a["get"] is not True:
            @pl.when(jnp.logical_not(a["get"]))
            def _():
                at = slice(a["place"], a["place"] + ROWS)
                for layer in range(nx + 2 * REACH):
                    clear(logs, layer, at)
                for layer in range(nx + 2 * DEGREE):
                    clear(srcs, layer, at)
                for side in (0, 1):
                    for step in (1, 2):
                        clear(packs, side, step - 1, slice(None), at)
                    clear(got_rows, side, a["index"])
                    clear(got_corner, side, a["index"])

    row = iota((wide_y, wide_z), 0)
    lane = iota((wide_y, wide_z), 1)

    def cuts(axis, ring_, length, total, tile):
        n, here = sizes[axis], me[axis]
        if n == 1:
            return [total - 1]
        if n == 2:
            return [jnp.where(here == 0, total - 1, length - 1)]
        return [length + tile - 1, jnp.where(here < n - 1, -1, length - 1),
                jnp.where(here > 0, -1, total - 1)]

    cuts_y = cuts("gy", ring_y, ny, wide_y, ROWS)
    cuts_z = cuts("gz", ring_z, nz, wide_z, LANES)

    def cut(t, index, at):
        for c in at:
            t = jnp.where(index == c, 0.0, t)
        return t

    row_pair, lane_pair = row | 1, lane | 1
    even_row = even((wide_y, wide_z), 0)

    all_rows = slice(0, wide_y)
    own_part = slice(0, ny)
    rim_part = slice(ny, wide_y)

    def fine_k(i, part_=all_rows):
        inv_k[REACH + i, part_] = jnp.exp(-logs[REACH + i, part_])

    def fine_z(i, part_=all_rows):
        mine = inv_k[REACH + i, part_]
        t_z[DEGREE + i, part_] = cut(2.0 * inverse(mine + roll(mine, -1, 1)), lane[part_], cuts_z)

    def fine_y(i, at=slice(None)):
        mine = inv_k[REACH + i, :, at]
        t_y[DEGREE + i, :, at] = cut(2.0 * inverse(mine + roll(mine, -1, 0)), row[:, at], cuts_y)

    def fine_d_core(i):
        y, z = t_y[DEGREE + i, :, 0:nz], t_z[DEGREE + i, own_part]
        x = t_x[(REACH + i,) + core] + t_x[(REACH + i - 1,) + core]
        back = roll(z, 1, 1)
        u_z[DEGREE + i, own_part] = back
        total = (y + roll(y, 1, 0))[:ny] + (z + back)[:, :nz] + x
        inv_d[(DEGREE + i,) + core] = inverse(total + STORAGE)

    flag = {(step, side): get.astype(jnp.float32)
            for step in (1, 2) for _, _, get, side in slots_x(step)}

    def fine_x(i, part_=all_rows):
        t = 2.0 * inverse(inv_k[REACH + i, part_] + inv_k[REACH + i + 1, part_])
        if i == -1:
            t = t * flag[1, 0]
        if i == nx - 1:
            t = t * flag[1, 1]
        t_x[REACH + i, part_] = t

    def fine_d(i):
        y, z = t_y[DEGREE + i], t_z[DEGREE + i]
        back = roll(z, 1, 1)
        u_z[DEGREE + i] = back
        total = (y + roll(y, 1, 0)) + (z + back) + (t_x[REACH + i] + t_x[REACH + i - 1])
        inv_d[DEGREE + i] = inverse(total + STORAGE)

    def coarse_yz(i):
        mine = c_inv_k[i]
        c_t_y[i] = cut(4.0 * inverse(mine + roll(mine, -2, 0)), row_pair, cuts_y)
        c_t_z[i] = cut(4.0 * inverse(mine + roll(mine, -2, 1)), lane_pair, cuts_z)

    def swap(a):
        return jnp.where(even_row, roll(a, -1, 0), roll(a, 1, 0))

    def coarse_x(i):
        if i < 0:
            mine = c_inv_k[0]
            c_t_x[0] = 4.0 * inverse(mine + swap(mine))
            return
        t = 4.0 * inverse(c_inv_k[i] + c_inv_k[i + 1])
        if i in (0, 2):
            step = i // 2 + 1
            t = t * jnp.where(even_row, flag[step, 0], flag[step, 1])
        c_t_x[i + 1] = t

    def coarse_d(i):
        y, z = c_t_y[i], c_t_z[i]
        back = roll(z, 2, 1)
        c_u_z[i] = back
        total = (y + roll(y, 2, 0)) + (z + back) + (c_t_x[i] + c_t_x[i + 1])
        c_inv_d[i] = inverse(total + 8.0 * STORAGE)

    low_in.wait()
    high_in.wait()
    low = jnp.full((1, wide_z), low_ref[0])
    high = jnp.full((1, wide_z), high_ref[0])
    theta = (high + low) * 0.5
    delta = (high - low) * 0.5
    sigma = theta / delta
    rho = 1.0 / sigma
    inv_theta = 1.0 / theta
    keep, gain = [None], [None]
    for _ in range(DEGREE):
        rho_next = 1.0 / (2.0 * sigma - rho)
        keep.append(rho_next * rho)
        gain.append(2.0 * rho_next / delta)
        rho = rho_next

    def fine_first(i, at=(slice(None), slice(None))):
        dirs1[(DEGREE + i,) + at] = (srcs[(DEGREE + i,) + at] * inv_d[(DEGREE + i,) + at]
                                     * inv_theta[:, at[1]])

    def coarse_first(i, at=(slice(None), slice(None))):
        c_dirs1[(i,) + at] = c_res[(i,) + at] * c_inv_d[(i,) + at] * inv_theta[:, at[1]]

    fields = [None, dirs1, dirs2, dirs3]
    c_fields = [None, c_dirs1, c_dirs2, c_dirs3]

    def flows(d, y, z, u, k):
        y = y * (d - roll(d, -k, 0))
        return (y - roll(y, k, 0)) + (z * (d - roll(d, -k, 1)) + u * (d - roll(d, k, 1)))

    def core_flows(d, y, z, u, k):
        dy, dz = d[:, :nz], d[:ny]
        y = y[:, :nz] * (dy - roll(dy, -k, 0))
        z = (z[:ny] * (dz - roll(dz, -k, 1)) + u[:ny] * (dz - roll(dz, k, 1)))[:, :nz]
        return (y - roll(y, k, 0))[:ny] + z

    def fine_turn(turn, i, small=False):
        ref, base = fields[turn], DEGREE + 1 - turn
        at = core if small else (all_rows, slice(0, wide_z))
        d = ref[base + i]
        flow = (core_flows if small else flows)(d, t_y[DEGREE + i], t_z[DEGREE + i], u_z[DEGREE + i], 1)
        d = d[at]
        r = (srcs if turn == 1 else res)[(DEGREE + i,) + at] - STORAGE * d - flow
        r = r - t_x[(REACH + i,) + at] * (d - ref[(base + i + 1,) + at])
        r = r - t_x[(REACH + i - 1,) + at] * (d - ref[(base + i - 1,) + at])
        later = keep[turn][:, at[1]] * d + gain[turn][:, at[1]] * (r * inv_d[(DEGREE + i,) + at])
        if turn < DEGREE:
            res[(DEGREE + i,) + at] = r
            fields[turn + 1][(base - 1 + i,) + at] = later
        else:
            part[i] = dirs1[(DEGREE + i,) + at] + dirs2[(DEGREE - 1 + i,) + at] + d
            last[i] = later

    def coarse_turn(turn, i, small=False):
        ref = c_fields[turn]
        at = core if small else (all_rows, slice(0, wide_z))
        d = ref[i]
        flow = (core_flows if small else flows)(d, c_t_y[i], c_t_z[i], c_u_z[i], 2)
        d = d[at]
        if i > 0:
            inner_side = ref[(i - 1,) + at]
        else:
            inner_side = jnp.where(even(d.shape, 0), roll(d, -1, 0), roll(d, 1, 0))
        r = c_res[(i,) + at] - 8.0 * STORAGE * d - flow
        r = r - c_t_x[(i + 1,) + at] * (d - ref[(i + 1,) + at])
        r = r - c_t_x[(i,) + at] * (d - inner_side)
        later = keep[turn][:, at[1]] * d + gain[turn][:, at[1]] * (r * c_inv_d[(i,) + at])
        if turn < DEGREE:
            c_res[(i,) + at] = r
            c_fields[turn + 1][(i,) + at] = later
        else:
            total = c_dirs1[(i,) + at] + c_dirs2[(i,) + at] + d + later
            top = even((ny, nz), 0)
            coarse[0] = jnp.where(top, total, roll(total, 1, 0))
            coarse[1] = jnp.where(top, roll(total, -1, 0), total)

    def unpack_rows(side, kind):
        for a in ring_y:
            place_rows(side, a, kind, got_rows[side, a["index"], kind], slice(0, nz))

    def spread(step, kind, near):
        left, right = packs[0, step - 1, kind], packs[1, step - 1, kind]
        top = even(left.shape, 0)
        if near:
            a = jnp.where(top, roll(left, -1, 0), roll(right, 1, 0))
        else:
            a = jnp.where(top, left, right)
        return jnp.concatenate([spread_lanes(a[:, :half]), a[:, half:]], axis=1)

    def spread_lanes(main):
        even_lane = even(main.shape, 1)
        return jnp.concatenate([jnp.where(even_lane, main, roll(main, 1, 1)),
                                jnp.where(even_lane, roll(main, -1, 1), main)], axis=1)

    def spread_far():
        left, right = got_far[0], got_far[1]
        first = even(left.shape, 0)
        upper = jnp.where(first, left, roll(right, 1, 0))
        lower = jnp.where(first, roll(left, -1, 0), right)
        return spread_lanes(jnp.concatenate([upper, lower], axis=0))

    def halo(i):
        return (-i, nx - 1 + i)

    mine = range(nx)
    inner = range(1, nx - 1)
    ends = (0, nx - 1)

    if ring_z:
        for i in mine:
            inv_k[(REACH + i,) + beside] = jnp.exp(-logs[(REACH + i,) + beside])
        for i in range(nx - 1):
            t_x[(REACH + i,) + beside] = 2.0 * inverse(
                inv_k[(REACH + i,) + beside] + inv_k[(REACH + i + 1,) + beside])
    for i in mine:
        fine_z(i, own_part)
    arrive(y_first)
    for i in inner:
        if ring_y:
            inv_k[REACH + i, rim_part, 0:nz] = jnp.exp(-logs[REACH + i, rim_part, 0:nz])
        fine_y(i, slice(0, nz))
        fine_d_core(i)
        fine_first(i, core)
    start(x_dir)
    arrive(packs_far)
    start(pass_y)
    start(pass_z)
    arrive(y_log)
    if ring_y:
        for i in mine:
            fine_k(i, rim_part)
        for i in mine:
            fine_z(i, rim_part)
        for i in range(nx - 1):
            fine_x(i, rim_part)
        keep_coarse(0, rim, own_coarse(0, rim))
    for i in mine:
        fine_y(i)
    for i in inner:
        fine_d(i)
    arrive(y_src)
    for i in inner:
        if ring_z:
            fine_first(i, beside)
        if ring_y:
            fine_first(i, rim)
    if ring_y:
        keep_coarse(1, rim, own_coarse(1, rim))
    coarse_yz(0)
    coarse_x(-1)

    arrive(x_log[1])
    arrive(rows)
    arrive(lanes)
    arrive(corner)
    for side in (0, 1):
        unpack_rows(side, 0)
        unpack_rows(side, 1)
        for b in ring_z:
            unpack_lanes(side, b)
    for i in halo(1) + halo(2):
        fine_k(i)
    for i in halo(1):
        fine_y(i)
        fine_z(i)
    for i in (-2, -1, nx - 1, nx):
        fine_x(i)
    for i in ends + halo(1):
        fine_d(i)
    for i in ends:
        fine_first(i)
    for i in inner:
        fine_turn(1, i)
    arrive(x_src[1])
    for i in halo(1):
        fine_first(i)
    for i in ends:
        fine_turn(1, i)
    for i in inner:
        fine_turn(2, i)

    arrive(packs_near)
    arrive(packs_edge)
    c_inv_k[1] = jnp.exp(-spread(1, 0, True))
    c_inv_k[2] = jnp.exp(-spread(1, 0, False))
    c_res[1] = spread(1, 1, True)
    c_res[2] = spread(1, 1, False)
    coarse_yz(1)
    coarse_x(0)
    coarse_x(1)
    coarse_yz(2)
    for i in (0, 1):
        coarse_d(i)
        coarse_first(i)
    coarse_turn(1, 0)

    arrive(pass_z)
    for side in (0, 1):
        for b in ring_z:
            unpack_far(side, b)
    arrive(pass_y)
    c_inv_k[3] = jnp.exp(-spread(2, 0, True))
    c_inv_k[4] = jnp.exp(-spread(2, 0, False))
    c_res[(3,) + core] = spread_far()
    coarse_yz(3)
    coarse_x(2)
    coarse_x(3)
    for i in (2, 3):
        coarse_d(i)
    coarse_first(2)
    coarse_first(3, core)
    coarse_turn(1, 1)
    coarse_turn(1, 2, True)
    coarse_turn(2, 0)
    coarse_turn(2, 1, True)
    coarse_turn(3, 0, True)

    arrive(x_log[3])
    for i in halo(3):
        fine_k(i)
    for i in halo(2):
        fine_y(i)
        fine_z(i)
    for i in (-3, nx + 1):
        fine_x(i)
    for i in halo(2):
        fine_d(i)
    arrive(x_src[2])
    for i in halo(2):
        fine_first(i)
    for i in halo(1):
        fine_turn(1, i)
    for i in ends:
        fine_turn(2, i)
    for i in inner:
        fine_turn(3, i, True)

    for group in ([z_log, z_src, y_first, y_log, y_src, rows, corner, x_dir, packs_near, packs_edge, packs_far, pass_y, pass_z, lanes]
                  + list(x_log.values()) + list(x_src.values())):
        drain(group)

    arrive(x_dir)
    for i in halo(2):
        fine_turn(1, i, True)
    for i in halo(1):
        fine_turn(2, i, True)
    for i in ends:
        fine_turn(3, i, True)


def shards(sizes, log_perm, source, low_bound, high_bound):
    nx, ny, nz = log_perm.shape
    wide_y = ny + ROWS * sides(sizes["gy"])
    wide_z = nz + LANES * sides(sizes["gz"])
    half = nz // 2
    f32 = lambda *shape: pltpu.VMEM(shape, jnp.float32)
    fine = lambda reach: f32(nx + 2 * reach, wide_y, wide_z)
    pairs = lambda n: f32(n, wide_y, wide_z)
    log_perm = pltpu.with_memory_space_constraint(log_perm, pltpu.HBM)
    source = pltpu.with_memory_space_constraint(source, pltpu.HBM)
    hbm = pl.BlockSpec(memory_space=pltpu.HBM)
    vmem = pl.BlockSpec(memory_space=pltpu.VMEM)
    whole = jax.ShapeDtypeStruct((nx, ny, nz), jnp.float32)
    messages = 96
    part, last, coarse = pl.pallas_call(
        functools.partial(kernel, sizes),
        out_shape=(whole, whole, jax.ShapeDtypeStruct((nx // 2, ny, nz), jnp.float32)),
        in_specs=[hbm] * 4,
        out_specs=(vmem,) * 3,
        scratch_shapes=[
            pltpu.SMEM((1,), jnp.float32),
            pltpu.SMEM((1,), jnp.float32),
            fine(REACH), fine(DEGREE),
            f32(2, 2, 2, wide_y, half + wide_z - nz),
            f32(2, ny, half + wide_z - nz),
            f32(2, max(1, sides(sizes["gy"])), 2, ROWS, nz),
            f32(2, max(1, sides(sizes["gy"])), 2, ROWS, nz),
            f32(2, max(1, sides(sizes["gz"])), ny, LANES),
            f32(2, 2, max(1, sides(sizes["gz"])), ny, LANES),
            f32(2, ny // 2, half),
            f32(2, ny // 2, half),
            f32(2, max(1, sides(sizes["gy"])), max(1, sides(sizes["gz"])), ROWS, LANES),
            f32(2, max(1, sides(sizes["gy"])), max(1, sides(sizes["gz"])), ROWS, LANES),
            fine(REACH), fine(REACH), fine(DEGREE), fine(DEGREE), fine(DEGREE), fine(DEGREE), fine(DEGREE),
            fine(DEGREE), fine(DEGREE - 1), fine(DEGREE - 2),
            pairs(5), pairs(5), pairs(4), pairs(4), pairs(4), pairs(4), pairs(4), pairs(4), pairs(3), pairs(2),
            pltpu.SemaphoreType.DMA((4,)),
            pltpu.SemaphoreType.DMA((messages,)),
            pltpu.SemaphoreType.DMA((messages,)),
        ],
        compiler_params=pltpu.CompilerParams(
            collective_id=0, has_side_effects=True, vmem_limit_bytes=24 * 2**20),
    )(low_bound, high_bound, log_perm, source)
    fine_pressure = part + last
    return fine_pressure, fine_pressure - jnp.repeat(coarse, 2, axis=0)


def solution(mesh):
    sizes = {axis: mesh.shape[axis] for axis in AXES}
    spec = P(("groups", "gx"), "gy", "gz")
    return jax.shard_map(
        functools.partial(shards, sizes),
        mesh=mesh,
        in_specs=(spec, spec, P(), P()),
        out_specs=(spec, spec),
        check_vma=False,
    )
```
